32 devices in a mesh: space: 8 (over z, core), spec: 4 (over y, x).
Axes of the slice: x: 2, y: 2, z: 4, core: 2. Of those that a mesh axis runs over, the one named last changes fastest.
Arguments:
- action: float32 [16, 24, 64, 512], P('spec', None, 'space'), may hold values from 0.1 to 1
- currents: float32 [2, 128, 1024], P(None, 'space', 'spec'), may hold values from -1.2 to 1.2
- wet: int32 [128, 1024], P('space', 'spec'), may hold values 0 or 1
- courant: float32 [16], replicated, may hold values from 0.1 to 0.35
- energy: float32 [16], replicated, may hold values from 0.3 to 3
- src: int32 [96, 512, 4], P('space'), may hold values from 4096 to 29695, as said below
- weights: float32 [96, 512, 4], P('space'), as said below
Outputs:
- new_action: float32 [16, 24, 64, 512], P('spec', None, 'space')
- new_currents: float32 [2, 128, 1024], P(None, 'space', 'spec')
The draws below stay inside these ranges and needn't reach their ends.
Inputs may be any that keep to these rules, and one draw needn't show every extreme that they name: `src`: row e of block s refers to ocean rows 2 (e - 2) + 8 + j + a of the pair of ocean row blocks s and s + 1 (j 0 or 1 per wave cell, a the corner's row bit) and columns (2 x + i + b) mod 1024; the four corners of a cell are distinct; the two outer rows on each side of a block's lists refer to the same ocean cells, with the same weights, as the lists of the same wave rows in the neighbouring blocks. Positive; the 4 weights of a wave cell sum to one; rows that describe the same wave row are equal.
All inputs are finite; a program needn't handle non-finite values. No bound on the sum of `wet` on one device may be relied on, other than what follows from the above.
Results may differ from the reference program's by a relative error of at most 0.00009.
Values sent between devices are 32-bit elements; how exact they have to be, the bound alone decides.
No kernel may reach another device: no remote copies, remote signals or barrier semaphores. Data moves between devices by JAX's collectives and lax.ppermute only.
A program may use at most 128 MiB of HBM per device.

```python
import math
import jax
import jax.numpy as jnp
from jax import lax

ND = 24
NF = 16
WR = 8
GX = 512
K = 4
GY = 64
WE = 12
OR = 16
OY = 128
OXG = 1024
N_SPACE = 8


def remap_lists(key, low_weight):
    base = jax.random.fold_in(key, 101)

    def single_row(index):
        block_index = index // WE
        offset = index % WE
        global_row = block_index * WR + offset - 2
        row_key = jax.random.fold_in(base, global_row % GY)
        key_jitter, key_slide, key_weight = jax.random.split(row_key, 3)
        jitter = jax.random.randint(key_jitter, (GX,), 0, 2)
        slide = jax.random.randint(key_slide, (GX,), 0, 2)
        spread = jax.random.uniform(key_weight, (GX, K), minval=low_weight, maxval=1.0)
        corner = jnp.arange(K, dtype=jnp.int32)
        row_local = 2 * (offset - 2) + WR + jitter[:, None] + corner[None, :] // 2
        column = (2 * jnp.arange(GX, dtype=jnp.int32)[:, None] + slide[:, None] + corner[None, :] % 2) % OXG
        return (row_local * OXG + column, spread / jnp.sum(spread, axis=1, keepdims=True))
    return jax.vmap(single_row)(jnp.arange(N_SPACE * WE, dtype=jnp.int32))


def draw_src(key, part):
    return remap_lists(key, 0.2)[0].astype(jnp.int32)


def draw_weights(key, part):
    low_weight = 0.2
    return remap_lists(key, low_weight)[1].astype(jnp.float32)


def with_ends(entries, own_key, low, top_value):
    shape = entries.shape
    place = [jax.random.randint(jax.random.fold_in(own_key, axis), (), 0, shape[axis]) for axis in range(len(shape))]
    entries = entries.at[tuple(place)].set(low)
    longest = shape.index(max(shape))
    place[longest] = (place[longest] + 1) % shape[longest]
    return entries.at[tuple(place)].set(top_value)


def levels(own_key, shape, cuts, smallest, high):
    loudness, own = 1.0, jax.random.fold_in(own_key, 6)
    for position, parts in cuts:
        draws = jnp.exp(jax.random.uniform(jax.random.fold_in(own, position), (parts,), jnp.float32, smallest / len(cuts), high / len(cuts)))
        loudness = loudness * jnp.repeat(draws, shape[position] // parts).reshape([-1 if axis == position else 1 for axis in range(len(shape))])
    return loudness


def gaussian(own_key, dims, scale, bound, cuts=(), kind=jnp.bfloat16):
    entries = scale * jax.random.normal(own_key, dims, jnp.float32)
    if cuts:
        entries = entries * levels(own_key, dims, cuts, -0.22, 0.18)
    return jnp.clip(entries, -bound, bound).astype(kind)


def setup_inputs(seed: int = 0) -> dict:
    key_of = jax.random.split(jax.random.key(seed), 8)
    return {
        "action": jnp.clip(jnp.exp(math.log(1.0) - 2.3025851 * jax.random.uniform(key_of[0], (NF, ND, GY, GX), jnp.float32) ** levels(key_of[0], (NF, ND, GY, GX), ((0, 4), (2, 8)), -0.2, 0.2)), 0.1, 1.0),
        "currents": gaussian(key_of[1], (2, OY, OXG), 0.3, 1.2, ((1, 8), (2, 4)), jnp.float32),
        "wet": with_ends((jax.random.randint(key_of[2], (OY, OXG), 0, 4) < 3).astype(jnp.int32), jax.random.fold_in(key_of[2], 1), 0, 1),
        "courant": jnp.clip(jax.random.uniform(key_of[3], (NF,), jnp.float32, 0.1, 0.35), 0.1, 0.35),
        "energy": jnp.clip(jnp.exp(jax.random.uniform(key_of[4], (NF,), jnp.float32, math.log(0.3), math.log(3.0))), 0.3, 3.0),
        "src": draw_src(jax.random.fold_in(key_of[7], 71), 0),
        "weights": draw_weights(jax.random.fold_in(key_of[7], 71), 0),
    }


drift_factor = 0.2
refract_factor = 1.5
damping = 0.95
force_gain = 0.5

def centred(field, axis):
    return (jnp.roll(field, -1, axis) - jnp.roll(field, 1, axis)) * 0.5

def advance_global(field, speed, cosine, sine, east, north, turn):
    speed_x = speed * cosine[:, None, None] + drift_factor * east[None]
    face_x = jnp.maximum(speed_x, 0.0) * field + jnp.minimum(jnp.roll(speed_x, -1, 2), 0.0) * jnp.roll(field, -1, 2)
    speed_y = speed * sine[:, None, None] + drift_factor * north[None]
    face_y = jnp.maximum(speed_y, 0.0) * field + jnp.minimum(jnp.roll(speed_y, -1, 1), 0.0) * jnp.roll(field, -1, 1)
    face_turn = jnp.maximum(turn, 0.0) * field + jnp.minimum(jnp.roll(turn, -1, 0), 0.0) * jnp.roll(field, -1, 0)
    return field - (face_x - jnp.roll(face_x, 1, 2)) - (face_y - jnp.roll(face_y, 1, 1)) - (face_turn - jnp.roll(face_turn, 1, 0))

def reference(action, currents, wet, courant, energy, src, weights):
    wet_float = wet.astype(jnp.float32)
    masked = currents * wet_float[None]
    src_own = src.reshape(N_SPACE, WE, GX, K)[:, 2:WR + 2]
    weight_own = weights.reshape(N_SPACE, WE, GX, K)[:, 2:WR + 2]
    blocks = jnp.arange(N_SPACE, dtype=jnp.int32)[:, None, None, None]
    rows = (blocks * OR + src_own // OXG) % OY
    cols = src_own % OXG
    picked = masked[:, rows, cols]
    wave_current = lax.optimization_barrier(jnp.sum(weight_own[None] * picked, axis=-1)).reshape(2, GY, GX)
    east, north = (wave_current[0], wave_current[1])
    angles = 2.0 * math.pi * (jnp.arange(ND, dtype=jnp.float32) + 0.5) / ND
    cosine, sine = (jnp.cos(angles), jnp.sin(angles))
    grad_east_x, grad_north_x = (centred(east, 1), centred(north, 1))
    grad_east_y, grad_north_y = (centred(east, 0), centred(north, 0))
    cos3, sin3 = (cosine[:, None, None], sine[:, None, None])
    turn = refract_factor * (sin3 * cos3 * (grad_east_x - grad_north_y)[None] + sin3 * sin3 * grad_east_y[None] - cos3 * cos3 * grad_north_x[None])
    ratio = 0.5 + 0.5 * jnp.arange(NF, dtype=jnp.float32) / (NF - 1)
    amplitude = energy / math.sqrt(ND * NF)
    coef = jnp.stack([amplitude[:, None] * (ratio[:, None] * (cosine * cosine)[None] + ratio[:, None] - 0.5), amplitude[:, None] * (ratio[:, None] * (sine * sine)[None] + ratio[:, None] - 0.5), amplitude[:, None] * ratio[:, None] * (sine * cosine)[None]], axis=1)

    def per_frequency(inputs):
        field, speed, weight_table = inputs
        field = advance_global(field, speed, cosine, sine, east, north, turn)
        field = advance_global(field, speed, cosine, sine, east, north, turn)
        partial_stress = jnp.einsum('kd,dyx->kyx', weight_table, field, precision=lax.Precision.HIGHEST)
        return (field, partial_stress)
    new_action, stresses = lax.map(per_frequency, (action, courant, coef))
    stress = lax.optimization_barrier(jnp.sum(stresses, axis=0))
    force_x = -(centred(stress[0], 1) + centred(stress[2], 0))
    force_y = -(centred(stress[2], 1) + centred(stress[1], 0))
    force = jnp.stack([force_x, force_y]).reshape(2, N_SPACE, WR, GX)
    contributions = (weight_own[None] * force[..., None]).reshape(2, -1)
    target = (rows * OXG + cols).reshape(-1)
    ocean_force = jnp.stack([jax.ops.segment_sum(contributions[0], target, num_segments=OY * OXG), jax.ops.segment_sum(contributions[1], target, num_segments=OY * OXG)]).reshape(2, OY, OXG)
    new_currents = wet_float[None] * (damping * currents + force_gain * ocean_force)
    return (new_action, new_currents)
```

```python
import functools
import math

import jax
import jax.numpy as jnp
import numpy as np
from jax import lax
from jax.experimental import pallas as pl
from jax.experimental.pallas import tpu as pltpu
from jax.sharding import PartitionSpec as P

drift_factor = 0.2
refract_factor = 1.5
damping = 0.95
force_gain = 0.5

LANES = 128
HIGHEST = lax.Precision.HIGHEST
VMEM = pl.BlockSpec(memory_space=pltpu.VMEM)
SMEM = pl.BlockSpec(memory_space=pltpu.SMEM)


def from_offset(block, axis, offset):
    count = lax.axis_size(axis)
    return lax.ppermute(block, axis, [((i + offset) % count, i) for i in range(count)])


def from_xor(block, axis, bits):
    count = lax.axis_size(axis)
    return lax.ppermute(block, axis, [(i ^ bits, i) for i in range(count)])


def params(**kw):
    return pltpu.CompilerParams(vmem_limit_bytes=48 * 1024 * 1024, **kw)


def split_matrix(width):
    row = lax.broadcasted_iota(jnp.int32, (width, width), 0)
    col = lax.broadcasted_iota(jnp.int32, (width, width), 1)
    half = width // 2
    source = jnp.where(col < half, 2 * col, 2 * (col - half) + 1)
    return (row == source).astype(jnp.float32)


def merge_matrix(width):
    row = lax.broadcasted_iota(jnp.int32, (width, width), 0)
    col = lax.broadcasted_iota(jnp.int32, (width, width), 1)
    half = width // 2
    target = jnp.where(row < half, 2 * row, 2 * (row - half) + 1)
    return (col == target).astype(jnp.float32)


def split_kernel(own_ref, next_ref, out_ref):
    comps, rows, width = own_ref.shape
    matrix = split_matrix(width)
    for part, ref in enumerate((own_ref, next_ref)):
        cells = ref[...].reshape(comps * rows, width)
        split = jnp.dot(cells, matrix, precision=HIGHEST, preferred_element_type=jnp.float32)
        out_ref[:, part * rows : (part + 1) * rows, :] = split.reshape(comps, rows, width)


def tables_kernel(ocean_cols, wave_rows, tail_rows, src_ref, weight_ref, table_ref, tail_ref):
    list_rows, corners, columns = src_ref.shape
    shape = (list_rows, columns)
    entry_row = lax.broadcasted_iota(jnp.int32, shape, 0)
    column = lax.broadcasted_iota(jnp.int32, shape, 1)
    base = (2 * (entry_row - 2) + wave_rows) * ocean_cols
    cell = [
        base + jnp.where(2 * column + step >= ocean_cols, 2 * column + step - ocean_cols, 2 * column + step)
        for step in range(3)
    ]
    sums = [jnp.zeros(shape, jnp.float32) for _ in range(9)]
    for corner in range(corners):
        source = src_ref[:, corner, :]
        weight = weight_ref[:, corner, :]
        for step_row in range(3):
            for step_col in range(3):
                hit = source == cell[step_col] + step_row * ocean_cols
                place = 3 * step_row + step_col
                sums[place] = sums[place] + jnp.where(hit, weight, 0.0)
    for place in range(9):
        table_ref[place] = sums[place]
    first = 2 + wave_rows // 2 - 1
    for place in range(9):
        tail_ref[place] = table_ref[place, first : first + tail_rows, :]


def wide(table, columns):
    return jnp.concatenate([table] * (columns // LANES), axis=1)


def advance_kernel(
    total_freq, axis, pieces, *refs
):
    piece_refs = refs[:pieces]
    (table_ref, trig_ref, speed_ref, energy_ref, field_ref, low_ref, high_ref) = refs[pieces : pieces + 7]
    out_ref, stress_ref = refs[pieces + 7 : pieces + 9]
    ocean_ref, flow_ref, grad_ref, turn_ref, mid_ref, sum_ref = refs[pieces + 9 :]
    freqs, wave_rows, directions, columns = field_ref.shape
    list_rows = table_ref.shape[1]
    index = lax.axis_index(axis)
    tiles = columns // LANES
    for bits, ref in enumerate(piece_refs):
        half = ref.shape[2] // 2
        count = half // LANES
        start = (index ^ bits) * count if pieces > 1 else 0
        for parity in range(2):
            for tile in range(count):
                lane = parity * half + tile * LANES
                ocean_ref[parity, start + tile] = ref[:, :, lane : lane + LANES]
    first = wave_rows - 4

    def lift(parity, comp, rows):
        return jnp.concatenate([ocean_ref[parity, tile, comp, rows, :] for tile in range(tiles)], axis=1)

    for comp in range(2):
        total = None
        for step_row in range(3):
            rows = pl.ds(first + step_row, list_rows, stride=2)
            even, odd = lift(0, comp, rows), lift(1, comp, rows)
            for step_col, lifted in enumerate((even, odd, pltpu.roll(even, columns - 1, 1))):
                term = table_ref[3 * step_row + step_col] * lifted
                total = term if total is None else total + term
        flow_ref[comp, :list_rows] = total
    inner = list_rows - 2
    east, north = flow_ref[0, 1 : 1 + inner], flow_ref[1, 1 : 1 + inner]
    east_y = (flow_ref[0, 2 : 2 + inner] - flow_ref[0, 0:inner]) * 0.5
    north_y = (flow_ref[1, 2 : 2 + inner] - flow_ref[1, 0:inner]) * 0.5
    east_x = (pltpu.roll(east, columns - 1, 1) - pltpu.roll(east, 1, 1)) * 0.5
    north_x = (pltpu.roll(north, columns - 1, 1) - pltpu.roll(north, 1, 1)) * 0.5
    grad_ref[0, :inner] = refract_factor * (east_x - north_y)
    grad_ref[1, :inner] = refract_factor * east_y
    grad_ref[2, :inner] = refract_factor * north_x
    for comp in range(2):
        flow_ref[comp, :list_rows] = drift_factor * flow_ref[comp, :list_rows]
    full = (directions, columns)

    def spread(ref, *at):
        *lead, row = at
        return jnp.broadcast_to(ref[(*lead, pl.ds(row, 1), slice(None))].reshape(1, columns), full)

    cosine, sine = trig_ref[0], trig_ref[1]
    cross, sin2, cos2 = (wide(trig_ref[k], columns) for k in (2, 3, 4))
    for row in range(inner):
        turn = cross * spread(grad_ref, 0, row) + sin2 * spread(grad_ref, 1, row) - cos2 * spread(grad_ref, 2, row)
        turn_ref[0, row] = jnp.maximum(turn, 0.0)
        turn_ref[1, row] = jnp.minimum(turn, 0.0)
    sum_ref[...] = jnp.zeros_like(sum_ref)
    start = index * freqs

    def one_frequency(freq, carry):
        speed = speed_ref[start + freq]
        speed_cos = wide(speed * cosine, columns)
        speed_sin = wide(speed * sine, columns)

        def cells(row):
            if row < 0:
                return low_ref[freq, 2 + row]
            if row >= wave_rows:
                return high_ref[freq, row - wave_rows]
            return field_ref[freq, row]

        def sweep(read, low, high, write):
            before = read(low - 1)
            north_before = speed_sin + spread(flow_ref, 1, low - 1 + 2)
            part = jnp.maximum(north_before, 0.0) * before
            here = read(low)
            north_here = speed_sin + spread(flow_ref, 1, low + 2)
            face_before = part + jnp.minimum(north_here, 0.0) * here
            for row in range(low, high):
                after = read(row + 1)
                north_after = speed_sin + spread(flow_ref, 1, row + 1 + 2)
                face_here = jnp.maximum(north_here, 0.0) * here + jnp.minimum(north_after, 0.0) * after
                speed_x = speed_cos + spread(flow_ref, 0, row + 2)
                face_x = jnp.maximum(speed_x, 0.0) * here + pltpu.roll(
                    jnp.minimum(speed_x, 0.0) * here, columns - 1, 1
                )
                face_turn = turn_ref[0, row + 1] * here + pltpu.roll(
                    turn_ref[1, row + 1] * here, directions - 1, 0
                )
                write(
                    row,
                    here
                    - (face_x - pltpu.roll(face_x, 1, 1))
                    - (face_here - face_before)
                    - (face_turn - pltpu.roll(face_turn, 1, 0)),
                )
                face_before, here, north_here = face_here, after, north_after

        def keep(row, value):
            mid_ref[row + 1] = value

        sweep(cells, -1, wave_rows + 1, keep)
        ratio = 0.5 + 0.5 * (start + freq).astype(jnp.float32) / (total_freq - 1)
        amplitude = energy_ref[start + freq] / math.sqrt(directions * total_freq)
        scale, rest = amplitude * ratio, amplitude * (ratio - 0.5)

        def finish(row, value):
            out_ref[freq, row] = value
            plain = weighted = mixed = None
            for tile in range(0, directions, 8):
                slab = value[tile : tile + 8]
                a, b = cos2[tile : tile + 8] * slab, cross[tile : tile + 8] * slab
                plain = slab if plain is None else plain + slab
                weighted = a if weighted is None else weighted + a
                mixed = b if mixed is None else mixed + b
            sum_ref[0, row] += scale * weighted + rest * plain
            sum_ref[1, row] += scale * (plain - weighted) + rest * plain
            sum_ref[2, row] += scale * mixed

        sweep(lambda row: mid_ref[row + 1], 0, wave_rows, finish)
        return carry

    lax.fori_loop(0, freqs, one_frequency, 0)
    for kind in range(3):
        for row in range(wave_rows):
            stress_ref[kind, row : row + 1] = jnp.sum(sum_ref[kind, row], axis=0, keepdims=True)


def force_terms(own_ref, prev_ref, table_ref, tail_ref, stress_ref, coupling_ref):
    wave_rows, columns = own_ref.shape[1:]
    half = wave_rows // 2
    count = wave_rows + 1
    behind = half + 2
    for kind in range(3):
        stress_ref[kind, 0:behind] = prev_ref[kind, wave_rows - behind : wave_rows]
        stress_ref[kind, behind : behind + half + 1] = own_ref[kind, 0 : half + 1]
    far = half - 1
    for place in range(9):
        coupling_ref[place, 0:far] = tail_ref[place]
        coupling_ref[place, far:count] = table_ref[place, 0 : count - far]

    def along_x(kind):
        middle = stress_ref[kind, 1 : 1 + count]
        return (pltpu.roll(middle, columns - 1, 1) - pltpu.roll(middle, 1, 1)) * 0.5

    def along_y(kind):
        return (stress_ref[kind, 2 : 2 + count] - stress_ref[kind, 0:count]) * 0.5

    forces = (-(along_x(0) + along_y(2)), -(along_x(2) + along_y(1)))
    return forces


def force_kernel(axis, own_ref, prev_ref, table_ref, tail_ref, current_ref, wet_ref, out_ref,
                 stress_ref, coupling_ref, push_ref, chunk_ref, merge_ref):
    wave_rows, columns = own_ref.shape[1:]
    width = current_ref.shape[2]
    half = width // 2
    forces = force_terms(own_ref, prev_ref, table_ref, tail_ref, stress_ref, coupling_ref)
    count = wave_rows + 1
    start = pl.multiple_of(lax.axis_index(axis) * half, LANES)
    for comp, force in enumerate(forces):
        for step_row in range(3):
            for step_col in range(3):
                push_ref[0, 3 * step_row + step_col, :count] = coupling_ref[3 * step_row + step_col] * force

        def near(place):
            return push_ref[0, place, 1:count]

        def far(place):
            return push_ref[0, place, 0 : count - 1]

        even_even = near(0) + far(6) + pltpu.roll(near(2) + far(8), 1, 1)
        even_odd = near(1) + far(7)
        odd_even = near(3) + pltpu.roll(near(5), 1, 1)
        odd_odd = near(4)
        for parity, (even, odd) in enumerate(((even_even, even_odd), (odd_even, odd_odd))):
            chunk_ref[0, comp, parity] = even
            chunk_ref[1, comp, parity] = odd
    rows = 4 * wave_rows
    even = chunk_ref[0, :, :, :, pl.ds(start, half)].reshape(rows, half)
    odd = chunk_ref[1, :, :, :, pl.ds(start, half)].reshape(rows, half)
    merged = jnp.dot(
        jnp.concatenate([even, odd], axis=1), merge_matrix(width), precision=HIGHEST,
        preferred_element_type=jnp.float32,
    ).reshape(2, 2, wave_rows, width)
    wet = wet_ref[...].astype(jnp.float32)
    for comp in range(2):
        for tile in range(width // LANES):
            lanes = slice(tile * LANES, (tile + 1) * LANES)
            for parity in range(2):
                lines = pl.ds(parity, wave_rows, stride=2)
                merge_ref[comp, tile, lines, :] = merged[comp, parity, :, lanes]
            out_ref[comp, :, lanes] = wet[:, lanes] * (
                damping * current_ref[comp, :, lanes] + force_gain * merge_ref[comp, tile]
            )


def push_kernel(own_ref, prev_ref, table_ref, tail_ref, out_ref, stress_ref, coupling_ref, push_ref):
    wave_rows, columns = own_ref.shape[1:]
    forces = force_terms(own_ref, prev_ref, table_ref, tail_ref, stress_ref, coupling_ref)
    count = wave_rows + 1
    for comp, force in enumerate(forces):
        for place in range(9):
            push_ref[0, place, :count] = coupling_ref[place] * force
        near = [push_ref[0, place, 1:count] for place in range(9)]
        far = [push_ref[0, place, 0 : count - 1] for place in range(9)]
        out_ref[0, comp, 0] = near[0] + far[6] + pltpu.roll(near[2] + far[8], 1, 1)
        out_ref[1, comp, 0] = near[1] + far[7]
        out_ref[0, comp, 1] = near[3] + pltpu.roll(near[5], 1, 1)
        out_ref[1, comp, 1] = near[4]


def per_device(action, currents, wet, courant, energy, src, weights):
    f32 = jnp.float32
    freqs, directions, wave_rows, columns = action.shape
    list_rows = src.shape[0]
    ocean_rows, width = wet.shape
    spec = lax.axis_size("spec")
    ocean_cols = width * spec
    half = width // 2
    aligned = half % LANES == 0 and spec <= 4
    masked = currents * wet.astype(f32)[None]
    masked_next = from_offset(masked, "space", 1)
    field = jnp.transpose(action, (0, 2, 1, 3))
    low = from_offset(field[:, wave_rows - 2 :], "space", -1)
    high = from_offset(field[:, :2], "space", 1)
    tail_rows = wave_rows // 2 - 1
    tables, tail = pl.pallas_call(
        functools.partial(tables_kernel, ocean_cols, wave_rows, tail_rows),
        out_shape=(
            jax.ShapeDtypeStruct((9, list_rows, columns), f32),
            jax.ShapeDtypeStruct((9, tail_rows, columns), f32),
        ),
        in_specs=[VMEM] * 2,
        out_specs=(VMEM, VMEM),
        compiler_params=params(),
        name="tables",
    )(jnp.transpose(src, (0, 2, 1)), jnp.transpose(weights, (0, 2, 1)))
    tail_prev = from_offset(tail, "space", -1)
    if aligned:
        piece = pl.pallas_call(
            split_kernel,
            out_shape=jax.ShapeDtypeStruct((2, 2 * ocean_rows, width), f32),
            in_specs=[VMEM] * 2,
            out_specs=VMEM,
            compiler_params=params(),
            name="split",
        )(masked, masked_next)
        pieces = [piece] + [from_xor(piece, "spec", bits) for bits in range(1, spec)]
    else:
        both = lax.all_gather(jnp.concatenate([masked, masked_next], axis=1), "spec", axis=2, tiled=True)
        pieces = [jnp.concatenate([both[:, :, 0::2], both[:, :, 1::2]], axis=2)]
    angles = 2.0 * math.pi * (np.arange(directions) + 0.5) / directions
    cosine, sine = np.cos(angles), np.sin(angles)
    trig = np.stack([cosine, sine, sine * cosine, sine * sine, cosine * cosine]).astype(np.float32)
    trig = jnp.asarray(np.repeat(trig[:, :, None], LANES, axis=2))
    total_freq = freqs * spec
    padded = -(-list_rows // 8) * 8
    out_field, stress = pl.pallas_call(
        functools.partial(advance_kernel, total_freq, "spec", len(pieces)),
        out_shape=(
            jax.ShapeDtypeStruct(field.shape, f32),
            jax.ShapeDtypeStruct((3, wave_rows, columns), f32),
        ),
        in_specs=[VMEM] * len(pieces) + [VMEM, VMEM, SMEM, SMEM, VMEM, VMEM, VMEM],
        out_specs=(VMEM, VMEM),
        scratch_shapes=[
            pltpu.VMEM((2, columns // LANES, 2, 2 * ocean_rows, LANES), f32),
            pltpu.VMEM((2, padded, columns), f32),
            pltpu.VMEM((3, padded, columns), f32),
            pltpu.VMEM((2, list_rows - 2, directions, columns), f32),
            pltpu.VMEM((wave_rows + 2, directions, columns), f32),
            pltpu.VMEM((3, wave_rows, 8, columns), f32),
        ],
        compiler_params=params(),
        name="advance",
    )(*pieces, tables, trig, courant, energy, field, low, high)
    new_action = jnp.transpose(out_field, (0, 2, 1, 3))
    if spec <= 4:
        stress = stress + sum(from_xor(stress, "spec", bits) for bits in range(1, spec))
    else:
        stress = lax.psum(stress, "spec")
    stress_prev = from_offset(stress, "space", -1)
    count = wave_rows + 1
    scratch = [
        pltpu.VMEM((3, 2 * wave_rows, columns), f32),
        pltpu.VMEM((9, count, columns), f32),
        pltpu.VMEM((1, 9, count, columns), f32),
    ]
    if aligned:
        updated = pl.pallas_call(
            functools.partial(force_kernel, "spec"),
            out_shape=jax.ShapeDtypeStruct(currents.shape, f32),
            in_specs=[VMEM] * 6,
            out_specs=VMEM,
            scratch_shapes=scratch
            + [
                pltpu.VMEM((2, 2, 2, wave_rows, columns), f32),
                pltpu.VMEM((2, width // LANES, ocean_rows, LANES), f32),
            ],
            compiler_params=params(),
            name="force",
        )(stress, stress_prev, tables, tail_prev, currents, wet)
    else:
        pushed = pl.pallas_call(
            push_kernel,
            out_shape=jax.ShapeDtypeStruct((2, 2, 2, wave_rows, columns), f32),
            in_specs=[VMEM] * 4,
            out_specs=VMEM,
            scratch_shapes=scratch,
            compiler_params=params(),
            name="push",
        )(stress, stress_prev, tables, tail_prev)
        grid = jnp.transpose(pushed, (1, 3, 2, 4, 0)).reshape(2, ocean_rows, ocean_cols)
        share = lax.dynamic_slice_in_dim(grid, lax.axis_index("spec") * width, width, 2)
        updated = wet.astype(f32)[None] * (damping * currents + force_gain * share)
    return (new_action, updated)


def solution(mesh):
    in_specs = (
        P("spec", None, "space", None),
        P(None, "space", "spec"),
        P("space", "spec"),
        P(),
        P(),
        P("space", None, None),
        P("space", None, None),
    )
    out_specs = (P("spec", None, "space", None), P(None, "space", "spec"))
    return jax.shard_map(
        per_device, mesh=mesh, in_specs=in_specs, out_specs=out_specs, check_vma=False
    )
```

```python
import functools
import math

import jax
import jax.numpy as jnp
import numpy as np
from jax import lax
from jax.experimental import pallas as pl
from jax.experimental.pallas import tpu as pltpu
from jax.sharding import PartitionSpec as P


drift_factor = 0.2
refract_factor = 1.5
damping = 0.95
force_gain = 0.5

LANES = 128
HIGHEST = lax.Precision.HIGHEST
VMEM = pl.BlockSpec(memory_space=pltpu.VMEM)
SMEM = pl.BlockSpec(memory_space=pltpu.SMEM)


def from_offset(block, axis, offset):
    count = lax.axis_size(axis)
    return lax.ppermute(block, axis, [((i + offset) % count, i) for i in range(count)])


def from_xor(block, axis, bits):
    count = lax.axis_size(axis)
    return lax.ppermute(block, axis, [(i ^ bits, i) for i in range(count)])


def params(**kw):
    return pltpu.CompilerParams(vmem_limit_bytes=48 * 1024 * 1024, **kw)


def split_matrix(width):
    row = lax.broadcasted_iota(jnp.int32, (width, width), 0)
    col = lax.broadcasted_iota(jnp.int32, (width, width), 1)
    half = width // 2
    source = jnp.where(col < half, 2 * col, 2 * (col - half) + 1)
    return (row == source).astype(jnp.float32)


def merge_matrix(width):
    row = lax.broadcasted_iota(jnp.int32, (width, width), 0)
    col = lax.broadcasted_iota(jnp.int32, (width, width), 1)
    half = width // 2
    target = jnp.where(row < half, 2 * row, 2 * (row - half) + 1)
    return (col == target).astype(jnp.float32)


def split_kernel(own_ref, next_ref, out_ref):
    comps, rows, width = own_ref.shape
    matrix = split_matrix(width)
    for part, ref in enumerate((own_ref, next_ref)):
        cells = ref[...].reshape(comps * rows, width)
        split = jnp.dot(cells, matrix, precision=HIGHEST, preferred_element_type=jnp.float32)
        out_ref[:, part * rows : (part + 1) * rows, :] = split.reshape(comps, rows, width)


def roll_lanes(x, shift):
    lane = lax.broadcasted_iota(jnp.int32, x.shape, x.ndim - 1)
    turned = pltpu.roll(x, shift % LANES, x.ndim - 1)
    if shift == 1:
        return jnp.where(lane == 0, roll_lead(turned, 1, x.ndim - 3), turned)
    return jnp.where(lane == LANES - 1, roll_lead(turned, -1, x.ndim - 3), turned)


def roll_lead(x, shift, axis):
    count = x.shape[axis]
    cut = (-shift) % count
    if cut == 0:
        return x
    return jnp.concatenate(
        [lax.slice_in_dim(x, cut, count, axis=axis), lax.slice_in_dim(x, 0, cut, axis=axis)], axis=axis
    )


def roll_directions(x, shift):
    groups = x.shape[0]
    if shift == 1:
        edge = pltpu.roll(x[groups - 1 :], 1, 2)
        return jnp.concatenate([edge, x[: groups - 1]], axis=0)
    edge = pltpu.roll(x[:1], 7, 2)
    return jnp.concatenate([x[1:], edge], axis=0)


def row_view(ref, freq):
    return ref.at[freq].reshape(ref.shape[1] * ref.shape[2] * 8, LANES)


def row_slots(groups, tiles, row):
    return [
        [pl.ds((group * tiles + tile) * 8 + row, 8, stride=groups * tiles * 8) for tile in range(tiles)]
        for group in range(groups)
    ]


def load_row(view, groups, tiles, row):
    slots = row_slots(groups, tiles, row)
    return jnp.stack([jnp.stack([view[slot, :] for slot in line]) for line in slots])


def store_row(view, row, value):
    groups, tiles = value.shape[:2]
    for group, line in enumerate(row_slots(groups, tiles, row)):
        for tile, slot in enumerate(line):
            view[slot, :] = value[group, tile]


def prepare_kernel(ocean_cols, tail_rows, src_ref, weight_ref, field_ref, table_ref, low_ref, high_ref):
    list_rows, corners, columns = src_ref.shape
    freqs, directions, tiles, wave_rows, _ = field_ref.shape
    groups = directions // 8
    shape = (list_rows, columns)
    entry_row = lax.broadcasted_iota(jnp.int32, shape, 0)
    column = lax.broadcasted_iota(jnp.int32, shape, 1)
    base = (2 * (entry_row - 2) + wave_rows) * ocean_cols
    cell = [
        base + jnp.where(2 * column + step >= ocean_cols, 2 * column + step - ocean_cols, 2 * column + step)
        for step in range(3)
    ]
    sums = [jnp.zeros(shape, jnp.float32) for _ in range(9)]
    for corner in range(corners):
        source = src_ref[:, corner, :]
        weight = weight_ref[:, corner, :]
        for step_row in range(3):
            for step_col in range(3):
                hit = source == cell[step_col] + step_row * ocean_cols
                place = 3 * step_row + step_col
                sums[place] = sums[place] + jnp.where(hit, weight, 0.0)
    for place in range(9):
        table_ref[place] = sums[place]
    first = 2 + wave_rows // 2 - 1
    lead = freqs * 2 * groups
    for place in range(9):
        for row in range(tail_rows):
            slot = place * tail_rows + row
            line = table_ref[place, first + row : first + row + 1, :]
            for tile in range(tiles):
                low_ref[lead + slot // 8, tile, slot % 8 : slot % 8 + 1, :] = line[
                    :, tile * LANES : (tile + 1) * LANES
                ]
    for freq in range(freqs):
        view = row_view(field_ref, freq)
        for row in range(2):
            at = (freq * 2 + row) * groups
            low_ref[at : at + groups] = load_row(view, groups, tiles, wave_rows - 2 + row)
            high_ref[at : at + groups] = load_row(view, groups, tiles, row)


def advance_kernel(total_freq, axis, pieces, *refs):
    piece_refs = refs[:pieces]
    (table_ref, trig_ref, speed_ref, energy_ref, field_ref, low_ref, high_ref) = refs[pieces : pieces + 7]
    out_ref, stress_ref = refs[pieces + 7 : pieces + 9]
    ocean_ref, flow_ref, grad_ref, turn_ref, mid_ref, sum_ref, speeds_ref = refs[pieces + 9 :]
    freqs, directions, tiles, wave_rows, _ = field_ref.shape
    groups = directions // 8
    list_rows = table_ref.shape[1]
    index = lax.axis_index(axis)
    for bits, ref in enumerate(piece_refs):
        half = ref.shape[2] // 2
        count = half // LANES
        start = (index ^ bits) * count if pieces > 1 else 0
        for parity in range(2):
            for tile in range(count):
                lane = parity * half + tile * LANES
                ocean_ref[parity, start + tile] = ref[:, :, lane : lane + LANES]
    first = wave_rows - 4

    def lift(parity, comp, rows):
        return jnp.stack([ocean_ref[parity, tile, comp, rows, :] for tile in range(tiles)])

    def table(place):
        whole = table_ref[place]
        return jnp.stack([whole[:, tile * LANES : (tile + 1) * LANES] for tile in range(tiles)])

    for comp in range(2):
        total = None
        for step_row in range(3):
            rows = pl.ds(first + step_row, list_rows, stride=2)
            even, odd = lift(0, comp, rows), lift(1, comp, rows)
            for step_col, lifted in enumerate((even, odd, roll_lanes(even, -1))):
                term = table(3 * step_row + step_col) * lifted
                total = term if total is None else total + term
        flow_ref[comp, :, :list_rows] = total
    inner = list_rows - 2
    east, north = flow_ref[0, :, 1 : 1 + inner], flow_ref[1, :, 1 : 1 + inner]
    east_y = (flow_ref[0, :, 2 : 2 + inner] - flow_ref[0, :, 0:inner]) * 0.5
    north_y = (flow_ref[1, :, 2 : 2 + inner] - flow_ref[1, :, 0:inner]) * 0.5
    east_x = (roll_lanes(east, -1) - roll_lanes(east, 1)) * 0.5
    north_x = (roll_lanes(north, -1) - roll_lanes(north, 1)) * 0.5
    grad_ref[0, :, :inner] = refract_factor * (east_x - north_y)
    grad_ref[1, :, :inner] = refract_factor * east_y
    grad_ref[2, :, :inner] = refract_factor * north_x
    for comp in range(2):
        flow_ref[comp, :, :list_rows] = drift_factor * flow_ref[comp, :, :list_rows]
    full = (groups, tiles, 8, LANES)

    def spread(ref, kind, row):
        lines = [ref[kind, tile, pl.ds(row, 8, stride=0), :] for tile in range(tiles)]
        return jnp.broadcast_to(jnp.stack(lines)[None], full)

    def wide(kind):
        return jnp.broadcast_to(trig_ref[kind][:, None], full)

    cross, sin2, cos2 = wide(2), wide(3), wide(4)
    for row in range(inner):
        turn = cross * spread(grad_ref, 0, row) + sin2 * spread(grad_ref, 1, row) - cos2 * spread(grad_ref, 2, row)
        turn_ref[0, row] = jnp.maximum(turn, 0.0)
        turn_ref[1, row] = jnp.minimum(turn, 0.0)
    sum_ref[...] = jnp.zeros_like(sum_ref)
    start = index * freqs

    def one_frequency(freq, carry):
        speed = speed_ref[start + freq]
        speed_cos = jnp.broadcast_to((speed * trig_ref[0])[:, None], full)
        speed_sin = jnp.broadcast_to((speed * trig_ref[1])[:, None], full)
        source, sink = row_view(field_ref, freq), row_view(out_ref, freq)

        def cells(row):
            if row < 0:
                return low_ref[pl.ds((freq * 2 + 2 + row) * groups, groups)]
            if row >= wave_rows:
                return high_ref[pl.ds((freq * 2 + row - wave_rows) * groups, groups)]
            return load_row(source, groups, tiles, row)

        def north(row, fresh):
            if not fresh:
                return speeds_ref[2, row + 1], speeds_ref[3, row + 1]
            value = speed_sin + spread(flow_ref, 1, row + 2)
            up, down = jnp.maximum(value, 0.0), jnp.minimum(value, 0.0)
            if 0 <= row + 1 < wave_rows + 2:
                speeds_ref[2, row + 1], speeds_ref[3, row + 1] = up, down
            return up, down

        def east(row, fresh):
            if not fresh:
                return speeds_ref[0, row + 1], speeds_ref[1, row + 1]
            value = speed_cos + spread(flow_ref, 0, row + 2)
            up, down = jnp.maximum(value, 0.0), jnp.minimum(value, 0.0)
            if 0 <= row < wave_rows:
                speeds_ref[0, row + 1], speeds_ref[1, row + 1] = up, down
            return up, down

        def sweep(read, fresh, low, high, write):
            before = read(low - 1)
            here = read(low)
            up, down = north(low, fresh)
            face_before = north(low - 1, fresh)[0] * before + down * here
            for row in range(low, high):
                after = read(row + 1)
                up_after, down_after = north(row + 1, fresh)
                face_here = up * here + down_after * after
                right, left = east(row, fresh)
                face_x = right * here + roll_lanes(left * here, -1)
                face_turn = turn_ref[0, row + 1] * here + roll_directions(turn_ref[1, row + 1] * here, -1)
                write(
                    row,
                    here
                    - (face_x - roll_lanes(face_x, 1))
                    - (face_here - face_before)
                    - (face_turn - roll_directions(face_turn, 1)),
                )
                face_before, here, up = face_here, after, up_after

        def keep(row, value):
            mid_ref[row + 1] = value

        sweep(cells, True, -1, wave_rows + 1, keep)
        ratio = 0.5 + 0.5 * (start + freq).astype(jnp.float32) / (total_freq - 1)
        amplitude = energy_ref[start + freq] / math.sqrt(directions * total_freq)
        scale, rest = amplitude * ratio, amplitude * (ratio - 0.5)

        def finish(row, value):
            store_row(sink, row, value)
            plain = jnp.sum(value, axis=0)
            weighted = jnp.sum(cos2 * value, axis=0)
            mixed = jnp.sum(cross * value, axis=0)
            sum_ref[0, row] += scale * weighted + rest * plain
            sum_ref[1, row] += scale * (plain - weighted) + rest * plain
            sum_ref[2, row] += scale * mixed

        sweep(lambda row: mid_ref[row + 1], False, 0, wave_rows, finish)
        return carry

    lax.fori_loop(0, freqs, one_frequency, 0)
    for kind in range(3):
        for row in range(wave_rows):
            line = jnp.sum(sum_ref[kind, row], axis=1, keepdims=True)
            for tile in range(tiles):
                stress_ref[kind, row : row + 1, tile * LANES : (tile + 1) * LANES] = line[tile]


def force_terms(own_ref, prev_ref, table_ref, tail_ref, stress_ref, coupling_ref):
    wave_rows, columns = own_ref.shape[1:]
    half = wave_rows // 2
    count = wave_rows + 1
    behind = half + 2
    for kind in range(3):
        stress_ref[kind, 0:behind] = prev_ref[kind, wave_rows - behind : wave_rows]
        stress_ref[kind, behind : behind + half + 1] = own_ref[kind, 0 : half + 1]
    far = half - 1
    lead = tail_ref.shape[0] - -(-9 * far // 8)
    for place in range(9):
        for row in range(far):
            slot = place * far + row
            for tile in range(columns // LANES):
                coupling_ref[place, row : row + 1, tile * LANES : (tile + 1) * LANES] = tail_ref[
                    lead + slot // 8, tile, slot % 8 : slot % 8 + 1, :
                ]
        coupling_ref[place, far:count] = table_ref[place, 0 : count - far]

    def along_x(kind):
        middle = stress_ref[kind, 1 : 1 + count]
        return (pltpu.roll(middle, columns - 1, 1) - pltpu.roll(middle, 1, 1)) * 0.5

    def along_y(kind):
        return (stress_ref[kind, 2 : 2 + count] - stress_ref[kind, 0:count]) * 0.5

    forces = (-(along_x(0) + along_y(2)), -(along_x(2) + along_y(1)))
    return forces


def force_kernel(axis, own_ref, prev_ref, table_ref, tail_ref, current_ref, wet_ref, out_ref,
                 stress_ref, coupling_ref, push_ref, chunk_ref, merge_ref):
    wave_rows, _ = own_ref.shape[1:]
    width = current_ref.shape[2]
    half = width // 2
    forces = force_terms(own_ref, prev_ref, table_ref, tail_ref, stress_ref, coupling_ref)
    count = wave_rows + 1
    start = pl.multiple_of(lax.axis_index(axis) * half, LANES)
    for comp, force in enumerate(forces):
        for step_row in range(3):
            for step_col in range(3):
                push_ref[0, 3 * step_row + step_col, :count] = coupling_ref[3 * step_row + step_col] * force

        def near(place):
            return push_ref[0, place, 1:count]

        def far(place):
            return push_ref[0, place, 0 : count - 1]

        even_even = near(0) + far(6) + pltpu.roll(near(2) + far(8), 1, 1)
        even_odd = near(1) + far(7)
        odd_even = near(3) + pltpu.roll(near(5), 1, 1)
        odd_odd = near(4)
        for parity, (even, odd) in enumerate(((even_even, even_odd), (odd_even, odd_odd))):
            chunk_ref[0, comp, parity] = even
            chunk_ref[1, comp, parity] = odd
    rows = 4 * wave_rows
    even = chunk_ref[0, :, :, :, pl.ds(start, half)].reshape(rows, half)
    odd = chunk_ref[1, :, :, :, pl.ds(start, half)].reshape(rows, half)
    merged = jnp.dot(
        jnp.concatenate([even, odd], axis=1), merge_matrix(width), precision=HIGHEST,
        preferred_element_type=jnp.float32,
    ).reshape(2, 2, wave_rows, width)
    wet = wet_ref[...].astype(jnp.float32)
    for comp in range(2):
        for tile in range(width // LANES):
            lanes = slice(tile * LANES, (tile + 1) * LANES)
            for parity in range(2):
                lines = pl.ds(parity, wave_rows, stride=2)
                merge_ref[comp, tile, lines, :] = merged[comp, parity, :, lanes]
            out_ref[comp, :, lanes] = wet[:, lanes] * (
                damping * current_ref[comp, :, lanes] + force_gain * merge_ref[comp, tile]
            )


def push_kernel(own_ref, prev_ref, table_ref, tail_ref, out_ref, stress_ref, coupling_ref, push_ref):
    wave_rows, _ = own_ref.shape[1:]
    forces = force_terms(own_ref, prev_ref, table_ref, tail_ref, stress_ref, coupling_ref)
    count = wave_rows + 1
    for comp, force in enumerate(forces):
        for place in range(9):
            push_ref[0, place, :count] = coupling_ref[place] * force
        near = [push_ref[0, place, 1:count] for place in range(9)]
        far = [push_ref[0, place, 0 : count - 1] for place in range(9)]
        out_ref[0, comp, 0] = near[0] + far[6] + pltpu.roll(near[2] + far[8], 1, 1)
        out_ref[1, comp, 0] = near[1] + far[7]
        out_ref[0, comp, 1] = near[3] + pltpu.roll(near[5], 1, 1)
        out_ref[1, comp, 1] = near[4]


def window(action, currents, wet, courant, energy, src, weights):
    f32 = jnp.float32
    freqs, directions, wave_rows, columns = action.shape
    groups, tiles = directions // 8, columns // LANES
    list_rows = src.shape[0]
    ocean_rows, width = wet.shape
    spec = lax.axis_size("spec")
    ocean_cols = width * spec
    half = width // 2
    aligned = half % LANES == 0 and spec <= 4
    masked = currents * wet.astype(f32)[None]
    masked_next = from_offset(masked, "space", 1)
    field = jnp.transpose(action.reshape(freqs, directions, wave_rows, tiles, LANES), (0, 1, 3, 2, 4))
    tail_rows = wave_rows // 2 - 1
    lead = freqs * 2 * groups
    tables, low, high = pl.pallas_call(
        functools.partial(prepare_kernel, ocean_cols, tail_rows),
        out_shape=(
            jax.ShapeDtypeStruct((9, list_rows, columns), f32),
            jax.ShapeDtypeStruct((lead + -(-9 * tail_rows // 8), tiles, 8, LANES), f32),
            jax.ShapeDtypeStruct((lead, tiles, 8, LANES), f32),
        ),
        in_specs=[VMEM] * 3,
        out_specs=(VMEM,) * 3,
        compiler_params=params(),
        name="prepare",
    )(jnp.transpose(src, (0, 2, 1)), jnp.transpose(weights, (0, 2, 1)), field)
    low = from_offset(low, "space", -1)
    high = from_offset(high, "space", 1)
    if aligned:
        piece = pl.pallas_call(
            split_kernel,
            out_shape=jax.ShapeDtypeStruct((2, 2 * ocean_rows, width), f32),
            in_specs=[VMEM] * 2,
            out_specs=VMEM,
            compiler_params=params(),
            name="split",
        )(masked, masked_next)
        pieces = [piece] + [from_xor(piece, "spec", bits) for bits in range(1, spec)]
    else:
        both = lax.all_gather(jnp.concatenate([masked, masked_next], axis=1), "spec", axis=2, tiled=True)
        pieces = [jnp.concatenate([both[:, :, 0::2], both[:, :, 1::2]], axis=2)]
    angles = 2.0 * math.pi * (np.arange(directions) + 0.5) / directions
    cosine, sine = np.cos(angles), np.sin(angles)
    trig = np.stack([cosine, sine, sine * cosine, sine * sine, cosine * cosine]).astype(np.float32)
    trig = trig.reshape(5, 8, groups).transpose(0, 2, 1)
    trig = jnp.asarray(np.repeat(trig[:, :, :, None], LANES, axis=3))
    total_freq = freqs * spec
    padded = -(-list_rows // 8) * 8
    out_field, stress = pl.pallas_call(
        functools.partial(advance_kernel, total_freq, "spec", len(pieces)),
        out_shape=(
            jax.ShapeDtypeStruct(field.shape, f32),
            jax.ShapeDtypeStruct((3, wave_rows, columns), f32),
        ),
        in_specs=[VMEM] * len(pieces) + [VMEM, VMEM, SMEM, SMEM, VMEM, VMEM, VMEM],
        out_specs=(VMEM, VMEM),
        scratch_shapes=[
            pltpu.VMEM((2, tiles, 2, 2 * ocean_rows, LANES), f32),
            pltpu.VMEM((2, tiles, padded, LANES), f32),
            pltpu.VMEM((3, tiles, padded, LANES), f32),
            pltpu.VMEM((2, list_rows - 2, groups, tiles, 8, LANES), f32),
            pltpu.VMEM((wave_rows + 2, groups, tiles, 8, LANES), f32),
            pltpu.VMEM((3, wave_rows, tiles, 8, LANES), f32),
            pltpu.VMEM((4, wave_rows + 2, groups, tiles, 8, LANES), f32),
        ],
        compiler_params=params(),
        name="advance",
    )(*pieces, tables, trig, courant, energy, field, low, high)
    new_action = jnp.transpose(out_field, (0, 1, 3, 2, 4)).reshape(action.shape)
    if spec <= 4:
        stress = stress + sum(from_xor(stress, "spec", bits) for bits in range(1, spec))
    else:
        stress = lax.psum(stress, "spec")
    stress_prev = from_offset(stress, "space", -1)
    count = wave_rows + 1
    scratch = [
        pltpu.VMEM((3, 2 * wave_rows, columns), f32),
        pltpu.VMEM((9, count, columns), f32),
        pltpu.VMEM((1, 9, count, columns), f32),
    ]
    if aligned:
        updated = pl.pallas_call(
            functools.partial(force_kernel, "spec"),
            out_shape=jax.ShapeDtypeStruct(currents.shape, f32),
            in_specs=[VMEM] * 6,
            out_specs=VMEM,
            scratch_shapes=scratch
            + [
                pltpu.VMEM((2, 2, 2, wave_rows, columns), f32),
                pltpu.VMEM((2, width // LANES, ocean_rows, LANES), f32),
            ],
            compiler_params=params(),
            name="force",
        )(stress, stress_prev, tables, low, currents, wet)
    else:
        pushed = pl.pallas_call(
            push_kernel,
            out_shape=jax.ShapeDtypeStruct((2, 2, 2, wave_rows, columns), f32),
            in_specs=[VMEM] * 4,
            out_specs=VMEM,
            scratch_shapes=scratch,
            compiler_params=params(),
            name="push",
        )(stress, stress_prev, tables, low)
        grid = jnp.transpose(pushed, (1, 3, 2, 4, 0)).reshape(2, ocean_rows, ocean_cols)
        share = lax.dynamic_slice_in_dim(grid, lax.axis_index("spec") * width, width, 2)
        updated = wet.astype(f32)[None] * (damping * currents + force_gain * share)
    return (new_action, updated)


def solution(mesh):
    in_specs = (
        P("spec", None, "space", None),
        P(None, "space", "spec"),
        P("space", "spec"),
        P(),
        P(),
        P("space", None, None),
        P("space", None, None),
    )
    out_specs = (P("spec", None, "space", None), P(None, "space", "spec"))
    return jax.shard_map(window, mesh=mesh, in_specs=in_specs, out_specs=out_specs, check_vma=False)
```

```python
import functools
import math

import jax
import jax.numpy as jnp
import numpy as np
from jax import lax
from jax.experimental import pallas as pl
from jax.experimental.pallas import tpu as pltpu
from jax.sharding import PartitionSpec as P


drift_factor = 0.2
refract_factor = 1.5
damping = 0.95
force_gain = 0.5

LANES = 128
HIGHEST = lax.Precision.HIGHEST
VMEM = pl.BlockSpec(memory_space=pltpu.VMEM)
SMEM = pl.BlockSpec(memory_space=pltpu.SMEM)
HBM = pl.BlockSpec(memory_space=pltpu.MemorySpace.HBM)
TAIL_VREGS = 4


def from_offset(block, axis, offset):
    count = lax.axis_size(axis)
    return lax.ppermute(block, axis, [((i + offset) % count, i) for i in range(count)])


def from_mesh(block, offset, bits):
    space, spec = lax.axis_size("space"), lax.axis_size("spec")
    route = [
        (((i + offset) % space) * spec + (j ^ bits), i * spec + j) for i in range(space) for j in range(spec)
    ]
    return lax.ppermute(block, ("space", "spec"), route)


def params(**kw):
    return pltpu.CompilerParams(vmem_limit_bytes=48 * 1024 * 1024, **kw)


def split_matrix(width):
    row = lax.broadcasted_iota(jnp.int32, (width, width), 0)
    col = lax.broadcasted_iota(jnp.int32, (width, width), 1)
    half = width // 2
    source = jnp.where(col < half, 2 * col, 2 * (col - half) + 1)
    return (row == source).astype(jnp.float32)


def merge_matrix(width):
    row = lax.broadcasted_iota(jnp.int32, (width, width), 0)
    col = lax.broadcasted_iota(jnp.int32, (width, width), 1)
    half = width // 2
    target = jnp.where(row < half, 2 * row, 2 * (row - half) + 1)
    return (col == target).astype(jnp.float32)


def roll_lanes(x, shift):
    lane = lax.broadcasted_iota(jnp.int32, x.shape, x.ndim - 1)
    turned = pltpu.roll(x, shift % LANES, x.ndim - 1)
    if shift == 1:
        return jnp.where(lane == 0, roll_lead(turned, 1, x.ndim - 3), turned)
    return jnp.where(lane == LANES - 1, roll_lead(turned, -1, x.ndim - 3), turned)


def roll_lead(x, shift, axis):
    count = x.shape[axis]
    cut = (-shift) % count
    if cut == 0:
        return x
    return jnp.concatenate(
        [lax.slice_in_dim(x, cut, count, axis=axis), lax.slice_in_dim(x, 0, cut, axis=axis)], axis=axis
    )


def roll_directions(x, shift):
    groups = x.shape[0]
    if shift == 1:
        edge = pltpu.roll(x[groups - 1 :], 1, 2)
        return jnp.concatenate([edge, x[: groups - 1]], axis=0)
    edge = pltpu.roll(x[:1], 7, 2)
    return jnp.concatenate([x[1:], edge], axis=0)


def row_view(ref, freq):
    return ref.at[freq].reshape(ref.shape[1] * ref.shape[2] * 8, LANES)


def row_slots(groups, tiles, row):
    return [
        [pl.ds((group * tiles + tile) * 8 + row, 8, stride=groups * tiles * 8) for tile in range(tiles)]
        for group in range(groups)
    ]


def load_row(view, groups, tiles, row):
    slots = row_slots(groups, tiles, row)
    return jnp.stack([jnp.stack([view[slot, :] for slot in line]) for line in slots])


def store_row(view, row, value):
    groups, tiles = value.shape[:2]
    for group, line in enumerate(row_slots(groups, tiles, row)):
        for tile, slot in enumerate(line):
            view[slot, :] = value[group, tile]


def tail_slot(tiles, which, slot):
    vreg = which * TAIL_VREGS + slot // 8
    return vreg // tiles, vreg % tiles, slot % 8


def chosen_tiles(axis, aligned, tiles):
    if not aligned:
        return list(range(tiles))
    index = lax.axis_index(axis)
    return [index, lax.rem(index + tiles - 1, tiles)]


def open_kernel(
    ocean_cols, tail_rows, axis, aligned, current_hbm, wet_hbm, src_hbm, weight_hbm, field_hbm,
    masked_ref, wet_out, table_ref, field_ref, low_ref, high_ref,
    current_ref, wet_ref, src_ref, weight_ref, sems,
):
    copies = [
        pltpu.make_async_copy(source, target, sems.at[k])
        for k, (source, target) in enumerate(
            (
                (current_hbm, current_ref),
                (wet_hbm, wet_ref),
                (src_hbm, src_ref),
                (weight_hbm, weight_ref),
                (field_hbm, field_ref),
            )
        )
    ]
    for copy in copies:
        copy.start()
    list_rows, corners, columns = src_ref.shape
    freqs, directions, tiles, wave_rows, _ = field_ref.shape
    groups = directions // 8
    copies[0].wait()
    copies[1].wait()
    wet = wet_ref[...].astype(jnp.float32)
    wet_out[...] = wet
    masked_ref[...] = current_ref[...] * wet[None]
    shape = (list_rows, columns)
    entry_row = lax.broadcasted_iota(jnp.int32, shape, 0)
    column = lax.broadcasted_iota(jnp.int32, shape, 1)
    base = (2 * (entry_row - 2) + wave_rows) * ocean_cols
    cell = [
        base + jnp.where(2 * column + step >= ocean_cols, 2 * column + step - ocean_cols, 2 * column + step)
        for step in range(3)
    ]
    copies[2].wait()
    copies[3].wait()
    sums = [jnp.zeros(shape, jnp.float32) for _ in range(9)]
    for corner in range(corners):
        source = src_ref[:, corner, :]
        weight = weight_ref[:, corner, :]
        for step_row in range(3):
            for step_col in range(3):
                hit = source == cell[step_col] + step_row * ocean_cols
                place = 3 * step_row + step_col
                sums[place] = sums[place] + jnp.where(hit, weight, 0.0)
    for place in range(9):
        for tile in range(tiles):
            table_ref[place, tile, :list_rows] = sums[place][:, tile * LANES : (tile + 1) * LANES]
    first = 2 + wave_rows // 2 - 1
    lead = freqs * 2 * groups
    for which, tile in enumerate(chosen_tiles(axis, aligned, tiles)):
        for place in range(9):
            for row in range(tail_rows):
                block, at, line = tail_slot(tiles, which, place * tail_rows + row)
                low_ref[lead + block, at, line : line + 1, :] = table_ref[
                    place, tile, first + row : first + row + 1, :
                ]
    copies[4].wait()
    for freq in range(freqs):
        view = row_view(field_ref, freq)
        for row in range(2):
            at = (freq * 2 + row) * groups
            low_ref[at : at + groups] = load_row(view, groups, tiles, wave_rows - 2 + row)
            high_ref[at : at + groups] = load_row(view, groups, tiles, row)


def flow_tile(table_ref, tile, evens, odds, nexts):
    total = None
    for step_row in range(3):
        even = evens[step_row]
        list_rows = even.shape[0]
        lane = lax.broadcasted_iota(jnp.int32, even.shape, 1)
        edge = 0.0 if nexts is None else pltpu.roll(nexts[step_row], LANES - 1, 1)
        shifted = jnp.where(lane == LANES - 1, edge, pltpu.roll(even, LANES - 1, 1))
        for step_col, lifted in enumerate((even, odds[step_row], shifted)):
            term = table_ref[3 * step_row + step_col, tile, :list_rows] * lifted
            total = term if total is None else total + term
    return total


def row_steps(ref, parity, tile, comp, first, list_rows):
    return [ref[parity, tile, comp, pl.ds(first + step, list_rows, stride=2), :] for step in range(3)]


def flow_kernel(axis, list_rows, first, own_ref, x_ref, z_ref, xz_ref, table_ref, part_ref, ocean_ref):
    comps, rows, width = own_ref.shape
    tiles = table_ref.shape[1]
    half = width // 2
    index = lax.axis_index(axis)
    place = lax.rem(index, 2)
    matrix = split_matrix(width)
    cells = jnp.concatenate(
        [ref[...].reshape(comps * rows, width) for ref in (own_ref, z_ref, x_ref, xz_ref)], axis=0
    )
    split = jnp.dot(cells, matrix, precision=HIGHEST, preferred_element_type=jnp.float32)
    split = split.reshape(4, comps, rows, width)
    for parity in range(2):
        lanes = slice(parity * half, (parity + 1) * half)
        for block in range(2):
            at = slice(block * rows, (block + 1) * rows)
            ocean_ref[parity, place, :, at] = split[block, :, :, lanes]
            ocean_ref[parity, 1 - place, :, at] = split[2 + block, :, :, lanes]
    tile = index - place
    before = lax.rem(tile + tiles - 1, tiles)
    for comp in range(comps):
        evens = [row_steps(ocean_ref, 0, k, comp, first, list_rows) for k in range(2)]
        odds = [row_steps(ocean_ref, 1, k, comp, first, list_rows) for k in range(2)]
        part_ref[0, comp, :list_rows] = flow_tile(table_ref, tile, evens[0], odds[0], evens[1])
        part_ref[1, comp, :list_rows] = flow_tile(table_ref, tile + 1, evens[1], odds[1], None)
        lane = lax.broadcasted_iota(jnp.int32, (list_rows, LANES), 1)
        spill = None
        for step in range(3):
            edge = jnp.where(lane == LANES - 1, pltpu.roll(evens[0][step], LANES - 1, 1), 0.0)
            term = table_ref[3 * step + 2, before, :list_rows] * edge
            spill = term if spill is None else spill + term
        part_ref[2, comp, :list_rows] = spill


def flow_all_kernel(list_rows, first, ocean_ref, table_ref, flow_ref):
    tiles = table_ref.shape[1]
    for comp in range(2):
        evens = [row_steps(ocean_ref, 0, k, comp, first, list_rows) for k in range(tiles)]
        odds = [row_steps(ocean_ref, 1, k, comp, first, list_rows) for k in range(tiles)]
        for tile in range(tiles):
            flow_ref[tile, comp, :list_rows] = flow_tile(
                table_ref, tile, evens[tile], odds[tile], evens[(tile + 1) % tiles]
            )


def advance_kernel(total_freq, axis, list_rows, parts, *refs):
    part_refs = refs[:parts]
    (trig_ref, speed_ref, energy_ref, field_ref, low_ref, high_ref) = refs[parts : parts + 6]
    out_ref, stress_ref = refs[parts + 6 : parts + 8]
    flow_ref, grad_ref, turn_ref, mid_ref, sum_ref, speeds_ref = refs[parts + 8 :]
    freqs, directions, tiles, wave_rows, _ = field_ref.shape
    groups = directions // 8
    index = lax.axis_index(axis)
    for comp in range(2):
        if parts == 1:
            for tile in range(tiles):
                flow_ref[comp, tile] = part_refs[0][tile, comp]
        else:
            tile = index - lax.rem(index, 2)
            other = tiles // 2 - tile
            own, theirs = part_refs
            flow_ref[comp, tile] = own[0, comp]
            flow_ref[comp, tile + 1] = own[1, comp] + theirs[2, comp]
            flow_ref[comp, other] = theirs[0, comp]
            flow_ref[comp, other + 1] = theirs[1, comp] + own[2, comp]
    inner = list_rows - 2
    east, north = flow_ref[0, :, 1 : 1 + inner], flow_ref[1, :, 1 : 1 + inner]
    east_y = (flow_ref[0, :, 2 : 2 + inner] - flow_ref[0, :, 0:inner]) * 0.5
    north_y = (flow_ref[1, :, 2 : 2 + inner] - flow_ref[1, :, 0:inner]) * 0.5
    east_x = (roll_lanes(east, -1) - roll_lanes(east, 1)) * 0.5
    north_x = (roll_lanes(north, -1) - roll_lanes(north, 1)) * 0.5
    grad_ref[0, :, :inner] = refract_factor * (east_x - north_y)
    grad_ref[1, :, :inner] = refract_factor * east_y
    grad_ref[2, :, :inner] = refract_factor * north_x
    for comp in range(2):
        flow_ref[comp, :, :list_rows] = drift_factor * flow_ref[comp, :, :list_rows]
    full = (groups, tiles, 8, LANES)

    def spread(ref, kind, row):
        lines = [ref[kind, tile, pl.ds(row, 8, stride=0), :] for tile in range(tiles)]
        return jnp.broadcast_to(jnp.stack(lines)[None], full)

    def wide(kind):
        return jnp.broadcast_to(trig_ref[kind][:, None], full)

    cross, sin2, cos2 = wide(2), wide(3), wide(4)
    for row in range(inner):
        turn = cross * spread(grad_ref, 0, row) + sin2 * spread(grad_ref, 1, row) - cos2 * spread(grad_ref, 2, row)
        turn_ref[0, row] = jnp.maximum(turn, 0.0)
        turn_ref[1, row] = jnp.minimum(turn, 0.0)
    sum_ref[...] = jnp.zeros_like(sum_ref)
    start = index * freqs

    def one_frequency(freq, carry):
        speed = speed_ref[start + freq]
        speed_cos = jnp.broadcast_to((speed * trig_ref[0])[:, None], full)
        speed_sin = jnp.broadcast_to((speed * trig_ref[1])[:, None], full)
        source, sink = row_view(field_ref, freq), row_view(out_ref, freq)

        def cells(row):
            if row < 0:
                return low_ref[pl.ds((freq * 2 + 2 + row) * groups, groups)]
            if row >= wave_rows:
                return high_ref[pl.ds((freq * 2 + row - wave_rows) * groups, groups)]
            return load_row(source, groups, tiles, row)

        def north(row, fresh):
            if not fresh:
                return speeds_ref[2, row + 1], speeds_ref[3, row + 1]
            value = speed_sin + spread(flow_ref, 1, row + 2)
            up, down = jnp.maximum(value, 0.0), jnp.minimum(value, 0.0)
            if 0 <= row + 1 < wave_rows + 2:
                speeds_ref[2, row + 1], speeds_ref[3, row + 1] = up, down
            return up, down

        def east(row, fresh):
            if not fresh:
                return speeds_ref[0, row + 1], speeds_ref[1, row + 1]
            value = speed_cos + spread(flow_ref, 0, row + 2)
            up, down = jnp.maximum(value, 0.0), jnp.minimum(value, 0.0)
            if 0 <= row < wave_rows:
                speeds_ref[0, row + 1], speeds_ref[1, row + 1] = up, down
            return up, down

        def sweep(read, fresh, low, high, write):
            before = read(low - 1)
            here = read(low)
            up, down = north(low, fresh)
            face_before = north(low - 1, fresh)[0] * before + down * here
            for row in range(low, high):
                after = read(row + 1)
                up_after, down_after = north(row + 1, fresh)
                face_here = up * here + down_after * after
                right, left = east(row, fresh)
                face_x = right * here + roll_lanes(left * here, -1)
                face_turn = turn_ref[0, row + 1] * here + roll_directions(turn_ref[1, row + 1] * here, -1)
                write(
                    row,
                    here
                    - (face_x - roll_lanes(face_x, 1))
                    - (face_here - face_before)
                    - (face_turn - roll_directions(face_turn, 1)),
                )
                face_before, here, up = face_here, after, up_after

        def keep(row, value):
            mid_ref[row + 1] = value

        sweep(cells, True, -1, wave_rows + 1, keep)
        ratio = 0.5 + 0.5 * (start + freq).astype(jnp.float32) / (total_freq - 1)
        amplitude = energy_ref[start + freq] / math.sqrt(directions * total_freq)
        scale, rest = amplitude * ratio, amplitude * (ratio - 0.5)

        def finish(row, value):
            store_row(sink, row, value)
            plain = jnp.sum(value, axis=0)
            weighted = jnp.sum(cos2 * value, axis=0)
            mixed = jnp.sum(cross * value, axis=0)
            sum_ref[0, row] += scale * weighted + rest * plain
            sum_ref[1, row] += scale * (plain - weighted) + rest * plain
            sum_ref[2, row] += scale * mixed

        sweep(lambda row: mid_ref[row + 1], False, 0, wave_rows, finish)
        return carry

    lax.fori_loop(0, freqs, one_frequency, 0)
    for kind in range(3):
        for row in range(wave_rows):
            line = jnp.sum(sum_ref[kind, row], axis=1, keepdims=True)
            for tile in range(tiles):
                stress_ref[kind, tile, row : row + 1] = line[tile]


def stress_column(own, prev, half):
    return prev[prev.shape[0] - half - 2 :], own[: half + 1]


def edge_tile(after, before):
    lane = lax.broadcasted_iota(jnp.int32, after.shape, after.ndim - 1)
    return jnp.where(lane < LANES // 2, after, before)


def pair_kernel(axis, own_ref, x_ref, z_ref, xz_ref, keep_ref, send_ref):
    kinds, tiles, wave_rows, _ = own_ref.shape
    half = wave_rows // 2
    index = lax.axis_index(axis)
    for target, out_ref in ((index, keep_ref), (index ^ 2, send_ref)):
        after = lax.rem(target + 1, tiles)
        before = lax.rem(target + tiles - 1, tiles)
        for kind in range(kinds):

            def own(tile):
                return own_ref[kind, tile] + x_ref[kind, tile]

            def prev(tile):
                return z_ref[kind, tile] + xz_ref[kind, tile]

            upper, lower = stress_column(own(target), prev(target), half)
            out_ref[0, kind, 0 : half + 2] = upper
            out_ref[0, kind, half + 2 : wave_rows + 3] = lower
            upper, lower = stress_column(
                edge_tile(own(after), own(before)), edge_tile(prev(after), prev(before)), half
            )
            out_ref[1, kind, 0 : half + 2] = upper
            out_ref[1, kind, half + 2 : wave_rows + 3] = lower


def settle_kernel(axis, aligned, tail_rows, field_ref, low_ref, table_ref, out_hbm, coupling_ref, sem):
    copy = pltpu.make_async_copy(field_ref, out_hbm, sem)
    copy.start()
    freqs, directions, tiles, wave_rows, _ = field_ref.shape
    lead = freqs * 2 * (directions // 8)
    count = wave_rows + 1
    for which, tile in enumerate(chosen_tiles(axis, aligned, tiles)):
        for place in range(9):
            for row in range(tail_rows):
                block, at, line = tail_slot(tiles, which, place * tail_rows + row)
                coupling_ref[which, place, row : row + 1, :] = low_ref[lead + block, at, line : line + 1, :]
            coupling_ref[which, place, tail_rows:count] = table_ref[place, tile, 0 : count - tail_rows]
    copy.wait()


def push_tile(stress_ref, coupling_ref, here, edge, push_ref, count):
    lane = lax.broadcasted_iota(jnp.int32, (count, LANES), 1)

    def middle(part, kind):
        return stress_ref[part, kind, 1 : 1 + count]

    def along_y(part, kind):
        return (stress_ref[part, kind, 2 : 2 + count] - stress_ref[part, kind, 0:count]) * 0.5

    def along_x(part, kind):
        tile, rim = middle(0, kind), middle(1, kind)
        after = jnp.where(lane == LANES - 1, pltpu.roll(rim, LANES - 1, 1), pltpu.roll(tile, LANES - 1, 1))
        if part == 0:
            before = jnp.where(lane == 0, pltpu.roll(rim, 1, 1), pltpu.roll(tile, 1, 1))
            return (after - before) * 0.5
        return (pltpu.roll(tile, LANES - 1, 1) - pltpu.roll(rim, 1, 1)) * 0.5

    def forces(part):
        return (
            -(along_x(part, 0) + along_y(part, 2)),
            -(along_x(part, 2) + along_y(part, 1)),
        )

    inner, rim = forces(0), forces(1)
    result = []
    for comp in range(2):
        for place in range(9):
            value = coupling_ref[here, place, :count] * inner[comp]
            if place % 3 == 2:
                spill = coupling_ref[edge, place, :count] * rim[comp]
                value = jnp.where(lane == 0, pltpu.roll(spill, 1, 1), pltpu.roll(value, 1, 1))
            push_ref[place, :count] = value
        near = [push_ref[place, 1:count] for place in range(9)]
        far = [push_ref[place, 0 : count - 1] for place in range(9)]
        result.append(
            (
                (near[0] + far[6] + near[2] + far[8], near[1] + far[7]),
                (near[3] + near[5], near[4]),
            )
        )
    return result


def force_kernel(keep_ref, come_ref, coupling_ref, masked_ref, wet_ref, out_ref, stress_ref, push_ref, merge_ref):
    ocean_rows, width = wet_ref.shape
    wave_rows = ocean_rows // 2
    count = wave_rows + 1
    stress_ref[...] = keep_ref[...] + come_ref[...]
    pushed = push_tile(stress_ref, coupling_ref, 0, 1, push_ref, count)
    cells = jnp.concatenate(
        [
            jnp.concatenate([even, odd], axis=1)
            for component in pushed
            for even, odd in component
        ],
        axis=0,
    )
    merged = jnp.dot(
        cells, merge_matrix(width), precision=HIGHEST, preferred_element_type=jnp.float32
    ).reshape(2, 2, wave_rows, width)
    wet = wet_ref[...]
    for comp in range(2):
        for tile in range(width // LANES):
            lanes = slice(tile * LANES, (tile + 1) * LANES)
            for parity in range(2):
                lines = pl.ds(parity, wave_rows, stride=2)
                merge_ref[comp, tile, lines, :] = merged[comp, parity, :, lanes]
            out_ref[comp, :, lanes] = (
                damping * masked_ref[comp, :, lanes] + force_gain * wet[:, lanes] * merge_ref[comp, tile]
            )


def push_all_kernel(own_ref, prev_ref, coupling_ref, out_ref, stress_ref, push_ref):
    kinds, tiles, wave_rows, _ = own_ref.shape
    half = wave_rows // 2
    for tile in range(tiles):
        after, before = (tile + 1) % tiles, (tile - 1) % tiles
        for kind in range(kinds):
            upper, lower = stress_column(own_ref[kind, tile], prev_ref[kind, tile], half)
            stress_ref[0, kind, 0 : half + 2] = upper
            stress_ref[0, kind, half + 2 : wave_rows + 3] = lower
            upper, lower = stress_column(
                edge_tile(own_ref[kind, after], own_ref[kind, before]),
                edge_tile(prev_ref[kind, after], prev_ref[kind, before]),
                half,
            )
            stress_ref[1, kind, 0 : half + 2] = upper
            stress_ref[1, kind, half + 2 : wave_rows + 3] = lower
        pushed = push_tile(stress_ref, coupling_ref, tile, before, push_ref, wave_rows + 1)
        for comp in range(2):
            for parity in range(2):
                for side in range(2):
                    out_ref[side, comp, parity, tile] = pushed[comp][parity][side]


def call(kernel, outs, ins, out_specs=None, **kw):
    f32 = jnp.float32
    shapes = tuple(jax.ShapeDtypeStruct(shape, f32) for shape in outs)
    if out_specs is None:
        out_specs = (VMEM,) * len(outs)
    return pl.pallas_call(kernel, out_shape=shapes, in_specs=ins, out_specs=out_specs, compiler_params=params(), **kw)


def window(action, currents, wet, courant, energy, src, weights):
    f32 = jnp.float32
    freqs, directions, wave_rows, columns = action.shape
    groups, tiles = directions // 8, columns // LANES
    list_rows = src.shape[0]
    ocean_rows, width = wet.shape
    spec = lax.axis_size("spec")
    ocean_cols = width * spec
    aligned = width == 2 * LANES and spec == 4
    tail_rows = wave_rows // 2 - 1
    lead = freqs * 2 * groups
    chosen = 2 if aligned else tiles
    padded = -(-list_rows // 8) * 8
    first = wave_rows - 4
    field = jnp.transpose(action.reshape(freqs, directions, wave_rows, tiles, LANES), (0, 1, 3, 2, 4))
    source, weight = jnp.transpose(src, (0, 2, 1)), jnp.transpose(weights, (0, 2, 1))
    masked, wet_float, tables, held, low, high = call(
        functools.partial(open_kernel, ocean_cols, tail_rows, "spec", aligned),
        (
            currents.shape,
            wet.shape,
            (9, tiles, padded, LANES),
            field.shape,
            (lead + -(-chosen * TAIL_VREGS // tiles), tiles, 8, LANES),
            (lead, tiles, 8, LANES),
        ),
        [HBM] * 5,
        scratch_shapes=[
            pltpu.VMEM(currents.shape, f32),
            pltpu.VMEM(wet.shape, jnp.int32),
            pltpu.VMEM(source.shape, jnp.int32),
            pltpu.VMEM(weight.shape, f32),
            pltpu.SemaphoreType.DMA((5,)),
        ],
    )(*(pltpu.with_memory_space_constraint(x, pltpu.MemorySpace.HBM) for x in (currents, wet, source, weight, field)))
    if aligned:
        z = from_mesh(masked, 1, 0)
        xz = from_mesh(masked, 1, 1)
        x = from_mesh(masked, 0, 1)
    else:
        z = from_offset(masked, "space", 1)
    low = from_offset(low, "space", -1)
    high = from_offset(high, "space", 1)
    if aligned:
        (part,) = call(
            functools.partial(flow_kernel, "spec", list_rows, first),
            ((3, 2, padded, LANES),),
            [VMEM] * 5,
            scratch_shapes=[pltpu.VMEM((2, 2, 2, 2 * ocean_rows, LANES), f32)],
        )(masked, x, z, xz, tables)
        parts = [part, from_mesh(part, 0, 2)]
    else:
        both = lax.all_gather(jnp.concatenate([masked, z], axis=1), "spec", axis=2, tiled=True)
        ocean = both.reshape(2, 2 * ocean_rows, tiles, LANES, 2).transpose(4, 2, 0, 1, 3)
        parts = call(
            functools.partial(flow_all_kernel, list_rows, first), ((tiles, 2, padded, LANES),), [VMEM] * 2
        )(ocean, tables)
    angles = 2.0 * math.pi * (np.arange(directions) + 0.5) / directions
    cosine, sine = np.cos(angles), np.sin(angles)
    trig = np.stack([cosine, sine, sine * cosine, sine * sine, cosine * cosine]).astype(np.float32)
    trig = trig.reshape(5, 8, groups).transpose(0, 2, 1)
    trig = jnp.asarray(np.repeat(trig[:, :, :, None], LANES, axis=3))
    cell = (groups, tiles, 8, LANES)
    moved, stress = call(
        functools.partial(advance_kernel, freqs * spec, "spec", list_rows, len(parts)),
        (field.shape, (3, tiles, wave_rows, LANES)),
        [VMEM] * (len(parts) + 1) + [SMEM] * 2 + [VMEM] * 3,
        scratch_shapes=[
            pltpu.VMEM((2, tiles, padded, LANES), f32),
            pltpu.VMEM((3, tiles, padded, LANES), f32),
            pltpu.VMEM((2, list_rows - 2) + cell, f32),
            pltpu.VMEM((wave_rows + 2,) + cell, f32),
            pltpu.VMEM((3, wave_rows, tiles, 8, LANES), f32),
            pltpu.VMEM((4, wave_rows + 2) + cell, f32),
        ],
    )(*parts, trig, courant, energy, held, low, high)
    if aligned:
        z = from_mesh(stress, -1, 0)
        xz = from_mesh(stress, -1, 1)
        x = from_mesh(stress, 0, 1)
    out_field, coupling = call(
        functools.partial(settle_kernel, "spec", aligned, tail_rows),
        (field.shape, (chosen, 9, 2 * wave_rows, LANES)),
        [VMEM] * 3,
        out_specs=(HBM, VMEM),
        scratch_shapes=[pltpu.SemaphoreType.DMA(())],
    )(moved, low, tables)
    new_action = jnp.transpose(out_field, (0, 1, 3, 2, 4)).reshape(action.shape)
    column = (2, 3, 2 * wave_rows, LANES)
    scratch = [pltpu.VMEM(column, f32), pltpu.VMEM((9, 2 * wave_rows, LANES), f32)]
    if aligned:
        keep, send = call(functools.partial(pair_kernel, "spec"), (column, column), [VMEM] * 4)(stress, x, z, xz)
        come = from_mesh(send, 0, 2)
        (updated,) = call(
            force_kernel,
            (currents.shape,),
            [VMEM] * 5,
            scratch_shapes=scratch + [pltpu.VMEM((2, width // LANES, ocean_rows, LANES), f32)],
        )(keep, come, coupling, masked, wet_float)
    else:
        stress = lax.psum(stress, "spec")
        prev = from_offset(stress, "space", -1)
        (pushed,) = call(
            push_all_kernel, ((2, 2, 2, tiles, wave_rows, LANES),), [VMEM] * 3, scratch_shapes=scratch
        )(stress, prev, coupling)
        grid = jnp.transpose(pushed, (1, 4, 2, 3, 5, 0)).reshape(2, ocean_rows, ocean_cols)
        share = lax.dynamic_slice_in_dim(grid, lax.axis_index("spec") * width, width, 2)
        updated = damping * masked + force_gain * wet_float[None] * share
    return (new_action, updated)


def solution(mesh):
    in_specs = (
        P("spec", None, "space", None),
        P(None, "space", "spec"),
        P("space", "spec"),
        P(),
        P(),
        P("space", None, None),
        P("space", None, None),
    )
    out_specs = (P("spec", None, "space", None), P(None, "space", "spec"))
    return jax.shard_map(window, mesh=mesh, in_specs=in_specs, out_specs=out_specs, check_vma=False)
```

```python
import functools
import math

import jax
import jax.numpy as jnp
import numpy as np
from jax import lax
from jax.experimental import pallas as pl
from jax.experimental.pallas import tpu as pltpu
from jax.sharding import PartitionSpec as P


drift_factor = 0.2
refract_factor = 1.5
damping = 0.95
force_gain = 0.5

LANES = 128
HIGHEST = lax.Precision.HIGHEST
VMEM = pl.BlockSpec(memory_space=pltpu.VMEM)
SMEM = pl.BlockSpec(memory_space=pltpu.SMEM)
HBM = pl.BlockSpec(memory_space=pltpu.MemorySpace.HBM)
TAIL_VREGS = 4


def from_offset(block, axis, offset):
    count = lax.axis_size(axis)
    return lax.ppermute(block, axis, [((i + offset) % count, i) for i in range(count)])


def from_mesh(block, offset, bits):
    space, spec = lax.axis_size("space"), lax.axis_size("spec")
    route = [
        (((i + offset) % space) * spec + (j ^ bits), i * spec + j) for i in range(space) for j in range(spec)
    ]
    return lax.ppermute(block, ("space", "spec"), route)


def swap_pairs(block, axis, first):
    count = lax.axis_size(axis)
    route = []
    for i in range(first, first + count, 2):
        low, high = i % count, (i + 1) % count
        route += [(low, high), (high, low)]
    return lax.ppermute(block, axis, route)


def params(**kw):
    return pltpu.CompilerParams(vmem_limit_bytes=48 * 1024 * 1024, **kw)


def split_matrix(width):
    row = lax.broadcasted_iota(jnp.int32, (width, width), 0)
    col = lax.broadcasted_iota(jnp.int32, (width, width), 1)
    half = width // 2
    source = jnp.where(col < half, 2 * col, 2 * (col - half) + 1)
    return (row == source).astype(jnp.float32)


def merge_matrix(width):
    row = lax.broadcasted_iota(jnp.int32, (width, width), 0)
    col = lax.broadcasted_iota(jnp.int32, (width, width), 1)
    half = width // 2
    target = jnp.where(row < half, 2 * row, 2 * (row - half) + 1)
    return (col == target).astype(jnp.float32)


def roll_lanes(x, shift):
    lane = lax.broadcasted_iota(jnp.int32, x.shape, x.ndim - 1)
    turned = pltpu.roll(x, shift % LANES, x.ndim - 1)
    if shift == 1:
        return jnp.where(lane == 0, roll_lead(turned, 1, x.ndim - 3), turned)
    return jnp.where(lane == LANES - 1, roll_lead(turned, -1, x.ndim - 3), turned)


def roll_lead(x, shift, axis):
    count = x.shape[axis]
    cut = (-shift) % count
    if cut == 0:
        return x
    return jnp.concatenate(
        [lax.slice_in_dim(x, cut, count, axis=axis), lax.slice_in_dim(x, 0, cut, axis=axis)], axis=axis
    )


def roll_directions(x, shift):
    groups = x.shape[0]
    if shift == 1:
        edge = pltpu.roll(x[groups - 1 :], 1, 2)
        return jnp.concatenate([edge, x[: groups - 1]], axis=0)
    edge = pltpu.roll(x[:1], 7, 2)
    return jnp.concatenate([x[1:], edge], axis=0)


def row_view(ref, freq):
    return ref.at[freq].reshape(ref.shape[1] * ref.shape[2] * 8, LANES)


def row_slots(groups, tiles, row):
    return [
        [pl.ds((group * tiles + tile) * 8 + row, 8, stride=groups * tiles * 8) for tile in range(tiles)]
        for group in range(groups)
    ]


def load_row(view, groups, tiles, row):
    slots = row_slots(groups, tiles, row)
    return jnp.stack([jnp.stack([view[slot, :] for slot in line]) for line in slots])


def store_row(view, row, value):
    groups, tiles = value.shape[:2]
    for group, line in enumerate(row_slots(groups, tiles, row)):
        for tile, slot in enumerate(line):
            view[slot, :] = value[group, tile]


def tail_slot(which, slot):
    return which * TAIL_VREGS + slot // 8, slot % 8


def chosen_tiles(axis, aligned, tiles):
    if not aligned:
        return list(range(tiles))
    index = lax.axis_index(axis)
    return [index, lax.rem(index + tiles - 1, tiles)]


def open_kernel(
    axis, current_hbm, wet_hbm, field_hbm, masked_ref, wet_out, field_ref, near_ref, far_ref,
    current_ref, wet_ref, sems,
):
    copies = [
        pltpu.make_async_copy(source, target, sems.at[k])
        for k, (source, target) in enumerate(
            ((current_hbm, current_ref), (wet_hbm, wet_ref), (field_hbm, field_ref))
        )
    ]
    for copy in copies:
        copy.start()
    freqs, directions, tiles, wave_rows, _ = field_ref.shape
    groups = directions // 8
    copies[0].wait()
    copies[1].wait()
    wet = wet_ref[...].astype(jnp.float32)
    wet_out[...] = wet
    masked_ref[...] = current_ref[...] * wet[None]
    odd = lax.rem(lax.axis_index(axis), 2)
    last = wave_rows - 2
    copies[2].wait()
    for freq in range(freqs):
        view = row_view(field_ref, freq)
        for row in range(2):
            at = (freq * 2 + row) * groups
            near_ref[at : at + groups] = load_row(view, groups, tiles, last * (1 - odd) + row)
            far_ref[at : at + groups] = load_row(view, groups, tiles, last * odd + row)


def tables_kernel(
    ocean_cols, wave_rows, tail_rows, axis, aligned, src_hbm, weight_hbm, table_ref, tail_ref,
    src_ref, weight_ref, sems,
):
    copies = [
        pltpu.make_async_copy(src_hbm, src_ref, sems.at[0]),
        pltpu.make_async_copy(weight_hbm, weight_ref, sems.at[1]),
    ]
    for copy in copies:
        copy.start()
    list_rows, corners, columns = src_ref.shape
    tiles = columns // LANES
    shape = (list_rows, columns)
    entry_row = lax.broadcasted_iota(jnp.int32, shape, 0)
    column = lax.broadcasted_iota(jnp.int32, shape, 1)
    base = (2 * (entry_row - 2) + wave_rows) * ocean_cols
    cell = [
        base + jnp.where(2 * column + step >= ocean_cols, 2 * column + step - ocean_cols, 2 * column + step)
        for step in range(3)
    ]
    for copy in copies:
        copy.wait()
    sums = [jnp.zeros(shape, jnp.float32) for _ in range(9)]
    for corner in range(corners):
        source = src_ref[:, corner, :]
        weight = weight_ref[:, corner, :]
        for step_row in range(3):
            for step_col in range(3):
                hit = source == cell[step_col] + step_row * ocean_cols
                place = 3 * step_row + step_col
                sums[place] = sums[place] + jnp.where(hit, weight, 0.0)
    for place in range(9):
        for tile in range(tiles):
            table_ref[place, tile, :list_rows] = sums[place][:, tile * LANES : (tile + 1) * LANES]
    first = 2 + wave_rows // 2 - 1
    for which, tile in enumerate(chosen_tiles(axis, aligned, tiles)):
        for place in range(9):
            for row in range(tail_rows):
                vreg, line = tail_slot(which, place * tail_rows + row)
                tail_ref[vreg, line : line + 1, :] = table_ref[place, tile, first + row : first + row + 1, :]


def flow_tile(table_ref, tile, evens, odds, nexts):
    total = None
    for step_row in range(3):
        even = evens[step_row]
        list_rows = even.shape[0]
        lane = lax.broadcasted_iota(jnp.int32, even.shape, 1)
        edge = 0.0 if nexts is None else pltpu.roll(nexts[step_row], LANES - 1, 1)
        shifted = jnp.where(lane == LANES - 1, edge, pltpu.roll(even, LANES - 1, 1))
        for step_col, lifted in enumerate((even, odds[step_row], shifted)):
            term = table_ref[3 * step_row + step_col, tile, :list_rows] * lifted
            total = term if total is None else total + term
    return total


def row_steps(ref, parity, tile, comp, first, list_rows):
    return [ref[parity, tile, comp, pl.ds(first + step, list_rows, stride=2), :] for step in range(3)]


def flow_kernel(axis, list_rows, first, own_ref, x_ref, z_ref, xz_ref, table_ref, part_ref, ocean_ref):
    comps, rows, width = own_ref.shape
    tiles = table_ref.shape[1]
    half = width // 2
    index = lax.axis_index(axis)
    place = lax.rem(index, 2)
    matrix = split_matrix(width)
    cells = jnp.concatenate(
        [ref[...].reshape(comps * rows, width) for ref in (own_ref, z_ref, x_ref, xz_ref)], axis=0
    )
    split = jnp.dot(cells, matrix, precision=HIGHEST, preferred_element_type=jnp.float32)
    split = split.reshape(4, comps, rows, width)
    for parity in range(2):
        lanes = slice(parity * half, (parity + 1) * half)
        for block in range(2):
            at = slice(block * rows, (block + 1) * rows)
            ocean_ref[parity, place, :, at] = split[block, :, :, lanes]
            ocean_ref[parity, 1 - place, :, at] = split[2 + block, :, :, lanes]
    tile = index - place
    before = lax.rem(tile + tiles - 1, tiles)
    for comp in range(comps):
        evens = [row_steps(ocean_ref, 0, k, comp, first, list_rows) for k in range(2)]
        odds = [row_steps(ocean_ref, 1, k, comp, first, list_rows) for k in range(2)]
        part_ref[0, comp, :list_rows] = flow_tile(table_ref, tile, evens[0], odds[0], evens[1])
        part_ref[1, comp, :list_rows] = flow_tile(table_ref, tile + 1, evens[1], odds[1], None)
        lane = lax.broadcasted_iota(jnp.int32, (list_rows, LANES), 1)
        spill = None
        for step in range(3):
            edge = jnp.where(lane == LANES - 1, pltpu.roll(evens[0][step], LANES - 1, 1), 0.0)
            term = table_ref[3 * step + 2, before, :list_rows] * edge
            spill = term if spill is None else spill + term
        part_ref[2, comp, :list_rows] = spill


def flow_all_kernel(list_rows, first, ocean_ref, table_ref, flow_ref):
    tiles = table_ref.shape[1]
    for comp in range(2):
        evens = [row_steps(ocean_ref, 0, k, comp, first, list_rows) for k in range(tiles)]
        odds = [row_steps(ocean_ref, 1, k, comp, first, list_rows) for k in range(tiles)]
        for tile in range(tiles):
            flow_ref[tile, comp, :list_rows] = flow_tile(
                table_ref, tile, evens[tile], odds[tile], evens[(tile + 1) % tiles]
            )


def spread_row(ref, lead, row, groups):
    tiles = ref.shape[-3]
    lines = [ref[(*lead, tile, pl.ds(row, 8, stride=0), slice(None))] for tile in range(tiles)]
    return jnp.broadcast_to(jnp.stack(lines)[None], (groups, tiles, 8, LANES))


class Speeds:
    def __init__(self, speed, trig_ref, flow_ref, keep_ref):
        groups, tiles = trig_ref.shape[1], flow_ref.shape[1]
        shape = (groups, tiles, 8, LANES)
        self.groups, self.flow_ref, self.keep_ref = groups, flow_ref, keep_ref
        self.base = [jnp.broadcast_to((speed * trig_ref[k])[:, None], shape) for k in range(2)]
        self.seen = set()

    def parts(self, comp, row):
        slot = row + 2
        if (comp, row) in self.seen:
            return self.keep_ref[2 * comp, slot], self.keep_ref[2 * comp + 1, slot]
        value = self.base[comp] + spread_row(self.flow_ref, (comp,), slot, self.groups)
        up, down = jnp.maximum(value, 0.0), jnp.minimum(value, 0.0)
        self.keep_ref[2 * comp, slot], self.keep_ref[2 * comp + 1, slot] = up, down
        self.seen.add((comp, row))
        return up, down


def sweep(read, speeds, turn_ref, low, high, write):
    here = read(low)
    up, down = speeds.parts(1, low)
    face_before = speeds.parts(1, low - 1)[0] * read(low - 1) + down * here
    for row in range(low, high):
        after = read(row + 1)
        up_after, down_after = speeds.parts(1, row + 1)
        face_here = up * here + down_after * after
        right, left = speeds.parts(0, row)
        face_x = right * here + roll_lanes(left * here, -1)
        face_turn = turn_ref[0, row + 1] * here + roll_directions(turn_ref[1, row + 1] * here, -1)
        write(
            row,
            here
            - (face_x - roll_lanes(face_x, 1))
            - (face_here - face_before)
            - (face_turn - roll_directions(face_turn, 1)),
        )
        face_before, here, up = face_here, after, up_after


def add_stress(value, trig_ref, scale, rest, sum_ref, slot):
    shape = value.shape
    cross = jnp.broadcast_to(trig_ref[2][:, None], shape)
    cos2 = jnp.broadcast_to(trig_ref[4][:, None], shape)
    plain = jnp.sum(value, axis=0)
    weighted = jnp.sum(cos2 * value, axis=0)
    mixed = jnp.sum(cross * value, axis=0)
    sum_ref[0, slot] += scale * weighted + rest * plain
    sum_ref[1, slot] += scale * (plain - weighted) + rest * plain
    sum_ref[2, slot] += scale * mixed


def stress_scales(energy_ref, number, total_freq, directions):
    ratio = 0.5 + 0.5 * number.astype(jnp.float32) / (total_freq - 1)
    amplitude = energy_ref[number] / math.sqrt(directions * total_freq)
    return amplitude * ratio, amplitude * (ratio - 0.5)


def inner_kernel(total_freq, axis, list_rows, parts, *refs):
    part_refs = refs[:parts]
    (trig_ref, speed_ref, energy_ref, field_ref) = refs[parts : parts + 4]
    flow_ref, turn_ref, mid_ref, out_ref, sum_ref = refs[parts + 4 : parts + 9]
    grad_ref, keep_ref = refs[parts + 9 :]
    freqs, directions, tiles, wave_rows, _ = field_ref.shape
    groups = directions // 8
    index = lax.axis_index(axis)
    for comp in range(2):
        if parts == 1:
            for tile in range(tiles):
                flow_ref[comp, tile] = part_refs[0][tile, comp]
        else:
            tile = index - lax.rem(index, 2)
            other = tiles // 2 - tile
            own, theirs = part_refs
            flow_ref[comp, tile] = own[0, comp]
            flow_ref[comp, tile + 1] = own[1, comp] + theirs[2, comp]
            flow_ref[comp, other] = theirs[0, comp]
            flow_ref[comp, other + 1] = theirs[1, comp] + own[2, comp]
    inner = list_rows - 2
    east, north = flow_ref[0, :, 1 : 1 + inner], flow_ref[1, :, 1 : 1 + inner]
    east_y = (flow_ref[0, :, 2 : 2 + inner] - flow_ref[0, :, 0:inner]) * 0.5
    north_y = (flow_ref[1, :, 2 : 2 + inner] - flow_ref[1, :, 0:inner]) * 0.5
    east_x = (roll_lanes(east, -1) - roll_lanes(east, 1)) * 0.5
    north_x = (roll_lanes(north, -1) - roll_lanes(north, 1)) * 0.5
    grad_ref[0, :, :inner] = refract_factor * (east_x - north_y)
    grad_ref[1, :, :inner] = refract_factor * east_y
    grad_ref[2, :, :inner] = refract_factor * north_x
    for comp in range(2):
        flow_ref[comp, :, :list_rows] = drift_factor * flow_ref[comp, :, :list_rows]
    cross, sin2, cos2 = (
        jnp.broadcast_to(trig_ref[k][:, None], (groups, tiles, 8, LANES)) for k in (2, 3, 4)
    )
    for row in range(inner):
        first, second, third = (spread_row(grad_ref, (k,), row, groups) for k in range(3))
        turn = cross * first + sin2 * second - cos2 * third
        turn_ref[0, row] = jnp.maximum(turn, 0.0)
        turn_ref[1, row] = jnp.minimum(turn, 0.0)
    sum_ref[...] = jnp.zeros_like(sum_ref)
    start = index * freqs

    def one_frequency(freq, carry):
        speeds = Speeds(speed_ref[start + freq], trig_ref, flow_ref, keep_ref)
        source = row_view(field_ref, freq)

        def keep(row, value):
            mid_ref[freq, row - 1] = value

        sweep(lambda row: load_row(source, groups, tiles, row), speeds, turn_ref, 1, wave_rows - 1, keep)
        scale, rest = stress_scales(energy_ref, start + freq, total_freq, directions)

        def finish(row, value):
            out_ref[freq, row - 2] = value
            add_stress(value, trig_ref, scale, rest, sum_ref, row - 2)

        sweep(lambda row: mid_ref[freq, row - 1], speeds, turn_ref, 2, wave_rows - 2, finish)
        return carry

    lax.fori_loop(0, freqs, one_frequency, 0)


def outer_kernel(
    total_freq, axes, trig_ref, speed_ref, energy_ref, field_ref, near_ref, far_ref, flow_ref, turn_ref,
    mid_ref, inner_ref, out_ref, stress_ref, rim_ref, sum_ref, keep_ref,
):
    freqs, directions, tiles, wave_rows, _ = field_ref.shape
    groups = directions // 8
    start = lax.axis_index(axes[1]) * freqs
    odd = lax.rem(lax.axis_index(axes[0]), 2) == 1
    sum_ref[...] = jnp.zeros_like(sum_ref)
    rim = {-1: 0, 0: 1, wave_rows - 1: 2, wave_rows: 3}
    last = {0: 0, 1: 1, wave_rows - 2: 2, wave_rows - 1: 3}

    def one_frequency(freq, carry):
        speeds = Speeds(speed_ref[start + freq], trig_ref, flow_ref, keep_ref)
        source = row_view(field_ref, freq)

        def cells(row):
            if 0 <= row < wave_rows:
                return load_row(source, groups, tiles, row)
            at = pl.ds((freq * 2 + row % 2) * groups, groups)
            near, far = near_ref[at], far_ref[at]
            return jnp.where(odd, near, far) if row < 0 else jnp.where(odd, far, near)

        def keep(row, value):
            rim_ref[rim[row]] = value

        def middle(row):
            return rim_ref[rim[row]] if row in rim else mid_ref[freq, row - 1]

        scale, rest = stress_scales(energy_ref, start + freq, total_freq, directions)

        def finish(row, value):
            out_ref[freq, last[row]] = value
            add_stress(value, trig_ref, scale, rest, sum_ref, last[row])

        sweep(cells, speeds, turn_ref, -1, 1, keep)
        sweep(cells, speeds, turn_ref, wave_rows - 1, wave_rows + 1, keep)
        sweep(middle, speeds, turn_ref, 0, 2, finish)
        sweep(middle, speeds, turn_ref, wave_rows - 2, wave_rows, finish)
        return carry

    lax.fori_loop(0, freqs, one_frequency, 0)
    for kind in range(3):
        for row in range(wave_rows):
            part = sum_ref[kind, last[row]] if row in last else inner_ref[kind, row - 2]
            line = jnp.sum(part, axis=1, keepdims=True)
            for tile in range(tiles):
                stress_ref[kind, tile, row : row + 1] = line[tile]


def stress_column(own, prev, half):
    return prev[prev.shape[0] - half - 2 :], own[: half + 1]


def edge_tile(after, before):
    lane = lax.broadcasted_iota(jnp.int32, after.shape, after.ndim - 1)
    return jnp.where(lane < LANES // 2, after, before)


def pair_kernel(axis, own_ref, x_ref, z_ref, xz_ref, keep_ref, send_ref):
    kinds, tiles, wave_rows, _ = own_ref.shape
    half = wave_rows // 2
    index = lax.axis_index(axis)
    for target, out_ref in ((index, keep_ref), (index ^ 2, send_ref)):
        after = lax.rem(target + 1, tiles)
        before = lax.rem(target + tiles - 1, tiles)
        for kind in range(kinds):

            def own(tile):
                return own_ref[kind, tile] + x_ref[kind, tile]

            def prev(tile):
                return z_ref[kind, tile] + xz_ref[kind, tile]

            upper, lower = stress_column(own(target), prev(target), half)
            out_ref[0, kind, 0 : half + 2] = upper
            out_ref[0, kind, half + 2 : wave_rows + 3] = lower
            upper, lower = stress_column(
                edge_tile(own(after), own(before)), edge_tile(prev(after), prev(before)), half
            )
            out_ref[1, kind, 0 : half + 2] = upper
            out_ref[1, kind, half + 2 : wave_rows + 3] = lower


def settle_kernel(
    axis, aligned, tail_rows, inner_ref, outer_ref, tail_ref, table_ref, out_hbm, coupling_ref, field_ref, sems
):
    freqs, _, tiles, wave_rows, _ = field_ref.shape
    copies = []
    for freq in range(freqs):
        sink = row_view(field_ref, freq)
        for row in range(wave_rows):
            if 2 <= row < wave_rows - 2:
                store_row(sink, row, inner_ref[freq, row - 2])
            else:
                store_row(sink, row, outer_ref[freq, row if row < 2 else row - wave_rows + 4])
        copies.append(pltpu.make_async_copy(field_ref.at[freq], out_hbm.at[freq], sems.at[freq]))
        copies[-1].start()
    count = wave_rows + 1
    for which, tile in enumerate(chosen_tiles(axis, aligned, tiles)):
        for place in range(9):
            for row in range(tail_rows):
                vreg, line = tail_slot(which, place * tail_rows + row)
                coupling_ref[which, place, row : row + 1, :] = tail_ref[vreg, line : line + 1, :]
            coupling_ref[which, place, tail_rows:count] = table_ref[place, tile, 0 : count - tail_rows]
    for copy in copies:
        copy.wait()


def push_tile(stress_ref, coupling_ref, here, edge, push_ref, count):
    lane = lax.broadcasted_iota(jnp.int32, (count, LANES), 1)

    def middle(part, kind):
        return stress_ref[part, kind, 1 : 1 + count]

    def along_y(part, kind):
        return (stress_ref[part, kind, 2 : 2 + count] - stress_ref[part, kind, 0:count]) * 0.5

    def along_x(part, kind):
        tile, rim = middle(0, kind), middle(1, kind)
        after = jnp.where(lane == LANES - 1, pltpu.roll(rim, LANES - 1, 1), pltpu.roll(tile, LANES - 1, 1))
        if part == 0:
            before = jnp.where(lane == 0, pltpu.roll(rim, 1, 1), pltpu.roll(tile, 1, 1))
            return (after - before) * 0.5
        return (pltpu.roll(tile, LANES - 1, 1) - pltpu.roll(rim, 1, 1)) * 0.5

    def forces(part):
        return (
            -(along_x(part, 0) + along_y(part, 2)),
            -(along_x(part, 2) + along_y(part, 1)),
        )

    inner, rim = forces(0), forces(1)
    result = []
    for comp in range(2):
        for place in range(9):
            value = coupling_ref[here, place, :count] * inner[comp]
            if place % 3 == 2:
                spill = coupling_ref[edge, place, :count] * rim[comp]
                value = jnp.where(lane == 0, pltpu.roll(spill, 1, 1), pltpu.roll(value, 1, 1))
            push_ref[place, :count] = value
        near = [push_ref[place, 1:count] for place in range(9)]
        far = [push_ref[place, 0 : count - 1] for place in range(9)]
        result.append(
            (
                (near[0] + far[6] + near[2] + far[8], near[1] + far[7]),
                (near[3] + near[5], near[4]),
            )
        )
    return result


def force_kernel(keep_ref, come_ref, coupling_ref, masked_ref, wet_ref, out_ref, stress_ref, push_ref, merge_ref):
    ocean_rows, width = wet_ref.shape
    wave_rows = ocean_rows // 2
    count = wave_rows + 1
    stress_ref[...] = keep_ref[...] + come_ref[...]
    pushed = push_tile(stress_ref, coupling_ref, 0, 1, push_ref, count)
    cells = jnp.concatenate(
        [
            jnp.concatenate([even, odd], axis=1)
            for component in pushed
            for even, odd in component
        ],
        axis=0,
    )
    merged = jnp.dot(
        cells, merge_matrix(width), precision=HIGHEST, preferred_element_type=jnp.float32
    ).reshape(2, 2, wave_rows, width)
    wet = wet_ref[...]
    for comp in range(2):
        for tile in range(width // LANES):
            lanes = slice(tile * LANES, (tile + 1) * LANES)
            for parity in range(2):
                lines = pl.ds(parity, wave_rows, stride=2)
                merge_ref[comp, tile, lines, :] = merged[comp, parity, :, lanes]
            out_ref[comp, :, lanes] = (
                damping * masked_ref[comp, :, lanes] + force_gain * wet[:, lanes] * merge_ref[comp, tile]
            )


def push_all_kernel(own_ref, prev_ref, coupling_ref, out_ref, stress_ref, push_ref):
    kinds, tiles, wave_rows, _ = own_ref.shape
    half = wave_rows // 2
    for tile in range(tiles):
        after, before = (tile + 1) % tiles, (tile - 1) % tiles
        for kind in range(kinds):
            upper, lower = stress_column(own_ref[kind, tile], prev_ref[kind, tile], half)
            stress_ref[0, kind, 0 : half + 2] = upper
            stress_ref[0, kind, half + 2 : wave_rows + 3] = lower
            upper, lower = stress_column(
                edge_tile(own_ref[kind, after], own_ref[kind, before]),
                edge_tile(prev_ref[kind, after], prev_ref[kind, before]),
                half,
            )
            stress_ref[1, kind, 0 : half + 2] = upper
            stress_ref[1, kind, half + 2 : wave_rows + 3] = lower
        pushed = push_tile(stress_ref, coupling_ref, tile, before, push_ref, wave_rows + 1)
        for comp in range(2):
            for parity in range(2):
                for side in range(2):
                    out_ref[side, comp, parity, tile] = pushed[comp][parity][side]


def call(kernel, outs, ins, out_specs=None, **kw):
    f32 = jnp.float32
    shapes = tuple(jax.ShapeDtypeStruct(shape, f32) for shape in outs)
    if out_specs is None:
        out_specs = (VMEM,) * len(outs)
    return pl.pallas_call(kernel, out_shape=shapes, in_specs=ins, out_specs=out_specs, compiler_params=params(), **kw)


def in_hbm(*arrays):
    return [pltpu.with_memory_space_constraint(x, pltpu.MemorySpace.HBM) for x in arrays]


def window(action, currents, wet, courant, energy, src, weights):
    f32 = jnp.float32
    freqs, directions, wave_rows, columns = action.shape
    groups, tiles = directions // 8, columns // LANES
    list_rows = src.shape[0]
    ocean_rows, width = wet.shape
    spec = lax.axis_size("spec")
    ocean_cols = width * spec
    aligned = width == 2 * LANES and spec == 4
    tail_rows = wave_rows // 2 - 1
    lead = freqs * 2 * groups
    chosen = 2 if aligned else tiles
    padded = -(-list_rows // 8) * 8
    first = wave_rows - 4
    field = jnp.transpose(action.reshape(freqs, directions, wave_rows, tiles, LANES), (0, 1, 3, 2, 4))
    source, weight = jnp.transpose(src, (0, 2, 1)), jnp.transpose(weights, (0, 2, 1))
    cell = (groups, tiles, 8, LANES)
    masked, wet_float, held, near, far = call(
        functools.partial(open_kernel, "space"),
        (currents.shape, wet.shape, field.shape, (lead, tiles, 8, LANES), (lead, tiles, 8, LANES)),
        [HBM] * 3,
        scratch_shapes=[
            pltpu.VMEM(currents.shape, f32),
            pltpu.VMEM(wet.shape, jnp.int32),
            pltpu.SemaphoreType.DMA((3,)),
        ],
    )(*in_hbm(currents, wet, field))
    if aligned:
        xz = from_mesh(masked, 1, 1)
        z = from_mesh(masked, 1, 0)
        x = from_mesh(masked, 0, 1)
    else:
        z = from_offset(masked, "space", 1)
    far = swap_pairs(far, "space", 1)
    near = swap_pairs(near, "space", 0)
    tables, tail = call(
        functools.partial(tables_kernel, ocean_cols, wave_rows, tail_rows, "spec", aligned),
        ((9, tiles, padded, LANES), (chosen * TAIL_VREGS, 8, LANES)),
        [HBM] * 2,
        scratch_shapes=[
            pltpu.VMEM(source.shape, jnp.int32),
            pltpu.VMEM(weight.shape, f32),
            pltpu.SemaphoreType.DMA((2,)),
        ],
    )(*in_hbm(source, weight))
    tail = from_offset(tail, "space", -1)
    if aligned:
        (part,) = call(
            functools.partial(flow_kernel, "spec", list_rows, first),
            ((3, 2, padded, LANES),),
            [VMEM] * 5,
            scratch_shapes=[pltpu.VMEM((2, 2, 2, 2 * ocean_rows, LANES), f32)],
        )(masked, x, z, xz, tables)
        parts = [part, from_mesh(part, 0, 2)]
    else:
        both = lax.all_gather(jnp.concatenate([masked, z], axis=1), "spec", axis=2, tiled=True)
        ocean = both.reshape(2, 2 * ocean_rows, tiles, LANES, 2).transpose(4, 2, 0, 1, 3)
        parts = call(
            functools.partial(flow_all_kernel, list_rows, first), ((tiles, 2, padded, LANES),), [VMEM] * 2
        )(ocean, tables)
    angles = 2.0 * math.pi * (np.arange(directions) + 0.5) / directions
    cosine, sine = np.cos(angles), np.sin(angles)
    trig = np.stack([cosine, sine, sine * cosine, sine * sine, cosine * cosine]).astype(np.float32)
    trig = trig.reshape(5, 8, groups).transpose(0, 2, 1)
    trig = jnp.asarray(np.repeat(trig[:, :, :, None], LANES, axis=3))
    flow, turn, middle, inner, inner_stress = call(
        functools.partial(inner_kernel, freqs * spec, "spec", list_rows, len(parts)),
        (
            (2, tiles, padded, LANES),
            (2, list_rows - 2) + cell,
            (freqs, wave_rows - 2) + cell,
            (freqs, wave_rows - 4) + cell,
            (3, wave_rows - 4, tiles, 8, LANES),
        ),
        [VMEM] * (len(parts) + 1) + [SMEM] * 2 + [VMEM],
        scratch_shapes=[
            pltpu.VMEM((3, tiles, padded, LANES), f32),
            pltpu.VMEM((4, list_rows) + cell, f32),
        ],
    )(*parts, trig, courant, energy, held)
    outer, stress = call(
        functools.partial(outer_kernel, freqs * spec, ("space", "spec")),
        ((freqs, 4) + cell, (3, tiles, wave_rows, LANES)),
        [VMEM] + [SMEM] * 2 + [VMEM] * 7,
        scratch_shapes=[
            pltpu.VMEM((4,) + cell, f32),
            pltpu.VMEM((3, 4, tiles, 8, LANES), f32),
            pltpu.VMEM((4, list_rows) + cell, f32),
        ],
    )(trig, courant, energy, held, near, far, flow, turn, middle, inner_stress)
    if aligned:
        xz = from_mesh(stress, -1, 1)
        z = from_mesh(stress, -1, 0)
        x = from_mesh(stress, 0, 1)
    out_field, coupling = call(
        functools.partial(settle_kernel, "spec", aligned, tail_rows),
        (field.shape, (chosen, 9, 2 * wave_rows, LANES)),
        [VMEM] * 4,
        out_specs=(HBM, VMEM),
        scratch_shapes=[pltpu.VMEM(field.shape, f32), pltpu.SemaphoreType.DMA((freqs,))],
    )(inner, outer, tail, tables)
    new_action = jnp.transpose(out_field, (0, 1, 3, 2, 4)).reshape(action.shape)
    column = (2, 3, 2 * wave_rows, LANES)
    scratch = [pltpu.VMEM(column, f32), pltpu.VMEM((9, 2 * wave_rows, LANES), f32)]
    if aligned:
        keep, send = call(functools.partial(pair_kernel, "spec"), (column, column), [VMEM] * 4)(stress, x, z, xz)
        come = from_mesh(send, 0, 2)
        (updated,) = call(
            force_kernel,
            (currents.shape,),
            [VMEM] * 5,
            scratch_shapes=scratch + [pltpu.VMEM((2, width // LANES, ocean_rows, LANES), f32)],
        )(keep, come, coupling, masked, wet_float)
    else:
        stress = lax.psum(stress, "spec")
        prev = from_offset(stress, "space", -1)
        (pushed,) = call(
            push_all_kernel, ((2, 2, 2, tiles, wave_rows, LANES),), [VMEM] * 3, scratch_shapes=scratch
        )(stress, prev, coupling)
        grid = jnp.transpose(pushed, (1, 4, 2, 3, 5, 0)).reshape(2, ocean_rows, ocean_cols)
        share = lax.dynamic_slice_in_dim(grid, lax.axis_index("spec") * width, width, 2)
        updated = damping * masked + force_gain * wet_float[None] * share
    return (new_action, updated)


def solution(mesh):
    in_specs = (
        P("spec", None, "space", None),
        P(None, "space", "spec"),
        P("space", "spec"),
        P(),
        P(),
        P("space", None, None),
        P("space", None, None),
    )
    out_specs = (P("spec", None, "space", None), P(None, "space", "spec"))
    return jax.shard_map(window, mesh=mesh, in_specs=in_specs, out_specs=out_specs, check_vma=False)
```

```python
import functools
import math

import jax
import jax.numpy as jnp
import numpy as np
from jax import lax
from jax.experimental import pallas as pl
from jax.experimental.pallas import tpu as pltpu
from jax.sharding import PartitionSpec as P


drift_factor = 0.2
refract_factor = 1.5
damping = 0.95
force_gain = 0.5

LANES = 128
HIGHEST = lax.Precision.HIGHEST
VMEM = pl.BlockSpec(memory_space=pltpu.VMEM)
SMEM = pl.BlockSpec(memory_space=pltpu.SMEM)
HBM = pl.BlockSpec(memory_space=pltpu.MemorySpace.HBM)
TAIL_VREGS = 4


def from_offset(block, axis, offset):
    count = lax.axis_size(axis)
    return lax.ppermute(block, axis, [((i + offset) % count, i) for i in range(count)])


def from_mesh(block, offset, bits):
    space, spec = lax.axis_size("space"), lax.axis_size("spec")
    route = [
        (((i + offset) % space) * spec + (j ^ bits), i * spec + j) for i in range(space) for j in range(spec)
    ]
    return lax.ppermute(block, ("space", "spec"), route)


def params(**kw):
    return pltpu.CompilerParams(vmem_limit_bytes=48 * 1024 * 1024, **kw)


def split_matrix(width):
    row = lax.broadcasted_iota(jnp.int32, (width, width), 0)
    col = lax.broadcasted_iota(jnp.int32, (width, width), 1)
    half = width // 2
    source = jnp.where(col < half, 2 * col, 2 * (col - half) + 1)
    return (row == source).astype(jnp.float32)


def merge_matrix(width):
    row = lax.broadcasted_iota(jnp.int32, (width, width), 0)
    col = lax.broadcasted_iota(jnp.int32, (width, width), 1)
    half = width // 2
    target = jnp.where(row < half, 2 * row, 2 * (row - half) + 1)
    return (col == target).astype(jnp.float32)


def roll_lanes(x, shift):
    lane = lax.broadcasted_iota(jnp.int32, x.shape, x.ndim - 1)
    turned = pltpu.roll(x, shift % LANES, x.ndim - 1)
    if shift == 1:
        return jnp.where(lane == 0, roll_lead(turned, 1, x.ndim - 3), turned)
    return jnp.where(lane == LANES - 1, roll_lead(turned, -1, x.ndim - 3), turned)


def roll_lead(x, shift, axis):
    count = x.shape[axis]
    cut = (-shift) % count
    if cut == 0:
        return x
    return jnp.concatenate(
        [lax.slice_in_dim(x, cut, count, axis=axis), lax.slice_in_dim(x, 0, cut, axis=axis)], axis=axis
    )


def roll_directions(x, shift):
    groups = x.shape[0]
    if shift == 1:
        edge = pltpu.roll(x[groups - 1 :], 1, 2)
        return jnp.concatenate([edge, x[: groups - 1]], axis=0)
    edge = pltpu.roll(x[:1], 7, 2)
    return jnp.concatenate([x[1:], edge], axis=0)


def row_view(ref, freq):
    return ref.at[freq].reshape(ref.shape[1] * ref.shape[2] * 8, LANES)


def row_slots(groups, tiles, row):
    return [
        [pl.ds((tile * 8 * groups + group) * 8 + row, 8, stride=groups * 8) for tile in range(tiles)]
        for group in range(groups)
    ]


def load_row(view, groups, tiles, row):
    slots = row_slots(groups, tiles, row)
    return jnp.stack([jnp.stack([view[slot, :] for slot in line]) for line in slots])


def store_row(view, row, value):
    groups, tiles = value.shape[:2]
    for group, line in enumerate(row_slots(groups, tiles, row)):
        for tile, slot in enumerate(line):
            view[slot, :] = value[group, tile]


def tail_slot(which, slot):
    return which * TAIL_VREGS + slot // 8, slot % 8


def chosen_tiles(axis, aligned, tiles):
    if not aligned:
        return list(range(tiles))
    index = lax.axis_index(axis)
    return [index, lax.rem(index + tiles - 1, tiles)]


def tile_copies(tiled, whole, sems, out):
    freqs, tiles = tiled.shape[:2]
    for freq in range(freqs):
        for tile in range(tiles):
            ends = (tiled.at[freq, tile], whole.at[freq, :, tile])
            yield freq, pltpu.make_async_copy(*(ends if out else ends[::-1]), sems.at[freq, tile])


def open_kernel(
    ocean_cols, tail_rows, axis, aligned, current_hbm, wet_hbm, src_hbm, weight_hbm, field_hbm,
    masked_ref, wet_out, table_ref, tail_ref, field_ref, low_ref, high_ref,
    current_ref, wet_ref, src_ref, weight_ref, sems, field_sems,
):
    copies = [
        pltpu.make_async_copy(source, target, sems.at[k])
        for k, (source, target) in enumerate(
            (
                (current_hbm, current_ref),
                (wet_hbm, wet_ref),
                (src_hbm, src_ref),
                (weight_hbm, weight_ref),
            )
        )
    ]
    moves = list(tile_copies(field_ref, field_hbm, field_sems, False))
    for copy in copies:
        copy.start()
    for _, copy in moves:
        copy.start()
    list_rows, corners, columns = src_ref.shape
    freqs, tiles, directions, wave_rows, _ = field_ref.shape
    groups = directions // 8
    copies[0].wait()
    copies[1].wait()
    wet = wet_ref[...].astype(jnp.float32)
    wet_out[...] = wet
    masked_ref[...] = current_ref[...] * wet[None]
    shape = (list_rows, columns)
    entry_row = lax.broadcasted_iota(jnp.int32, shape, 0)
    column = lax.broadcasted_iota(jnp.int32, shape, 1)
    base = (2 * (entry_row - 2) + wave_rows) * ocean_cols
    cell = [
        base + jnp.where(2 * column + step >= ocean_cols, 2 * column + step - ocean_cols, 2 * column + step)
        for step in range(3)
    ]
    copies[2].wait()
    copies[3].wait()
    sums = [jnp.zeros(shape, jnp.float32) for _ in range(9)]
    for corner in range(corners):
        source = src_ref[:, corner, :]
        weight = weight_ref[:, corner, :]
        for step_row in range(3):
            for step_col in range(3):
                hit = source == cell[step_col] + step_row * ocean_cols
                place = 3 * step_row + step_col
                sums[place] = sums[place] + jnp.where(hit, weight, 0.0)
    for place in range(9):
        for tile in range(tiles):
            table_ref[place, tile, :list_rows] = sums[place][:, tile * LANES : (tile + 1) * LANES]
    first = 2 + wave_rows // 2 - 1
    for which, tile in enumerate(chosen_tiles(axis, aligned, tiles)):
        for place in range(9):
            for row in range(tail_rows):
                vreg, line = tail_slot(which, place * tail_rows + row)
                tail_ref[vreg, line : line + 1, :] = table_ref[place, tile, first + row : first + row + 1, :]
    for freq in range(freqs):
        for other, copy in moves:
            if other == freq:
                copy.wait()
        view = row_view(field_ref, freq)
        for row in range(2):
            at = (freq * 2 + row) * groups
            low_ref[at : at + groups] = load_row(view, groups, tiles, wave_rows - 2 + row)
            high_ref[at : at + groups] = load_row(view, groups, tiles, row)


def flow_tile(table_ref, tile, evens, odds, nexts):
    total = None
    for step_row in range(3):
        even = evens[step_row]
        list_rows = even.shape[0]
        lane = lax.broadcasted_iota(jnp.int32, even.shape, 1)
        edge = 0.0 if nexts is None else pltpu.roll(nexts[step_row], LANES - 1, 1)
        shifted = jnp.where(lane == LANES - 1, edge, pltpu.roll(even, LANES - 1, 1))
        for step_col, lifted in enumerate((even, odds[step_row], shifted)):
            term = table_ref[3 * step_row + step_col, tile, :list_rows] * lifted
            total = term if total is None else total + term
    return total


def row_steps(ref, parity, tile, comp, first, list_rows):
    return [ref[parity, tile, comp, pl.ds(first + step, list_rows, stride=2), :] for step in range(3)]


def flow_kernel(axis, list_rows, first, own_ref, x_ref, z_ref, xz_ref, table_ref, part_ref, ocean_ref):
    comps, rows, width = own_ref.shape
    tiles = table_ref.shape[1]
    half = width // 2
    index = lax.axis_index(axis)
    place = lax.rem(index, 2)
    matrix = split_matrix(width)
    cells = jnp.concatenate(
        [ref[...].reshape(comps * rows, width) for ref in (own_ref, z_ref, x_ref, xz_ref)], axis=0
    )
    split = jnp.dot(cells, matrix, precision=HIGHEST, preferred_element_type=jnp.float32)
    split = split.reshape(4, comps, rows, width)
    for parity in range(2):
        lanes = slice(parity * half, (parity + 1) * half)
        for block in range(2):
            at = slice(block * rows, (block + 1) * rows)
            ocean_ref[parity, place, :, at] = split[block, :, :, lanes]
            ocean_ref[parity, 1 - place, :, at] = split[2 + block, :, :, lanes]
    tile = index - place
    before = lax.rem(tile + tiles - 1, tiles)
    for comp in range(comps):
        evens = [row_steps(ocean_ref, 0, k, comp, first, list_rows) for k in range(2)]
        odds = [row_steps(ocean_ref, 1, k, comp, first, list_rows) for k in range(2)]
        part_ref[0, comp, :list_rows] = flow_tile(table_ref, tile, evens[0], odds[0], evens[1])
        part_ref[1, comp, :list_rows] = flow_tile(table_ref, tile + 1, evens[1], odds[1], None)
        lane = lax.broadcasted_iota(jnp.int32, (list_rows, LANES), 1)
        spill = None
        for step in range(3):
            edge = jnp.where(lane == LANES - 1, pltpu.roll(evens[0][step], LANES - 1, 1), 0.0)
            term = table_ref[3 * step + 2, before, :list_rows] * edge
            spill = term if spill is None else spill + term
        part_ref[2, comp, :list_rows] = spill


def flow_all_kernel(list_rows, first, ocean_ref, table_ref, flow_ref):
    tiles = table_ref.shape[1]
    for comp in range(2):
        evens = [row_steps(ocean_ref, 0, k, comp, first, list_rows) for k in range(tiles)]
        odds = [row_steps(ocean_ref, 1, k, comp, first, list_rows) for k in range(tiles)]
        for tile in range(tiles):
            flow_ref[tile, comp, :list_rows] = flow_tile(
                table_ref, tile, evens[tile], odds[tile], evens[(tile + 1) % tiles]
            )


def spread_row(ref, lead, row, groups):
    tiles = ref.shape[-3]
    lines = [ref[(*lead, tile, pl.ds(row, 8, stride=0), slice(None))] for tile in range(tiles)]
    return jnp.broadcast_to(jnp.stack(lines)[None], (groups, tiles, 8, LANES))


class Speeds:
    def __init__(self, speed, trig_ref, flow_ref, keep_ref):
        groups, tiles = trig_ref.shape[1], flow_ref.shape[1]
        shape = (groups, tiles, 8, LANES)
        self.groups, self.flow_ref, self.keep_ref = groups, flow_ref, keep_ref
        self.base = [jnp.broadcast_to((speed * trig_ref[k])[:, None], shape) for k in range(2)]
        self.seen = set()

    def parts(self, comp, row):
        slot = row + 2
        if (comp, row) in self.seen:
            return self.keep_ref[2 * comp, slot], self.keep_ref[2 * comp + 1, slot]
        value = self.base[comp] + spread_row(self.flow_ref, (comp,), slot, self.groups)
        up, down = jnp.maximum(value, 0.0), jnp.minimum(value, 0.0)
        self.keep_ref[2 * comp, slot], self.keep_ref[2 * comp + 1, slot] = up, down
        self.seen.add((comp, row))
        return up, down


def sweep(read, speeds, turn_ref, low, high, write):
    here = read(low)
    up, down = speeds.parts(1, low)
    face_before = speeds.parts(1, low - 1)[0] * read(low - 1) + down * here
    for row in range(low, high):
        after = read(row + 1)
        up_after, down_after = speeds.parts(1, row + 1)
        face_here = up * here + down_after * after
        right, left = speeds.parts(0, row)
        face_x = right * here + roll_lanes(left * here, -1)
        face_turn = turn_ref[0, row + 1] * here + roll_directions(turn_ref[1, row + 1] * here, -1)
        write(
            row,
            here
            - (face_x - roll_lanes(face_x, 1))
            - (face_here - face_before)
            - (face_turn - roll_directions(face_turn, 1)),
        )
        face_before, here, up = face_here, after, up_after


def add_stress(value, trig_ref, scale, rest, sum_ref, slot):
    shape = value.shape
    cross = jnp.broadcast_to(trig_ref[2][:, None], shape)
    cos2 = jnp.broadcast_to(trig_ref[4][:, None], shape)
    plain = jnp.sum(value, axis=0)
    weighted = jnp.sum(cos2 * value, axis=0)
    mixed = jnp.sum(cross * value, axis=0)
    sum_ref[0, slot] += scale * weighted + rest * plain
    sum_ref[1, slot] += scale * (plain - weighted) + rest * plain
    sum_ref[2, slot] += scale * mixed


def stress_scales(energy_ref, number, total_freq, directions):
    ratio = 0.5 + 0.5 * number.astype(jnp.float32) / (total_freq - 1)
    amplitude = energy_ref[number] / math.sqrt(directions * total_freq)
    return amplitude * ratio, amplitude * (ratio - 0.5)


def inner_kernel(total_freq, axis, list_rows, parts, *refs):
    part_refs = refs[:parts]
    (trig_ref, speed_ref, energy_ref, field_ref) = refs[parts : parts + 4]
    flow_ref, turn_ref, mid_ref, out_ref, sum_ref = refs[parts + 4 : parts + 9]
    grad_ref, keep_ref = refs[parts + 9 :]
    freqs, tiles, directions, wave_rows, _ = field_ref.shape
    groups = directions // 8
    index = lax.axis_index(axis)
    for comp in range(2):
        if parts == 1:
            for tile in range(tiles):
                flow_ref[comp, tile] = part_refs[0][tile, comp]
        else:
            tile = index - lax.rem(index, 2)
            other = tiles // 2 - tile
            own, theirs = part_refs
            flow_ref[comp, tile] = own[0, comp]
            flow_ref[comp, tile + 1] = own[1, comp] + theirs[2, comp]
            flow_ref[comp, other] = theirs[0, comp]
            flow_ref[comp, other + 1] = theirs[1, comp] + own[2, comp]
    inner = list_rows - 2
    east, north = flow_ref[0, :, 1 : 1 + inner], flow_ref[1, :, 1 : 1 + inner]
    east_y = (flow_ref[0, :, 2 : 2 + inner] - flow_ref[0, :, 0:inner]) * 0.5
    north_y = (flow_ref[1, :, 2 : 2 + inner] - flow_ref[1, :, 0:inner]) * 0.5
    east_x = (roll_lanes(east, -1) - roll_lanes(east, 1)) * 0.5
    north_x = (roll_lanes(north, -1) - roll_lanes(north, 1)) * 0.5
    grad_ref[0, :, :inner] = refract_factor * (east_x - north_y)
    grad_ref[1, :, :inner] = refract_factor * east_y
    grad_ref[2, :, :inner] = refract_factor * north_x
    for comp in range(2):
        flow_ref[comp, :, :list_rows] = drift_factor * flow_ref[comp, :, :list_rows]
    cross, sin2, cos2 = (
        jnp.broadcast_to(trig_ref[k][:, None], (groups, tiles, 8, LANES)) for k in (2, 3, 4)
    )
    for row in range(inner):
        first, second, third = (spread_row(grad_ref, (k,), row, groups) for k in range(3))
        turn = cross * first + sin2 * second - cos2 * third
        turn_ref[0, row] = jnp.maximum(turn, 0.0)
        turn_ref[1, row] = jnp.minimum(turn, 0.0)
    sum_ref[...] = jnp.zeros_like(sum_ref)
    start = index * freqs

    def one_frequency(freq, carry):
        speeds = Speeds(speed_ref[start + freq], trig_ref, flow_ref, keep_ref)
        source = row_view(field_ref, freq)

        def keep(row, value):
            mid_ref[freq, row - 1] = value

        sweep(lambda row: load_row(source, groups, tiles, row), speeds, turn_ref, 1, wave_rows - 1, keep)
        scale, rest = stress_scales(energy_ref, start + freq, total_freq, directions)

        def finish(row, value):
            out_ref[freq, row - 2] = value
            add_stress(value, trig_ref, scale, rest, sum_ref, row - 2)

        sweep(lambda row: mid_ref[freq, row - 1], speeds, turn_ref, 2, wave_rows - 2, finish)
        return carry

    lax.fori_loop(0, freqs, one_frequency, 0)


def outer_kernel(
    total_freq, axis, trig_ref, speed_ref, energy_ref, field_ref, low_ref, high_ref, flow_ref, turn_ref,
    mid_ref, inner_ref, out_ref, stress_ref, rim_ref, sum_ref, keep_ref,
):
    freqs, tiles, directions, wave_rows, _ = field_ref.shape
    groups = directions // 8
    start = lax.axis_index(axis) * freqs
    sum_ref[...] = jnp.zeros_like(sum_ref)
    rim = {-1: 0, 0: 1, wave_rows - 1: 2, wave_rows: 3}
    last = {0: 0, 1: 1, wave_rows - 2: 2, wave_rows - 1: 3}

    def one_frequency(freq, carry):
        speeds = Speeds(speed_ref[start + freq], trig_ref, flow_ref, keep_ref)
        source = row_view(field_ref, freq)

        def cells(row):
            if 0 <= row < wave_rows:
                return load_row(source, groups, tiles, row)
            at = pl.ds((freq * 2 + row % 2) * groups, groups)
            return low_ref[at] if row < 0 else high_ref[at]

        def keep(row, value):
            rim_ref[rim[row]] = value

        def middle(row):
            return rim_ref[rim[row]] if row in rim else mid_ref[freq, row - 1]

        scale, rest = stress_scales(energy_ref, start + freq, total_freq, directions)

        def finish(row, value):
            out_ref[freq, last[row]] = value
            add_stress(value, trig_ref, scale, rest, sum_ref, last[row])

        sweep(cells, speeds, turn_ref, -1, 1, keep)
        sweep(cells, speeds, turn_ref, wave_rows - 1, wave_rows + 1, keep)
        sweep(middle, speeds, turn_ref, 0, 2, finish)
        sweep(middle, speeds, turn_ref, wave_rows - 2, wave_rows, finish)
        return carry

    lax.fori_loop(0, freqs, one_frequency, 0)
    for kind in range(3):
        for row in range(wave_rows):
            part = sum_ref[kind, last[row]] if row in last else inner_ref[kind, row - 2]
            line = jnp.sum(part, axis=1, keepdims=True)
            for tile in range(tiles):
                stress_ref[kind, tile, row : row + 1] = line[tile]


def edge_tile(after, before):
    lane = lax.broadcasted_iota(jnp.int32, after.shape, after.ndim - 1)
    return jnp.where(lane < LANES // 2, after, before)


def pair_kernel(axis, own_ref, x_ref, z_ref, xz_ref, keep_ref, send_ref):
    kinds, tiles, wave_rows, _ = own_ref.shape
    half = wave_rows // 2
    index = lax.axis_index(axis)
    for target, out_ref in ((index, keep_ref), (index ^ 2, send_ref)):
        after = lax.rem(target + 1, tiles)
        before = lax.rem(target + tiles - 1, tiles)
        for kind in range(kinds):

            def own(tile):
                return own_ref[kind, tile] + x_ref[kind, tile]

            def prev(tile):
                return z_ref[kind, tile] + xz_ref[kind, tile]

            out_ref[0, kind, 0 : half + 2] = prev(target)[wave_rows - half - 2 :]
            out_ref[0, kind, half + 2 : wave_rows + 3] = own(target)[: half + 1]
            out_ref[1, kind, 0 : half + 2] = edge_tile(prev(after), prev(before))[wave_rows - half - 2 :]
            out_ref[1, kind, half + 2 : wave_rows + 3] = edge_tile(own(after), own(before))[: half + 1]


def settle_kernel(
    axis, aligned, tail_rows, inner_ref, outer_ref, tail_ref, table_ref, out_hbm, coupling_ref, field_ref, sems
):
    freqs, tiles, _, wave_rows, _ = field_ref.shape
    moves = list(tile_copies(field_ref, out_hbm, sems, True))
    for freq in range(freqs):
        sink = row_view(field_ref, freq)
        for row in range(wave_rows):
            if 2 <= row < wave_rows - 2:
                value = inner_ref[freq, row - 2]
            else:
                value = outer_ref[freq, row if row < 2 else row - wave_rows + 4]
            store_row(sink, row, value)
        for other, copy in moves:
            if other == freq:
                copy.start()
    count = wave_rows + 1
    for which, tile in enumerate(chosen_tiles(axis, aligned, tiles)):
        for place in range(9):
            for row in range(tail_rows):
                vreg, line = tail_slot(which, place * tail_rows + row)
                coupling_ref[which, place, row : row + 1, :] = tail_ref[vreg, line : line + 1, :]
            coupling_ref[which, place, tail_rows:count] = table_ref[place, tile, 0 : count - tail_rows]
    for _, copy in moves:
        copy.wait()


def push_tile(stress_ref, coupling_ref, here, edge, push_ref, count):
    lane = lax.broadcasted_iota(jnp.int32, (count, LANES), 1)

    def middle(part, kind):
        return stress_ref[part, kind, 1 : 1 + count]

    def along_y(part, kind):
        return (stress_ref[part, kind, 2 : 2 + count] - stress_ref[part, kind, 0:count]) * 0.5

    def along_x(part, kind):
        tile, rim = middle(0, kind), middle(1, kind)
        after = jnp.where(lane == LANES - 1, pltpu.roll(rim, LANES - 1, 1), pltpu.roll(tile, LANES - 1, 1))
        if part == 0:
            before = jnp.where(lane == 0, pltpu.roll(rim, 1, 1), pltpu.roll(tile, 1, 1))
            return (after - before) * 0.5
        return (pltpu.roll(tile, LANES - 1, 1) - pltpu.roll(rim, 1, 1)) * 0.5

    def forces(part):
        return (
            -(along_x(part, 0) + along_y(part, 2)),
            -(along_x(part, 2) + along_y(part, 1)),
        )

    inner, rim = forces(0), forces(1)
    result = []
    for comp in range(2):
        for place in range(9):
            value = coupling_ref[here, place, :count] * inner[comp]
            if place % 3 == 2:
                spill = coupling_ref[edge, place, :count] * rim[comp]
                value = jnp.where(lane == 0, pltpu.roll(spill, 1, 1), pltpu.roll(value, 1, 1))
            push_ref[place, :count] = value
        near = [push_ref[place, 1:count] for place in range(9)]
        far = [push_ref[place, 0 : count - 1] for place in range(9)]
        result.append(
            (
                (near[0] + far[6] + near[2] + far[8], near[1] + far[7]),
                (near[3] + near[5], near[4]),
            )
        )
    return result


def force_kernel(keep_ref, come_ref, coupling_ref, masked_ref, wet_ref, out_ref, stress_ref, push_ref, merge_ref):
    ocean_rows, width = wet_ref.shape
    wave_rows = ocean_rows // 2
    count = wave_rows + 1
    stress_ref[...] = keep_ref[...] + come_ref[...]
    pushed = push_tile(stress_ref, coupling_ref, 0, 1, push_ref, count)
    cells = jnp.concatenate(
        [
            jnp.concatenate([even, odd], axis=1)
            for component in pushed
            for even, odd in component
        ],
        axis=0,
    )
    merged = jnp.dot(
        cells, merge_matrix(width), precision=HIGHEST, preferred_element_type=jnp.float32
    ).reshape(2, 2, wave_rows, width)
    wet = wet_ref[...]
    for comp in range(2):
        for tile in range(width // LANES):
            lanes = slice(tile * LANES, (tile + 1) * LANES)
            for parity in range(2):
                lines = pl.ds(parity, wave_rows, stride=2)
                merge_ref[comp, tile, lines, :] = merged[comp, parity, :, lanes]
            out_ref[comp, :, lanes] = (
                damping * masked_ref[comp, :, lanes] + force_gain * wet[:, lanes] * merge_ref[comp, tile]
            )


def push_all_kernel(own_ref, prev_ref, coupling_ref, out_ref, stress_ref, push_ref):
    kinds, tiles, wave_rows, _ = own_ref.shape
    half = wave_rows // 2
    for tile in range(tiles):
        after, before = (tile + 1) % tiles, (tile - 1) % tiles
        for kind in range(kinds):
            stress_ref[0, kind, 0 : half + 2] = prev_ref[kind, tile][wave_rows - half - 2 :]
            stress_ref[0, kind, half + 2 : wave_rows + 3] = own_ref[kind, tile][: half + 1]
            stress_ref[1, kind, 0 : half + 2] = edge_tile(prev_ref[kind, after], prev_ref[kind, before])[
                wave_rows - half - 2 :
            ]
            stress_ref[1, kind, half + 2 : wave_rows + 3] = edge_tile(own_ref[kind, after], own_ref[kind, before])[
                : half + 1
            ]
        pushed = push_tile(stress_ref, coupling_ref, tile, before, push_ref, wave_rows + 1)
        for comp in range(2):
            for parity in range(2):
                for side in range(2):
                    out_ref[side, comp, parity, tile] = pushed[comp][parity][side]


def call(kernel, outs, ins, out_specs=None, **kw):
    f32 = jnp.float32
    shapes = tuple(jax.ShapeDtypeStruct(shape, f32) for shape in outs)
    if out_specs is None:
        out_specs = (VMEM,) * len(outs)
    return pl.pallas_call(kernel, out_shape=shapes, in_specs=ins, out_specs=out_specs, compiler_params=params(), **kw)


def in_hbm(*arrays):
    return [pltpu.with_memory_space_constraint(x, pltpu.MemorySpace.HBM) for x in arrays]


def window(action, currents, wet, courant, energy, src, weights):
    f32 = jnp.float32
    freqs, directions, wave_rows, columns = action.shape
    groups, tiles = directions // 8, columns // LANES
    list_rows = src.shape[0]
    ocean_rows, width = wet.shape
    spec = lax.axis_size("spec")
    ocean_cols = width * spec
    aligned = width == 2 * LANES and spec == 4
    tail_rows = wave_rows // 2 - 1
    lead = freqs * 2 * groups
    chosen = 2 if aligned else tiles
    padded = -(-list_rows // 8) * 8
    first = wave_rows - 4
    field = jnp.transpose(action.reshape(freqs, directions, wave_rows, tiles, LANES), (0, 1, 3, 2, 4))
    source, weight = jnp.transpose(src, (0, 2, 1)), jnp.transpose(weights, (0, 2, 1))
    cell = (groups, tiles, 8, LANES)
    home = (freqs, tiles, directions, wave_rows, LANES)
    masked, wet_float, tables, tail, held, low, high = call(
        functools.partial(open_kernel, ocean_cols, tail_rows, "spec", aligned),
        (
            currents.shape,
            wet.shape,
            (9, tiles, padded, LANES),
            (chosen * TAIL_VREGS, 8, LANES),
            home,
            (lead, tiles, 8, LANES),
            (lead, tiles, 8, LANES),
        ),
        [HBM] * 5,
        scratch_shapes=[
            pltpu.VMEM(currents.shape, f32),
            pltpu.VMEM(wet.shape, jnp.int32),
            pltpu.VMEM(source.shape, jnp.int32),
            pltpu.VMEM(weight.shape, f32),
            pltpu.SemaphoreType.DMA((4,)),
            pltpu.SemaphoreType.DMA((freqs, tiles)),
        ],
    )(*in_hbm(currents, wet, source, weight, field))
    if aligned:
        xz = from_mesh(masked, 1, 1)
        z = from_mesh(masked, 1, 0)
        x = from_mesh(masked, 0, 1)
    else:
        z = from_offset(masked, "space", 1)
    low = from_offset(low, "space", -1)
    high = from_offset(high, "space", 1)
    tail = from_offset(tail, "space", -1)
    if aligned:
        (part,) = call(
            functools.partial(flow_kernel, "spec", list_rows, first),
            ((3, 2, padded, LANES),),
            [VMEM] * 5,
            scratch_shapes=[pltpu.VMEM((2, 2, 2, 2 * ocean_rows, LANES), f32)],
        )(masked, x, z, xz, tables)
        parts = [part, from_mesh(part, 0, 2)]
    else:
        both = lax.all_gather(jnp.concatenate([masked, z], axis=1), "spec", axis=2, tiled=True)
        ocean = both.reshape(2, 2 * ocean_rows, tiles, LANES, 2).transpose(4, 2, 0, 1, 3)
        parts = call(
            functools.partial(flow_all_kernel, list_rows, first), ((tiles, 2, padded, LANES),), [VMEM] * 2
        )(ocean, tables)
    angles = 2.0 * math.pi * (np.arange(directions) + 0.5) / directions
    cosine, sine = np.cos(angles), np.sin(angles)
    trig = np.stack([cosine, sine, sine * cosine, sine * sine, cosine * cosine]).astype(np.float32)
    trig = trig.reshape(5, 8, groups).transpose(0, 2, 1)
    trig = jnp.asarray(np.repeat(trig[:, :, :, None], LANES, axis=3))
    flow, turn, middle, inner, inner_stress = call(
        functools.partial(inner_kernel, freqs * spec, "spec", list_rows, len(parts)),
        (
            (2, tiles, padded, LANES),
            (2, list_rows - 2) + cell,
            (freqs, wave_rows - 2) + cell,
            (freqs, wave_rows - 4) + cell,
            (3, wave_rows - 4, tiles, 8, LANES),
        ),
        [VMEM] * (len(parts) + 1) + [SMEM] * 2 + [VMEM],
        scratch_shapes=[
            pltpu.VMEM((3, tiles, padded, LANES), f32),
            pltpu.VMEM((4, list_rows) + cell, f32),
        ],
    )(*parts, trig, courant, energy, held)
    outer, stress = call(
        functools.partial(outer_kernel, freqs * spec, "spec"),
        ((freqs, 4) + cell, (3, tiles, wave_rows, LANES)),
        [VMEM] + [SMEM] * 2 + [VMEM] * 7,
        scratch_shapes=[
            pltpu.VMEM((4,) + cell, f32),
            pltpu.VMEM((3, 4, tiles, 8, LANES), f32),
            pltpu.VMEM((4, list_rows) + cell, f32),
        ],
    )(trig, courant, energy, held, low, high, flow, turn, middle, inner_stress)
    if aligned:
        xz = from_mesh(stress, -1, 1)
        z = from_mesh(stress, -1, 0)
        x = from_mesh(stress, 0, 1)
    out_field, coupling = call(
        functools.partial(settle_kernel, "spec", aligned, tail_rows),
        (field.shape, (chosen, 9, 2 * wave_rows, LANES)),
        [VMEM] * 4,
        out_specs=(HBM, VMEM),
        scratch_shapes=[pltpu.VMEM(home, f32), pltpu.SemaphoreType.DMA((freqs, tiles))],
    )(inner, outer, tail, tables)
    new_action = jnp.transpose(out_field, (0, 1, 3, 2, 4)).reshape(action.shape)
    column = (2, 3, 2 * wave_rows, LANES)
    scratch = [pltpu.VMEM(column, f32), pltpu.VMEM((9, 2 * wave_rows, LANES), f32)]
    if aligned:
        keep, send = call(functools.partial(pair_kernel, "spec"), (column, column), [VMEM] * 4)(stress, x, z, xz)
        come = from_mesh(send, 0, 2)
        (updated,) = call(
            force_kernel,
            (currents.shape,),
            [VMEM] * 5,
            scratch_shapes=scratch + [pltpu.VMEM((2, width // LANES, ocean_rows, LANES), f32)],
        )(keep, come, coupling, masked, wet_float)
    else:
        stress = lax.psum(stress, "spec")
        prev = from_offset(stress, "space", -1)
        (pushed,) = call(
            push_all_kernel, ((2, 2, 2, tiles, wave_rows, LANES),), [VMEM] * 3, scratch_shapes=scratch
        )(stress, prev, coupling)
        grid = jnp.transpose(pushed, (1, 4, 2, 3, 5, 0)).reshape(2, ocean_rows, ocean_cols)
        share = lax.dynamic_slice_in_dim(grid, lax.axis_index("spec") * width, width, 2)
        updated = damping * masked + force_gain * wet_float[None] * share
    return (new_action, updated)


def solution(mesh):
    in_specs = (
        P("spec", None, "space", None),
        P(None, "space", "spec"),
        P("space", "spec"),
        P(),
        P(),
        P("space", None, None),
        P("space", None, None),
    )
    out_specs = (P("spec", None, "space", None), P(None, "space", "spec"))
    return jax.shard_map(window, mesh=mesh, in_specs=in_specs, out_specs=out_specs, check_vma=False)
```

```python
import functools
import math

import jax
import jax.numpy as jnp
import numpy as np
from jax import lax
from jax.experimental import pallas as pl
from jax.experimental.pallas import tpu as pltpu
from jax.sharding import PartitionSpec as P


drift_factor = 0.2
refract_factor = 1.5
damping = 0.95
force_gain = 0.5

LANES = 128
HIGHEST = lax.Precision.HIGHEST
VMEM = pl.BlockSpec(memory_space=pltpu.VMEM)
SMEM = pl.BlockSpec(memory_space=pltpu.SMEM)
HBM = pl.BlockSpec(memory_space=pltpu.MemorySpace.HBM)
TAIL_VREGS = 4


def from_offset(block, axis, offset):
    count = lax.axis_size(axis)
    return lax.ppermute(block, axis, [((i + offset) % count, i) for i in range(count)])


def from_mesh(block, offset, bits):
    space, spec = lax.axis_size("space"), lax.axis_size("spec")
    route = [
        (((i + offset) % space) * spec + (j ^ bits), i * spec + j) for i in range(space) for j in range(spec)
    ]
    return lax.ppermute(block, ("space", "spec"), route)


def params(**kw):
    return pltpu.CompilerParams(vmem_limit_bytes=48 * 1024 * 1024, **kw)


def split_matrix(width):
    row = lax.broadcasted_iota(jnp.int32, (width, width), 0)
    col = lax.broadcasted_iota(jnp.int32, (width, width), 1)
    half = width // 2
    source = jnp.where(col < half, 2 * col, 2 * (col - half) + 1)
    return (row == source).astype(jnp.float32)


def merge_matrix(width):
    row = lax.broadcasted_iota(jnp.int32, (width, width), 0)
    col = lax.broadcasted_iota(jnp.int32, (width, width), 1)
    half = width // 2
    target = jnp.where(row < half, 2 * row, 2 * (row - half) + 1)
    return (col == target).astype(jnp.float32)


def roll_lanes(x, shift):
    lane = lax.broadcasted_iota(jnp.int32, x.shape, x.ndim - 1)
    turned = pltpu.roll(x, shift % LANES, x.ndim - 1)
    if shift == 1:
        return jnp.where(lane == 0, roll_lead(turned, 1, x.ndim - 3), turned)
    return jnp.where(lane == LANES - 1, roll_lead(turned, -1, x.ndim - 3), turned)


def roll_lead(x, shift, axis):
    count = x.shape[axis]
    cut = (-shift) % count
    if cut == 0:
        return x
    return jnp.concatenate(
        [lax.slice_in_dim(x, cut, count, axis=axis), lax.slice_in_dim(x, 0, cut, axis=axis)], axis=axis
    )


def roll_directions(x, shift):
    groups = x.shape[0]
    if shift == 1:
        edge = pltpu.roll(x[groups - 1 :], 1, 2)
        return jnp.concatenate([edge, x[: groups - 1]], axis=0)
    edge = pltpu.roll(x[:1], 7, 2)
    return jnp.concatenate([x[1:], edge], axis=0)


def row_view(ref, freq):
    return ref.at[freq].reshape(ref.shape[1] * ref.shape[2] * 8, LANES)


def row_slots(groups, tiles, row):
    return [
        [pl.ds((tile * 8 * groups + group) * 8 + row, 8, stride=groups * 8) for tile in range(tiles)]
        for group in range(groups)
    ]


def load_row(view, groups, tiles, row):
    slots = row_slots(groups, tiles, row)
    return jnp.stack([jnp.stack([view[slot, :] for slot in line]) for line in slots])


def store_row(view, row, value):
    groups, tiles = value.shape[:2]
    for group, line in enumerate(row_slots(groups, tiles, row)):
        for tile, slot in enumerate(line):
            view[slot, :] = value[group, tile]


def tail_slot(which, slot):
    return which * TAIL_VREGS + slot // 8, slot % 8


def chosen_tiles(axis, aligned, tiles):
    if not aligned:
        return list(range(tiles))
    index = lax.axis_index(axis)
    return [index, lax.rem(index + tiles - 1, tiles)]


def tile_copies(tiled, whole, sems):
    freqs, tiles = tiled.shape[:2]
    for freq in range(freqs):
        for tile in range(tiles):
            yield freq, pltpu.make_async_copy(tiled.at[freq, tile], whole.at[freq, :, tile], sems.at[freq, tile])


def open_kernel(
    ocean_cols, tail_rows, axis, aligned, current_hbm, wet_hbm, src_hbm, weight_hbm, field_hbm,
    masked_ref, wet_out, table_ref, tail_ref, field_ref, low_ref, high_ref,
    current_ref, wet_ref, src_ref, weight_ref, raw_ref, sems, field_sems,
):
    copies = [
        pltpu.make_async_copy(source, target, sems.at[k])
        for k, (source, target) in enumerate(
            ((current_hbm, current_ref), (wet_hbm, wet_ref), (src_hbm, src_ref), (weight_hbm, weight_ref))
        )
    ]
    list_rows, corners, columns = src_ref.shape
    freqs, tiles, directions, wave_rows, _ = field_ref.shape
    moves = [
        pltpu.make_async_copy(field_hbm.at[freq], raw_ref.at[freq], field_sems.at[freq]) for freq in range(freqs)
    ]
    for copy in copies:
        copy.start()
    for copy in moves:
        copy.start()
    groups = directions // 8
    shape = (list_rows, columns)
    entry_row = lax.broadcasted_iota(jnp.int32, shape, 0)
    column = lax.broadcasted_iota(jnp.int32, shape, 1)
    base = (2 * (entry_row - 2) + wave_rows) * ocean_cols
    cell = [
        base + jnp.where(2 * column + step >= ocean_cols, 2 * column + step - ocean_cols, 2 * column + step)
        for step in range(3)
    ]
    for copy in copies:
        copy.wait()
    wet = wet_ref[...].astype(jnp.float32)
    wet_out[...] = wet
    masked_ref[...] = current_ref[...] * wet[None]
    sums = [jnp.zeros(shape, jnp.float32) for _ in range(9)]
    for corner in range(corners):
        source = src_ref[:, corner, :]
        weight = weight_ref[:, corner, :]
        for step_row in range(3):
            for step_col in range(3):
                hit = source == cell[step_col] + step_row * ocean_cols
                place = 3 * step_row + step_col
                sums[place] = sums[place] + jnp.where(hit, weight, 0.0)
    for place in range(9):
        for tile in range(tiles):
            table_ref[place, tile, :list_rows] = sums[place][:, tile * LANES : (tile + 1) * LANES]
    first = 2 + wave_rows // 2 - 1
    for which, tile in enumerate(chosen_tiles(axis, aligned, tiles)):
        for place in range(9):
            for row in range(tail_rows):
                vreg, line = tail_slot(which, place * tail_rows + row)
                tail_ref[vreg, line : line + 1, :] = table_ref[place, tile, first + row : first + row + 1, :]
    for freq in range(freqs):
        moves[freq].wait()
        for tile in range(tiles):
            field_ref[freq, tile] = raw_ref[freq, :, tile]
        view = row_view(field_ref, freq)
        for row in range(2):
            at = (freq * 2 + row) * groups
            low_ref[at : at + groups] = load_row(view, groups, tiles, wave_rows - 2 + row)
            high_ref[at : at + groups] = load_row(view, groups, tiles, row)


def flow_tile(table_ref, tile, evens, odds, nexts):
    total = None
    for step_row in range(3):
        even = evens[step_row]
        list_rows = even.shape[0]
        lane = lax.broadcasted_iota(jnp.int32, even.shape, 1)
        edge = 0.0 if nexts is None else pltpu.roll(nexts[step_row], LANES - 1, 1)
        shifted = jnp.where(lane == LANES - 1, edge, pltpu.roll(even, LANES - 1, 1))
        for step_col, lifted in enumerate((even, odds[step_row], shifted)):
            term = table_ref[3 * step_row + step_col, tile, :list_rows] * lifted
            total = term if total is None else total + term
    return total


def row_steps(ref, parity, tile, comp, first, list_rows):
    return [ref[parity, tile, comp, pl.ds(first + step, list_rows, stride=2), :] for step in range(3)]


def flow_kernel(axis, list_rows, first, own_ref, current_ref, wet_ref, table_ref, part_ref, ocean_ref):
    comps, rows, width = own_ref.shape
    tiles = table_ref.shape[1]
    half = width // 2
    tile = lax.axis_index(axis)
    after = current_ref[...] * wet_ref[...].astype(jnp.float32)[None]
    cells = jnp.concatenate([x.reshape(comps * rows, width) for x in (own_ref[...], after)], axis=0)
    split = jnp.dot(cells, split_matrix(width), precision=HIGHEST, preferred_element_type=jnp.float32)
    split = split.reshape(2, comps, rows, width)
    for parity in range(2):
        for block in range(2):
            ocean_ref[parity, 0, :, block * rows : (block + 1) * rows] = split[
                block, :, :, parity * half : (parity + 1) * half
            ]
    before = lax.rem(tile + tiles - 1, tiles)
    lane = lax.broadcasted_iota(jnp.int32, (list_rows, LANES), 1)
    for comp in range(comps):
        even = row_steps(ocean_ref, 0, 0, comp, first, list_rows)
        odd = row_steps(ocean_ref, 1, 0, comp, first, list_rows)
        part_ref[0, comp, :list_rows] = flow_tile(table_ref, tile, even, odd, None)
        spill = None
        for step in range(3):
            edge = jnp.where(lane == LANES - 1, pltpu.roll(even[step], LANES - 1, 1), 0.0)
            term = table_ref[3 * step + 2, before, :list_rows] * edge
            spill = term if spill is None else spill + term
        part_ref[1, comp, :list_rows] = spill


def flow_all_kernel(list_rows, first, ocean_ref, table_ref, flow_ref):
    tiles = table_ref.shape[1]
    for comp in range(2):
        evens = [row_steps(ocean_ref, 0, k, comp, first, list_rows) for k in range(tiles)]
        odds = [row_steps(ocean_ref, 1, k, comp, first, list_rows) for k in range(tiles)]
        for tile in range(tiles):
            flow_ref[tile, comp, :list_rows] = flow_tile(
                table_ref, tile, evens[tile], odds[tile], evens[(tile + 1) % tiles]
            )


def spread_row(ref, lead, row, groups):
    tiles = ref.shape[-3]
    lines = [ref[(*lead, tile, pl.ds(row, 8, stride=0), slice(None))] for tile in range(tiles)]
    return jnp.broadcast_to(jnp.stack(lines)[None], (groups, tiles, 8, LANES))


class Speeds:
    def __init__(self, speed, trig_ref, flow_ref, keep_ref):
        groups, tiles = trig_ref.shape[1], flow_ref.shape[1]
        shape = (groups, tiles, 8, LANES)
        self.groups, self.flow_ref, self.keep_ref = groups, flow_ref, keep_ref
        self.base = [jnp.broadcast_to((speed * trig_ref[k])[:, None], shape) for k in range(2)]
        self.seen = set()

    def parts(self, comp, row):
        slot = row + 2
        if (comp, row) in self.seen:
            return self.keep_ref[2 * comp, slot], self.keep_ref[2 * comp + 1, slot]
        value = self.base[comp] + spread_row(self.flow_ref, (comp,), slot, self.groups)
        up, down = jnp.maximum(value, 0.0), jnp.minimum(value, 0.0)
        self.keep_ref[2 * comp, slot], self.keep_ref[2 * comp + 1, slot] = up, down
        self.seen.add((comp, row))
        return up, down


def sweep(read, speeds, turn_ref, low, high, write):
    here = read(low)
    up, down = speeds.parts(1, low)
    face_before = speeds.parts(1, low - 1)[0] * read(low - 1) + down * here
    for row in range(low, high):
        after = read(row + 1)
        up_after, down_after = speeds.parts(1, row + 1)
        face_here = up * here + down_after * after
        right, left = speeds.parts(0, row)
        face_x = right * here + roll_lanes(left * here, -1)
        face_turn = turn_ref[0, row + 1] * here + roll_directions(turn_ref[1, row + 1] * here, -1)
        write(
            row,
            here
            - (face_x - roll_lanes(face_x, 1))
            - (face_here - face_before)
            - (face_turn - roll_directions(face_turn, 1)),
        )
        face_before, here, up = face_here, after, up_after


def add_stress(value, trig_ref, scale, rest, sum_ref, slot):
    shape = value.shape
    cross = jnp.broadcast_to(trig_ref[2][:, None], shape)
    cos2 = jnp.broadcast_to(trig_ref[4][:, None], shape)
    plain = jnp.sum(value, axis=0)
    weighted = jnp.sum(cos2 * value, axis=0)
    mixed = jnp.sum(cross * value, axis=0)
    sum_ref[0, slot] += scale * weighted + rest * plain
    sum_ref[1, slot] += scale * (plain - weighted) + rest * plain
    sum_ref[2, slot] += scale * mixed


def stress_scales(energy_ref, number, total_freq, directions):
    ratio = 0.5 + 0.5 * number.astype(jnp.float32) / (total_freq - 1)
    amplitude = energy_ref[number] / math.sqrt(directions * total_freq)
    return amplitude * ratio, amplitude * (ratio - 0.5)


def inner_kernel(total_freq, axis, list_rows, parts, *refs):
    part_refs = refs[:parts]
    (trig_ref, speed_ref, energy_ref, field_ref) = refs[parts : parts + 4]
    flow_ref, turn_ref, mid_ref, out_ref, sum_ref = refs[parts + 4 : parts + 9]
    grad_ref, keep_ref = refs[parts + 9 :]
    freqs, tiles, directions, wave_rows, _ = field_ref.shape
    groups = directions // 8
    index = lax.axis_index(axis)
    for comp in range(2):
        if parts == 1:
            for tile in range(tiles):
                flow_ref[comp, tile] = part_refs[0][tile, comp]
        else:
            for bits in range(parts):
                flow_ref[comp, index ^ bits] = part_refs[bits][0, comp]
            for bits in range(parts):
                flow_ref[comp, lax.rem((index ^ bits) + tiles - 1, tiles)] += part_refs[bits][1, comp]
    inner = list_rows - 2
    east, north = flow_ref[0, :, 1 : 1 + inner], flow_ref[1, :, 1 : 1 + inner]
    east_y = (flow_ref[0, :, 2 : 2 + inner] - flow_ref[0, :, 0:inner]) * 0.5
    north_y = (flow_ref[1, :, 2 : 2 + inner] - flow_ref[1, :, 0:inner]) * 0.5
    east_x = (roll_lanes(east, -1) - roll_lanes(east, 1)) * 0.5
    north_x = (roll_lanes(north, -1) - roll_lanes(north, 1)) * 0.5
    grad_ref[0, :, :inner] = refract_factor * (east_x - north_y)
    grad_ref[1, :, :inner] = refract_factor * east_y
    grad_ref[2, :, :inner] = refract_factor * north_x
    for comp in range(2):
        flow_ref[comp, :, :list_rows] = drift_factor * flow_ref[comp, :, :list_rows]
    cross, sin2, cos2 = (
        jnp.broadcast_to(trig_ref[k][:, None], (groups, tiles, 8, LANES)) for k in (2, 3, 4)
    )
    for row in range(inner):
        first, second, third = (spread_row(grad_ref, (k,), row, groups) for k in range(3))
        turn = cross * first + sin2 * second - cos2 * third
        turn_ref[0, row] = jnp.maximum(turn, 0.0)
        turn_ref[1, row] = jnp.minimum(turn, 0.0)
    sum_ref[...] = jnp.zeros_like(sum_ref)
    start = index * freqs

    def one_frequency(freq, carry):
        speeds = Speeds(speed_ref[start + freq], trig_ref, flow_ref, keep_ref)
        source = row_view(field_ref, freq)

        def keep(row, value):
            mid_ref[freq, row - 1] = value

        sweep(lambda row: load_row(source, groups, tiles, row), speeds, turn_ref, 1, wave_rows - 1, keep)
        scale, rest = stress_scales(energy_ref, start + freq, total_freq, directions)

        def finish(row, value):
            out_ref[freq, row - 2] = value
            add_stress(value, trig_ref, scale, rest, sum_ref, row - 2)

        sweep(lambda row: mid_ref[freq, row - 1], speeds, turn_ref, 2, wave_rows - 2, finish)
        return carry

    lax.fori_loop(0, freqs, one_frequency, 0)


def outer_kernel(
    total_freq, axis, trig_ref, speed_ref, energy_ref, field_ref, low_ref, high_ref, flow_ref, turn_ref,
    mid_ref, inner_ref, out_ref, stress_ref, rim_ref, sum_ref, keep_ref,
):
    freqs, tiles, directions, wave_rows, _ = field_ref.shape
    groups = directions // 8
    start = lax.axis_index(axis) * freqs
    sum_ref[...] = jnp.zeros_like(sum_ref)
    rim = {-1: 0, 0: 1, wave_rows - 1: 2, wave_rows: 3}
    last = {0: 0, 1: 1, wave_rows - 2: 2, wave_rows - 1: 3}

    def one_frequency(freq, carry):
        speeds = Speeds(speed_ref[start + freq], trig_ref, flow_ref, keep_ref)
        source = row_view(field_ref, freq)

        def cells(row):
            if 0 <= row < wave_rows:
                return load_row(source, groups, tiles, row)
            at = pl.ds((freq * 2 + row % 2) * groups, groups)
            return low_ref[at] if row < 0 else high_ref[at]

        def keep(row, value):
            rim_ref[rim[row]] = value

        def middle(row):
            return rim_ref[rim[row]] if row in rim else mid_ref[freq, row - 1]

        scale, rest = stress_scales(energy_ref, start + freq, total_freq, directions)

        def finish(row, value):
            out_ref[freq, last[row]] = value
            add_stress(value, trig_ref, scale, rest, sum_ref, last[row])

        sweep(cells, speeds, turn_ref, -1, 1, keep)
        sweep(cells, speeds, turn_ref, wave_rows - 1, wave_rows + 1, keep)
        sweep(middle, speeds, turn_ref, 0, 2, finish)
        sweep(middle, speeds, turn_ref, wave_rows - 2, wave_rows, finish)
        return carry

    lax.fori_loop(0, freqs, one_frequency, 0)
    for kind in range(3):
        for row in range(wave_rows):
            part = sum_ref[kind, last[row]] if row in last else inner_ref[kind, row - 2]
            line = jnp.sum(part, axis=1, keepdims=True)
            for tile in range(tiles):
                stress_ref[kind, tile, row : row + 1] = line[tile]


def edge_tile(after, before):
    lane = lax.broadcasted_iota(jnp.int32, after.shape, after.ndim - 1)
    return jnp.where(lane < LANES // 2, after, before)


def pair_kernel(axis, own_ref, x_ref, z_ref, xz_ref, keep_ref, send_ref):
    kinds, tiles, wave_rows, _ = own_ref.shape
    half = wave_rows // 2
    index = lax.axis_index(axis)
    for target, out_ref in ((index, keep_ref), (index ^ 2, send_ref)):
        after = lax.rem(target + 1, tiles)
        before = lax.rem(target + tiles - 1, tiles)
        for kind in range(kinds):

            def own(tile):
                return own_ref[kind, tile] + x_ref[kind, tile]

            def prev(tile):
                return z_ref[kind, tile] + xz_ref[kind, tile]

            out_ref[0, kind, 0 : half + 2] = prev(target)[wave_rows - half - 2 :]
            out_ref[0, kind, half + 2 : wave_rows + 3] = own(target)[: half + 1]
            out_ref[1, kind, 0 : half + 2] = edge_tile(prev(after), prev(before))[wave_rows - half - 2 :]
            out_ref[1, kind, half + 2 : wave_rows + 3] = edge_tile(own(after), own(before))[: half + 1]


def settle_kernel(
    axis, aligned, tail_rows, inner_ref, outer_ref, tail_ref, table_ref, out_hbm, coupling_ref, field_ref, sems
):
    freqs, tiles, _, wave_rows, _ = field_ref.shape
    moves = list(tile_copies(field_ref, out_hbm, sems))
    for freq in range(freqs):
        sink = row_view(field_ref, freq)
        for row in range(wave_rows):
            if 2 <= row < wave_rows - 2:
                value = inner_ref[freq, row - 2]
            else:
                value = outer_ref[freq, row if row < 2 else row - wave_rows + 4]
            store_row(sink, row, value)
        for other, copy in moves:
            if other == freq:
                copy.start()
    count = wave_rows + 1
    for which, tile in enumerate(chosen_tiles(axis, aligned, tiles)):
        for place in range(9):
            for row in range(tail_rows):
                vreg, line = tail_slot(which, place * tail_rows + row)
                coupling_ref[which, place, row : row + 1, :] = tail_ref[vreg, line : line + 1, :]
            coupling_ref[which, place, tail_rows:count] = table_ref[place, tile, 0 : count - tail_rows]
    for _, copy in moves:
        copy.wait()


def push_tile(stress_ref, coupling_ref, here, edge, push_ref, count):
    lane = lax.broadcasted_iota(jnp.int32, (count, LANES), 1)

    def middle(part, kind):
        return stress_ref[part, kind, 1 : 1 + count]

    def along_y(part, kind):
        return (stress_ref[part, kind, 2 : 2 + count] - stress_ref[part, kind, 0:count]) * 0.5

    def along_x(part, kind):
        tile, rim = middle(0, kind), middle(1, kind)
        after = jnp.where(lane == LANES - 1, pltpu.roll(rim, LANES - 1, 1), pltpu.roll(tile, LANES - 1, 1))
        if part == 0:
            before = jnp.where(lane == 0, pltpu.roll(rim, 1, 1), pltpu.roll(tile, 1, 1))
            return (after - before) * 0.5
        return (pltpu.roll(tile, LANES - 1, 1) - pltpu.roll(rim, 1, 1)) * 0.5

    def forces(part):
        return (
            -(along_x(part, 0) + along_y(part, 2)),
            -(along_x(part, 2) + along_y(part, 1)),
        )

    inner, rim = forces(0), forces(1)
    result = []
    for comp in range(2):
        for place in range(9):
            value = coupling_ref[here, place, :count] * inner[comp]
            if place % 3 == 2:
                spill = coupling_ref[edge, place, :count] * rim[comp]
                value = jnp.where(lane == 0, pltpu.roll(spill, 1, 1), pltpu.roll(value, 1, 1))
            push_ref[place, :count] = value
        near = [push_ref[place, 1:count] for place in range(9)]
        far = [push_ref[place, 0 : count - 1] for place in range(9)]
        result.append(
            (
                (near[0] + far[6] + near[2] + far[8], near[1] + far[7]),
                (near[3] + near[5], near[4]),
            )
        )
    return result


def force_kernel(keep_ref, come_ref, coupling_ref, masked_ref, wet_ref, out_ref, stress_ref, push_ref, merge_ref):
    ocean_rows, width = wet_ref.shape
    wave_rows = ocean_rows // 2
    count = wave_rows + 1
    stress_ref[...] = keep_ref[...] + come_ref[...]
    pushed = push_tile(stress_ref, coupling_ref, 0, 1, push_ref, count)
    cells = jnp.concatenate(
        [
            jnp.concatenate([even, odd], axis=1)
            for component in pushed
            for even, odd in component
        ],
        axis=0,
    )
    merged = jnp.dot(
        cells, merge_matrix(width), precision=HIGHEST, preferred_element_type=jnp.float32
    ).reshape(2, 2, wave_rows, width)
    wet = wet_ref[...]
    for comp in range(2):
        for tile in range(width // LANES):
            lanes = slice(tile * LANES, (tile + 1) * LANES)
            for parity in range(2):
                lines = pl.ds(parity, wave_rows, stride=2)
                merge_ref[comp, tile, lines, :] = merged[comp, parity, :, lanes]
            out_ref[comp, :, lanes] = (
                damping * masked_ref[comp, :, lanes] + force_gain * wet[:, lanes] * merge_ref[comp, tile]
            )


def push_all_kernel(own_ref, prev_ref, coupling_ref, out_ref, stress_ref, push_ref):
    kinds, tiles, wave_rows, _ = own_ref.shape
    half = wave_rows // 2
    for tile in range(tiles):
        after, before = (tile + 1) % tiles, (tile - 1) % tiles
        for kind in range(kinds):
            stress_ref[0, kind, 0 : half + 2] = prev_ref[kind, tile][wave_rows - half - 2 :]
            stress_ref[0, kind, half + 2 : wave_rows + 3] = own_ref[kind, tile][: half + 1]
            stress_ref[1, kind, 0 : half + 2] = edge_tile(prev_ref[kind, after], prev_ref[kind, before])[
                wave_rows - half - 2 :
            ]
            stress_ref[1, kind, half + 2 : wave_rows + 3] = edge_tile(own_ref[kind, after], own_ref[kind, before])[
                : half + 1
            ]
        pushed = push_tile(stress_ref, coupling_ref, tile, before, push_ref, wave_rows + 1)
        for comp in range(2):
            for parity in range(2):
                for side in range(2):
                    out_ref[side, comp, parity, tile] = pushed[comp][parity][side]


def call(kernel, outs, ins, out_specs=None, **kw):
    f32 = jnp.float32
    shapes = tuple(jax.ShapeDtypeStruct(shape, f32) for shape in outs)
    if out_specs is None:
        out_specs = (VMEM,) * len(outs)
    return pl.pallas_call(kernel, out_shape=shapes, in_specs=ins, out_specs=out_specs, compiler_params=params(), **kw)


def in_hbm(*arrays):
    return [pltpu.with_memory_space_constraint(x, pltpu.MemorySpace.HBM) for x in arrays]


def window(action, currents, wet, courant, energy, src, weights):
    f32 = jnp.float32
    freqs, directions, wave_rows, columns = action.shape
    groups, tiles = directions // 8, columns // LANES
    list_rows = src.shape[0]
    ocean_rows, width = wet.shape
    spec = lax.axis_size("spec")
    ocean_cols = width * spec
    aligned = width == 2 * LANES and spec == 4
    tail_rows = wave_rows // 2 - 1
    lead = freqs * 2 * groups
    chosen = 2 if aligned else tiles
    padded = -(-list_rows // 8) * 8
    first = wave_rows - 4
    field = jnp.transpose(action.reshape(freqs, directions, wave_rows, tiles, LANES), (0, 1, 3, 2, 4))
    source, weight = jnp.transpose(src, (0, 2, 1)), jnp.transpose(weights, (0, 2, 1))
    cell = (groups, tiles, 8, LANES)
    home = (freqs, tiles, directions, wave_rows, LANES)
    z_current = from_offset(currents, "space", 1)
    z_wet = from_offset(wet, "space", 1)
    masked, wet_float, tables, tail, held, low, high = call(
        functools.partial(open_kernel, ocean_cols, tail_rows, "spec", aligned),
        (
            currents.shape,
            wet.shape,
            (9, tiles, padded, LANES),
            (chosen * TAIL_VREGS, 8, LANES),
            home,
            (lead, tiles, 8, LANES),
            (lead, tiles, 8, LANES),
        ),
        [HBM] * 5,
        scratch_shapes=[
            pltpu.VMEM(currents.shape, f32),
            pltpu.VMEM(wet.shape, jnp.int32),
            pltpu.VMEM(source.shape, jnp.int32),
            pltpu.VMEM(weight.shape, f32),
            pltpu.VMEM(field.shape, f32),
            pltpu.SemaphoreType.DMA((4,)),
            pltpu.SemaphoreType.DMA((freqs,)),
        ],
    )(*in_hbm(currents, wet, source, weight, field))
    low = from_offset(low, "space", -1)
    high = from_offset(high, "space", 1)
    tail = from_offset(tail, "space", -1)
    if aligned:
        (part,) = call(
            functools.partial(flow_kernel, "spec", list_rows, first),
            ((2, 2, padded, LANES),),
            [VMEM] * 4,
            scratch_shapes=[pltpu.VMEM((2, 1, 2, 2 * ocean_rows, LANES), f32)],
        )(masked, z_current, z_wet, tables)
        parts = [part]
        for bits in range(1, spec):
            parts.append(from_mesh(part, 0, bits))
    else:
        z = z_current * z_wet.astype(f32)[None]
        both = lax.all_gather(jnp.concatenate([masked, z], axis=1), "spec", axis=2, tiled=True)
        ocean = both.reshape(2, 2 * ocean_rows, tiles, LANES, 2).transpose(4, 2, 0, 1, 3)
        parts = call(
            functools.partial(flow_all_kernel, list_rows, first), ((tiles, 2, padded, LANES),), [VMEM] * 2
        )(ocean, tables)
    angles = 2.0 * math.pi * (np.arange(directions) + 0.5) / directions
    cosine, sine = np.cos(angles), np.sin(angles)
    trig = np.stack([cosine, sine, sine * cosine, sine * sine, cosine * cosine]).astype(np.float32)
    trig = trig.reshape(5, 8, groups).transpose(0, 2, 1)
    trig = jnp.asarray(np.repeat(trig[:, :, :, None], LANES, axis=3))
    flow, turn, middle, inner, inner_stress = call(
        functools.partial(inner_kernel, freqs * spec, "spec", list_rows, len(parts)),
        (
            (2, tiles, padded, LANES),
            (2, list_rows - 2) + cell,
            (freqs, wave_rows - 2) + cell,
            (freqs, wave_rows - 4) + cell,
            (3, wave_rows - 4, tiles, 8, LANES),
        ),
        [VMEM] * (len(parts) + 1) + [SMEM] * 2 + [VMEM],
        scratch_shapes=[
            pltpu.VMEM((3, tiles, padded, LANES), f32),
            pltpu.VMEM((4, list_rows) + cell, f32),
        ],
    )(*parts, trig, courant, energy, held)
    outer, stress = call(
        functools.partial(outer_kernel, freqs * spec, "spec"),
        ((freqs, 4) + cell, (3, tiles, wave_rows, LANES)),
        [VMEM] + [SMEM] * 2 + [VMEM] * 7,
        scratch_shapes=[
            pltpu.VMEM((4,) + cell, f32),
            pltpu.VMEM((3, 4, tiles, 8, LANES), f32),
            pltpu.VMEM((4, list_rows) + cell, f32),
        ],
    )(trig, courant, energy, held, low, high, flow, turn, middle, inner_stress)
    if aligned:
        xz = from_mesh(stress, -1, 1)
        z = from_mesh(stress, -1, 0)
        x = from_mesh(stress, 0, 1)
    out_field, coupling = call(
        functools.partial(settle_kernel, "spec", aligned, tail_rows),
        (field.shape, (chosen, 9, 2 * wave_rows, LANES)),
        [VMEM] * 4,
        out_specs=(HBM, VMEM),
        scratch_shapes=[pltpu.VMEM(home, f32), pltpu.SemaphoreType.DMA((freqs, tiles))],
    )(inner, outer, tail, tables)
    new_action = jnp.transpose(out_field, (0, 1, 3, 2, 4)).reshape(action.shape)
    column = (2, 3, 2 * wave_rows, LANES)
    scratch = [pltpu.VMEM(column, f32), pltpu.VMEM((9, 2 * wave_rows, LANES), f32)]
    if aligned:
        keep, send = call(functools.partial(pair_kernel, "spec"), (column, column), [VMEM] * 4)(stress, x, z, xz)
        come = from_mesh(send, 0, 2)
        (updated,) = call(
            force_kernel,
            (currents.shape,),
            [VMEM] * 5,
            scratch_shapes=scratch + [pltpu.VMEM((2, width // LANES, ocean_rows, LANES), f32)],
        )(keep, come, coupling, masked, wet_float)
    else:
        stress = lax.psum(stress, "spec")
        prev = from_offset(stress, "space", -1)
        (pushed,) = call(
            push_all_kernel, ((2, 2, 2, tiles, wave_rows, LANES),), [VMEM] * 3, scratch_shapes=scratch
        )(stress, prev, coupling)
        grid = jnp.transpose(pushed, (1, 4, 2, 3, 5, 0)).reshape(2, ocean_rows, ocean_cols)
        share = lax.dynamic_slice_in_dim(grid, lax.axis_index("spec") * width, width, 2)
        updated = damping * masked + force_gain * wet_float[None] * share
    return (new_action, updated)


def solution(mesh):
    in_specs = (
        P("spec", None, "space", None),
        P(None, "space", "spec"),
        P("space", "spec"),
        P(),
        P(),
        P("space", None, None),
        P("space", None, None),
    )
    out_specs = (P("spec", None, "space", None), P(None, "space", "spec"))
    return jax.shard_map(window, mesh=mesh, in_specs=in_specs, out_specs=out_specs, check_vma=False)
```

```python
import functools
import math

import jax
import jax.numpy as jnp
import numpy as np
from jax import lax
from jax.experimental import pallas as pl
from jax.experimental.pallas import tpu as pltpu
from jax.sharding import PartitionSpec as P


drift_factor = 0.2
refract_factor = 1.5
damping = 0.95
force_gain = 0.5

LANES = 128
HIGHEST = lax.Precision.HIGHEST
VMEM = pl.BlockSpec(memory_space=pltpu.VMEM)
SMEM = pl.BlockSpec(memory_space=pltpu.SMEM)
HBM = pl.BlockSpec(memory_space=pltpu.MemorySpace.HBM)
TAIL_VREGS = 4


def from_offset(block, axis, offset):
    count = lax.axis_size(axis)
    return lax.ppermute(block, axis, [((i + offset) % count, i) for i in range(count)])


def from_mesh(block, offset, bits):
    space, spec = lax.axis_size("space"), lax.axis_size("spec")
    route = [
        (((i + offset) % space) * spec + (j ^ bits), i * spec + j) for i in range(space) for j in range(spec)
    ]
    return lax.ppermute(block, ("space", "spec"), route)


def params(**kw):
    return pltpu.CompilerParams(vmem_limit_bytes=48 * 1024 * 1024, **kw)


def split_matrix(width):
    row = lax.broadcasted_iota(jnp.int32, (width, width), 0)
    col = lax.broadcasted_iota(jnp.int32, (width, width), 1)
    half = width // 2
    source = jnp.where(col < half, 2 * col, 2 * (col - half) + 1)
    return (row == source).astype(jnp.float32)


def merge_matrix(width):
    row = lax.broadcasted_iota(jnp.int32, (width, width), 0)
    col = lax.broadcasted_iota(jnp.int32, (width, width), 1)
    half = width // 2
    target = jnp.where(row < half, 2 * row, 2 * (row - half) + 1)
    return (col == target).astype(jnp.float32)


def roll_lanes(x, shift):
    lane = lax.broadcasted_iota(jnp.int32, x.shape, x.ndim - 1)
    turned = pltpu.roll(x, shift % LANES, x.ndim - 1)
    if shift == 1:
        return jnp.where(lane == 0, roll_lead(turned, 1, x.ndim - 3), turned)
    return jnp.where(lane == LANES - 1, roll_lead(turned, -1, x.ndim - 3), turned)


def roll_lead(x, shift, axis):
    count = x.shape[axis]
    cut = (-shift) % count
    if cut == 0:
        return x
    return jnp.concatenate(
        [lax.slice_in_dim(x, cut, count, axis=axis), lax.slice_in_dim(x, 0, cut, axis=axis)], axis=axis
    )


def roll_directions(x, shift):
    groups = x.shape[0]
    if shift == 1:
        edge = pltpu.roll(x[groups - 1 :], 1, 2)
        return jnp.concatenate([edge, x[: groups - 1]], axis=0)
    edge = pltpu.roll(x[:1], 7, 2)
    return jnp.concatenate([x[1:], edge], axis=0)


def row_view(ref, freq):
    return ref.at[freq].reshape(ref.shape[1] * ref.shape[2] * 8, LANES)


def row_slots(groups, tiles, row):
    return [
        [pl.ds((tile * 8 * groups + group) * 8 + row, 8, stride=groups * 8) for tile in range(tiles)]
        for group in range(groups)
    ]


def load_row(view, groups, tiles, row):
    slots = row_slots(groups, tiles, row)
    return jnp.stack([jnp.stack([view[slot, :] for slot in line]) for line in slots])


def store_row(view, row, value):
    groups, tiles = value.shape[:2]
    for group, line in enumerate(row_slots(groups, tiles, row)):
        for tile, slot in enumerate(line):
            view[slot, :] = value[group, tile]


def tail_slot(which, slot):
    return which * TAIL_VREGS + slot // 8, slot % 8


def chosen_tiles(axis, aligned, tiles):
    if not aligned:
        return list(range(tiles))
    index = lax.axis_index(axis)
    return [index, lax.rem(index + tiles - 1, tiles)]


def tile_copies(tiled, whole, sems):
    freqs, tiles = tiled.shape[:2]
    for freq in range(freqs):
        for tile in range(tiles):
            yield freq, pltpu.make_async_copy(tiled.at[freq, tile], whole.at[freq, :, tile], sems.at[freq, tile])


def open_kernel(
    ocean_cols, tail_rows, axis, aligned, current_hbm, wet_hbm, src_hbm, weight_hbm, field_hbm,
    masked_ref, wet_out, table_ref, tail_ref, field_ref, low_ref, high_ref,
    current_ref, wet_ref, src_ref, weight_ref, raw_ref, sems, field_sems,
):
    copies = [
        pltpu.make_async_copy(source, target, sems.at[k])
        for k, (source, target) in enumerate(
            ((current_hbm, current_ref), (wet_hbm, wet_ref), (src_hbm, src_ref), (weight_hbm, weight_ref))
        )
    ]
    list_rows, corners, columns = src_ref.shape
    freqs, tiles, directions, wave_rows, _ = field_ref.shape
    moves = [
        pltpu.make_async_copy(field_hbm.at[freq], raw_ref.at[freq], field_sems.at[freq]) for freq in range(freqs)
    ]
    for copy in copies:
        copy.start()
    for copy in moves:
        copy.start()
    groups = directions // 8
    shape = (list_rows, columns)
    entry_row = lax.broadcasted_iota(jnp.int32, shape, 0)
    column = lax.broadcasted_iota(jnp.int32, shape, 1)
    base = (2 * (entry_row - 2) + wave_rows) * ocean_cols
    cell = [
        base + jnp.where(2 * column + step >= ocean_cols, 2 * column + step - ocean_cols, 2 * column + step)
        for step in range(3)
    ]
    for copy in copies:
        copy.wait()
    wet = wet_ref[...].astype(jnp.float32)
    wet_out[...] = wet
    masked_ref[...] = current_ref[...] * wet[None]
    sums = [jnp.zeros(shape, jnp.float32) for _ in range(9)]
    for corner in range(corners):
        source = src_ref[:, corner, :]
        weight = weight_ref[:, corner, :]
        for step_row in range(3):
            for step_col in range(3):
                hit = source == cell[step_col] + step_row * ocean_cols
                place = 3 * step_row + step_col
                sums[place] = sums[place] + jnp.where(hit, weight, 0.0)
    for place in range(9):
        for tile in range(tiles):
            table_ref[place, tile, :list_rows] = sums[place][:, tile * LANES : (tile + 1) * LANES]
    first = 2 + wave_rows // 2 - 1
    for which, tile in enumerate(chosen_tiles(axis, aligned, tiles)):
        for place in range(9):
            for row in range(tail_rows):
                vreg, line = tail_slot(which, place * tail_rows + row)
                tail_ref[vreg, line : line + 1, :] = table_ref[place, tile, first + row : first + row + 1, :]
    for freq in range(freqs):
        moves[freq].wait()
        for tile in range(tiles):
            field_ref[freq, tile] = raw_ref[freq, :, tile]
        view = row_view(field_ref, freq)
        for row in range(2):
            at = (freq * 2 + row) * groups
            low_ref[at : at + groups] = load_row(view, groups, tiles, wave_rows - 2 + row)
            high_ref[at : at + groups] = load_row(view, groups, tiles, row)


def flow_tile(table_ref, tile, evens, odds, nexts):
    total = None
    for step_row in range(3):
        even = evens[step_row]
        list_rows = even.shape[0]
        lane = lax.broadcasted_iota(jnp.int32, even.shape, 1)
        edge = 0.0 if nexts is None else pltpu.roll(nexts[step_row], LANES - 1, 1)
        shifted = jnp.where(lane == LANES - 1, edge, pltpu.roll(even, LANES - 1, 1))
        for step_col, lifted in enumerate((even, odds[step_row], shifted)):
            term = table_ref[3 * step_row + step_col, tile, :list_rows] * lifted
            total = term if total is None else total + term
    return total


def row_steps(ref, parity, tile, comp, first, list_rows):
    return [ref[parity, tile, comp, pl.ds(first + step, list_rows, stride=2), :] for step in range(3)]


def flow_kernel(axis, list_rows, first, own_ref, current_ref, wet_ref, table_ref, part_ref, ocean_ref):
    comps, rows, width = own_ref.shape
    tiles = table_ref.shape[1]
    half = width // 2
    tile = lax.axis_index(axis)
    after = current_ref[...] * wet_ref[...].astype(jnp.float32)[None]
    cells = jnp.concatenate([x.reshape(comps * rows, width) for x in (own_ref[...], after)], axis=0)
    split = jnp.dot(cells, split_matrix(width), precision=HIGHEST, preferred_element_type=jnp.float32)
    split = split.reshape(2, comps, rows, width)
    for parity in range(2):
        for block in range(2):
            ocean_ref[parity, 0, :, block * rows : (block + 1) * rows] = split[
                block, :, :, parity * half : (parity + 1) * half
            ]
    before = lax.rem(tile + tiles - 1, tiles)
    lane = lax.broadcasted_iota(jnp.int32, (list_rows, LANES), 1)
    spill = None
    for comp in range(comps):
        even = row_steps(ocean_ref, 0, 0, comp, first, list_rows)
        odd = row_steps(ocean_ref, 1, 0, comp, first, list_rows)
        part_ref[comp * list_rows : (comp + 1) * list_rows] = flow_tile(table_ref, tile, even, odd, None)
        for step in range(3):
            weight = table_ref[3 * step + 2, before, :list_rows]
            weight = weight if comp == 0 else pltpu.roll(weight, LANES - comp, 1)
            edge = jnp.where(lane == LANES - 1 - comp, pltpu.roll(even[step], LANES - 1 - comp, 1), 0.0)
            spill = weight * edge if spill is None else spill + weight * edge
    part_ref[comps * list_rows : (comps + 1) * list_rows] = spill


def flow_all_kernel(list_rows, first, ocean_ref, table_ref, flow_ref):
    tiles = table_ref.shape[1]
    for comp in range(2):
        evens = [row_steps(ocean_ref, 0, k, comp, first, list_rows) for k in range(tiles)]
        odds = [row_steps(ocean_ref, 1, k, comp, first, list_rows) for k in range(tiles)]
        for tile in range(tiles):
            flow_ref[tile, comp, :list_rows] = flow_tile(
                table_ref, tile, evens[tile], odds[tile], evens[(tile + 1) % tiles]
            )


def spread_row(ref, lead, row, groups):
    tiles = ref.shape[-3]
    lines = [ref[(*lead, tile, pl.ds(row, 8, stride=0), slice(None))] for tile in range(tiles)]
    return jnp.broadcast_to(jnp.stack(lines)[None], (groups, tiles, 8, LANES))


class Speeds:
    def __init__(self, speed, trig_ref, flow_ref, keep_ref):
        groups, tiles = trig_ref.shape[1], flow_ref.shape[1]
        shape = (groups, tiles, 8, LANES)
        self.groups, self.flow_ref, self.keep_ref = groups, flow_ref, keep_ref
        self.base = [jnp.broadcast_to((speed * trig_ref[k])[:, None], shape) for k in range(2)]
        self.seen = set()

    def parts(self, comp, row):
        slot = row + 2
        if (comp, row) in self.seen:
            return self.keep_ref[2 * comp, slot], self.keep_ref[2 * comp + 1, slot]
        value = self.base[comp] + spread_row(self.flow_ref, (comp,), slot, self.groups)
        up, down = jnp.maximum(value, 0.0), jnp.minimum(value, 0.0)
        self.keep_ref[2 * comp, slot], self.keep_ref[2 * comp + 1, slot] = up, down
        self.seen.add((comp, row))
        return up, down


def sweep(read, speeds, turn_ref, low, high, write):
    here = read(low)
    up, down = speeds.parts(1, low)
    face_before = speeds.parts(1, low - 1)[0] * read(low - 1) + down * here
    for row in range(low, high):
        after = read(row + 1)
        up_after, down_after = speeds.parts(1, row + 1)
        face_here = up * here + down_after * after
        right, left = speeds.parts(0, row)
        face_x = right * here + roll_lanes(left * here, -1)
        face_turn = turn_ref[0, row + 1] * here + roll_directions(turn_ref[1, row + 1] * here, -1)
        write(
            row,
            here
            - (face_x - roll_lanes(face_x, 1))
            - (face_here - face_before)
            - (face_turn - roll_directions(face_turn, 1)),
        )
        face_before, here, up = face_here, after, up_after


def add_stress(value, tables, sum_ref, slot):
    for kind, table in enumerate(tables):
        sum_ref[kind, slot] += jnp.sum(table * value, axis=0)


def stress_tables(trig_ref, energy_ref, number, total_freq, shape):
    directions = shape[0] * 8
    ratio = 0.5 + 0.5 * number.astype(jnp.float32) / (total_freq - 1)
    amplitude = energy_ref[number] / math.sqrt(directions * total_freq)
    scale, rest = amplitude * ratio, amplitude * (ratio - 0.5)
    tables = (scale * trig_ref[4] + rest, scale * trig_ref[3] + rest, scale * trig_ref[2])
    return [jnp.broadcast_to(table[:, None], shape) for table in tables]


def add_stress_plain(value, trig_ref, scale, rest, sum_ref, slot):
    shape = value.shape
    cross = jnp.broadcast_to(trig_ref[2][:, None], shape)
    cos2 = jnp.broadcast_to(trig_ref[4][:, None], shape)
    plain = jnp.sum(value, axis=0)
    weighted = jnp.sum(cos2 * value, axis=0)
    mixed = jnp.sum(cross * value, axis=0)
    sum_ref[0, slot] += scale * weighted + rest * plain
    sum_ref[1, slot] += scale * (plain - weighted) + rest * plain
    sum_ref[2, slot] += scale * mixed


def stress_scales(energy_ref, number, total_freq, directions):
    ratio = 0.5 + 0.5 * number.astype(jnp.float32) / (total_freq - 1)
    amplitude = energy_ref[number] / math.sqrt(directions * total_freq)
    return amplitude * ratio, amplitude * (ratio - 0.5)


def inner_kernel(total_freq, axis, list_rows, parts, *refs):
    part_refs = refs[:parts]
    (trig_ref, speed_ref, energy_ref, field_ref) = refs[parts : parts + 4]
    flow_ref, turn_ref, mid_ref, out_ref, sum_ref = refs[parts + 4 : parts + 9]
    grad_ref, keep_ref = refs[parts + 9 :]
    freqs, tiles, directions, wave_rows, _ = field_ref.shape
    groups = directions // 8
    index = lax.axis_index(axis)
    for comp in range(2):
        if parts == 1:
            for tile in range(tiles):
                flow_ref[comp, tile] = part_refs[0][tile, comp]
        else:
            for bits in range(parts):
                rows = slice(comp * list_rows, (comp + 1) * list_rows)
                flow_ref[comp, index ^ bits, :list_rows] = part_refs[bits][rows]
            lane = lax.broadcasted_iota(jnp.int32, (list_rows, LANES), 1)
            for bits in range(parts):
                before = lax.rem((index ^ bits) + tiles - 1, tiles)
                spill = part_refs[bits][2 * list_rows : 3 * list_rows]
                spill = spill if comp == 0 else pltpu.roll(spill, comp, 1)
                flow_ref[comp, before, :list_rows] += jnp.where(lane == LANES - 1, spill, 0.0)
    inner = list_rows - 2
    east, north = flow_ref[0, :, 1 : 1 + inner], flow_ref[1, :, 1 : 1 + inner]
    east_y = (flow_ref[0, :, 2 : 2 + inner] - flow_ref[0, :, 0:inner]) * 0.5
    north_y = (flow_ref[1, :, 2 : 2 + inner] - flow_ref[1, :, 0:inner]) * 0.5
    east_x = (roll_lanes(east, -1) - roll_lanes(east, 1)) * 0.5
    north_x = (roll_lanes(north, -1) - roll_lanes(north, 1)) * 0.5
    grad_ref[0, :, :inner] = refract_factor * (east_x - north_y)
    grad_ref[1, :, :inner] = refract_factor * east_y
    grad_ref[2, :, :inner] = refract_factor * north_x
    for comp in range(2):
        flow_ref[comp, :, :list_rows] = drift_factor * flow_ref[comp, :, :list_rows]
    cross, sin2, cos2 = (
        jnp.broadcast_to(trig_ref[k][:, None], (groups, tiles, 8, LANES)) for k in (2, 3, 4)
    )
    for row in range(inner):
        first, second, third = (spread_row(grad_ref, (k,), row, groups) for k in range(3))
        turn = cross * first + sin2 * second - cos2 * third
        turn_ref[0, row] = jnp.maximum(turn, 0.0)
        turn_ref[1, row] = jnp.minimum(turn, 0.0)
    sum_ref[...] = jnp.zeros_like(sum_ref)
    start = index * freqs

    def one_frequency(freq, carry):
        speeds = Speeds(speed_ref[start + freq], trig_ref, flow_ref, keep_ref)
        source = row_view(field_ref, freq)

        def keep(row, value):
            mid_ref[freq, row - 1] = value

        sweep(lambda row: load_row(source, groups, tiles, row), speeds, turn_ref, 1, wave_rows - 1, keep)
        scale, rest = stress_scales(energy_ref, start + freq, total_freq, directions)

        def finish(row, value):
            out_ref[freq, row - 2] = value
            add_stress_plain(value, trig_ref, scale, rest, sum_ref, row - 2)

        sweep(lambda row: mid_ref[freq, row - 1], speeds, turn_ref, 2, wave_rows - 2, finish)
        return carry

    lax.fori_loop(0, freqs, one_frequency, 0)


def outer_kernel(
    total_freq, axis, trig_ref, speed_ref, energy_ref, field_ref, low_ref, high_ref, flow_ref, turn_ref,
    mid_ref, inner_ref, out_ref, stress_ref, rim_ref, sum_ref, keep_ref,
):
    freqs, tiles, directions, wave_rows, _ = field_ref.shape
    groups = directions // 8
    start = lax.axis_index(axis) * freqs
    sum_ref[...] = jnp.zeros_like(sum_ref)
    rim = {-1: 0, 0: 1, wave_rows - 1: 2, wave_rows: 3}
    last = {0: 0, 1: 1, wave_rows - 2: 2, wave_rows - 1: 3}

    def one_frequency(freq, carry):
        speeds = Speeds(speed_ref[start + freq], trig_ref, flow_ref, keep_ref)
        source = row_view(field_ref, freq)

        def cells(row):
            if 0 <= row < wave_rows:
                return load_row(source, groups, tiles, row)
            at = pl.ds((freq * 2 + row % 2) * groups, groups)
            return low_ref[at] if row < 0 else high_ref[at]

        def keep(row, value):
            rim_ref[rim[row]] = value

        def middle(row):
            return rim_ref[rim[row]] if row in rim else mid_ref[freq, row - 1]

        tables = stress_tables(trig_ref, energy_ref, start + freq, total_freq, (groups, tiles, 8, LANES))

        def finish(row, value):
            out_ref[freq, last[row]] = value
            add_stress(value, tables, sum_ref, last[row])

        sweep(cells, speeds, turn_ref, -1, 1, keep)
        sweep(cells, speeds, turn_ref, wave_rows - 1, wave_rows + 1, keep)
        sweep(middle, speeds, turn_ref, 0, 2, finish)
        sweep(middle, speeds, turn_ref, wave_rows - 2, wave_rows, finish)
        return carry

    lax.fori_loop(0, freqs, one_frequency, 0)
    for kind in range(3):
        for row in range(wave_rows):
            part = sum_ref[kind, last[row]] if row in last else inner_ref[kind, row - 2]
            line = jnp.sum(part, axis=1, keepdims=True)
            for tile in range(tiles):
                stress_ref[kind, tile, row : row + 1] = line[tile]


def edge_tile(after, before):
    lane = lax.broadcasted_iota(jnp.int32, after.shape, after.ndim - 1)
    return jnp.where(lane < LANES // 2, after, before)


def pack_stress(out_ref, center, edge, count):
    merged = None
    for kind in range(3):
        upper, lower = center(kind)
        cut = kind * count + upper.shape[0]
        out_ref[kind * count : cut] = upper
        out_ref[cut : (kind + 1) * count] = lower
        parts = edge(kind)
        if kind == 0:
            merged = list(parts)
            continue
        for k, part in enumerate(parts):
            lane = lax.broadcasted_iota(jnp.int32, part.shape, 1) - 4 * kind
            mine = jnp.logical_and(lane >= -2, lane <= 0)
            merged[k] = jnp.where(mine, pltpu.roll(part, 4 * kind, 1), merged[k])
    cut = 3 * count + merged[0].shape[0]
    out_ref[3 * count : cut] = merged[0]
    out_ref[cut : 4 * count] = merged[1]


def packed_rows(count):
    return -(-4 * count // 8) * 8


def pair_kernel(axis, own_ref, x_ref, z_ref, xz_ref, keep_ref, send_ref):
    tiles, wave_rows = own_ref.shape[1:3]
    half = wave_rows // 2
    index = lax.axis_index(axis)

    def own(kind, tile):
        return own_ref[kind, tile] + x_ref[kind, tile]

    def prev(kind, tile):
        return z_ref[kind, tile] + xz_ref[kind, tile]

    for target, out_ref in ((index, keep_ref), (index ^ 2, send_ref)):
        after = lax.rem(target + 1, tiles)
        before = lax.rem(target + tiles - 1, tiles)

        def center(kind):
            return prev(kind, target)[wave_rows - half - 2 :], own(kind, target)[: half + 1]

        def edge(kind):
            return (
                edge_tile(prev(kind, after), prev(kind, before))[wave_rows - half - 2 :],
                edge_tile(own(kind, after), own(kind, before))[: half + 1],
            )

        pack_stress(out_ref, center, edge, wave_rows + 3)


def settle_kernel(
    axis, aligned, tail_rows, inner_ref, outer_ref, tail_ref, table_ref, out_hbm, coupling_ref, field_ref, sems
):
    freqs, tiles, _, wave_rows, _ = field_ref.shape
    moves = list(tile_copies(field_ref, out_hbm, sems))
    for freq in range(freqs):
        sink = row_view(field_ref, freq)
        for row in range(wave_rows):
            if 2 <= row < wave_rows - 2:
                value = inner_ref[freq, row - 2]
            else:
                value = outer_ref[freq, row if row < 2 else row - wave_rows + 4]
            store_row(sink, row, value)
        for other, copy in moves:
            if other == freq:
                copy.start()
    count = wave_rows + 1
    for which, tile in enumerate(chosen_tiles(axis, aligned, tiles)):
        for place in range(9):
            for row in range(tail_rows):
                vreg, line = tail_slot(which, place * tail_rows + row)
                coupling_ref[which, place, row : row + 1, :] = tail_ref[vreg, line : line + 1, :]
            coupling_ref[which, place, tail_rows:count] = table_ref[place, tile, 0 : count - tail_rows]
    for _, copy in moves:
        copy.wait()


def push_tile(stress_ref, coupling_ref, here, edge, push_ref, count):
    lane = lax.broadcasted_iota(jnp.int32, (count, LANES), 1)
    span = count + 2

    def rows(part, kind, low):
        if part == 0:
            return stress_ref[kind * span + low : kind * span + low + count]
        value = stress_ref[3 * span + low : 3 * span + low + count]
        return value if kind == 0 else pltpu.roll(value, LANES - 4 * kind, 1)

    def along_y(part, kind):
        return (rows(part, kind, 2) - rows(part, kind, 0)) * 0.5

    def along_x(part, kind):
        tile, rim = rows(0, kind, 1), rows(1, kind, 1)
        after = jnp.where(lane == LANES - 1, pltpu.roll(rim, LANES - 1, 1), pltpu.roll(tile, LANES - 1, 1))
        if part == 0:
            before = jnp.where(lane == 0, pltpu.roll(rim, 1, 1), pltpu.roll(tile, 1, 1))
            return (after - before) * 0.5
        return (pltpu.roll(tile, LANES - 1, 1) - pltpu.roll(rim, 1, 1)) * 0.5

    def forces(part):
        return (
            -(along_x(part, 0) + along_y(part, 2)),
            -(along_x(part, 2) + along_y(part, 1)),
        )

    inner, rim = forces(0), forces(1)
    result = []
    for comp in range(2):
        for place in range(9):
            value = coupling_ref[here, place, :count] * inner[comp]
            if place % 3 == 2:
                spill = coupling_ref[edge, place, :count] * rim[comp]
                value = jnp.where(lane == 0, pltpu.roll(spill, 1, 1), pltpu.roll(value, 1, 1))
            push_ref[place, :count] = value
        near = [push_ref[place, 1:count] for place in range(9)]
        far = [push_ref[place, 0 : count - 1] for place in range(9)]
        result.append(
            (
                (near[0] + far[6] + near[2] + far[8], near[1] + far[7]),
                (near[3] + near[5], near[4]),
            )
        )
    return result


def force_kernel(keep_ref, come_ref, coupling_ref, masked_ref, wet_ref, out_ref, stress_ref, push_ref, merge_ref):
    ocean_rows, width = wet_ref.shape
    wave_rows = ocean_rows // 2
    count = wave_rows + 1
    stress_ref[...] = keep_ref[...] + come_ref[...]
    pushed = push_tile(stress_ref, coupling_ref, 0, 1, push_ref, count)
    cells = jnp.concatenate(
        [
            jnp.concatenate([even, odd], axis=1)
            for component in pushed
            for even, odd in component
        ],
        axis=0,
    )
    merged = jnp.dot(
        cells, merge_matrix(width), precision=HIGHEST, preferred_element_type=jnp.float32
    ).reshape(2, 2, wave_rows, width)
    wet = wet_ref[...]
    for comp in range(2):
        for tile in range(width // LANES):
            lanes = slice(tile * LANES, (tile + 1) * LANES)
            for parity in range(2):
                lines = pl.ds(parity, wave_rows, stride=2)
                merge_ref[comp, tile, lines, :] = merged[comp, parity, :, lanes]
            out_ref[comp, :, lanes] = (
                damping * masked_ref[comp, :, lanes] + force_gain * wet[:, lanes] * merge_ref[comp, tile]
            )


def push_all_kernel(own_ref, prev_ref, coupling_ref, out_ref, stress_ref, push_ref):
    tiles, wave_rows = own_ref.shape[1:3]
    half = wave_rows // 2
    for tile in range(tiles):
        after, before = (tile + 1) % tiles, (tile - 1) % tiles

        def center(kind):
            return prev_ref[kind, tile][wave_rows - half - 2 :], own_ref[kind, tile][: half + 1]

        def edge(kind):
            return (
                edge_tile(prev_ref[kind, after], prev_ref[kind, before])[wave_rows - half - 2 :],
                edge_tile(own_ref[kind, after], own_ref[kind, before])[: half + 1],
            )

        pack_stress(stress_ref, center, edge, wave_rows + 3)
        pushed = push_tile(stress_ref, coupling_ref, tile, before, push_ref, wave_rows + 1)
        for comp in range(2):
            for parity in range(2):
                for side in range(2):
                    out_ref[side, comp, parity, tile] = pushed[comp][parity][side]


def call(kernel, outs, ins, out_specs=None, **kw):
    f32 = jnp.float32
    shapes = tuple(jax.ShapeDtypeStruct(shape, f32) for shape in outs)
    if out_specs is None:
        out_specs = (VMEM,) * len(outs)
    return pl.pallas_call(kernel, out_shape=shapes, in_specs=ins, out_specs=out_specs, compiler_params=params(), **kw)


def in_hbm(*arrays):
    return [pltpu.with_memory_space_constraint(x, pltpu.MemorySpace.HBM) for x in arrays]


def window(action, currents, wet, courant, energy, src, weights):
    f32 = jnp.float32
    freqs, directions, wave_rows, columns = action.shape
    groups, tiles = directions // 8, columns // LANES
    list_rows = src.shape[0]
    ocean_rows, width = wet.shape
    spec = lax.axis_size("spec")
    ocean_cols = width * spec
    aligned = width == 2 * LANES and spec == 4
    tail_rows = wave_rows // 2 - 1
    lead = freqs * 2 * groups
    chosen = 2 if aligned else tiles
    padded = -(-list_rows // 8) * 8
    first = wave_rows - 4
    field = jnp.transpose(action.reshape(freqs, directions, wave_rows, tiles, LANES), (0, 1, 3, 2, 4))
    source, weight = jnp.transpose(src, (0, 2, 1)), jnp.transpose(weights, (0, 2, 1))
    cell = (groups, tiles, 8, LANES)
    home = (freqs, tiles, directions, wave_rows, LANES)
    z_current = from_offset(currents, "space", 1)
    z_wet = from_offset(wet, "space", 1)
    masked, wet_float, tables, tail, held, low, high = call(
        functools.partial(open_kernel, ocean_cols, tail_rows, "spec", aligned),
        (
            currents.shape,
            wet.shape,
            (9, tiles, padded, LANES),
            (chosen * TAIL_VREGS, 8, LANES),
            home,
            (lead, tiles, 8, LANES),
            (lead, tiles, 8, LANES),
        ),
        [HBM] * 5,
        scratch_shapes=[
            pltpu.VMEM(currents.shape, f32),
            pltpu.VMEM(wet.shape, jnp.int32),
            pltpu.VMEM(source.shape, jnp.int32),
            pltpu.VMEM(weight.shape, f32),
            pltpu.VMEM(field.shape, f32),
            pltpu.SemaphoreType.DMA((4,)),
            pltpu.SemaphoreType.DMA((freqs,)),
        ],
    )(*in_hbm(currents, wet, source, weight, field))
    low = from_offset(low, "space", -1)
    high = from_offset(high, "space", 1)
    tail = from_offset(tail, "space", -1)
    if aligned:
        (part,) = call(
            functools.partial(flow_kernel, "spec", list_rows, first),
            ((-(-3 * list_rows // 8) * 8, LANES),),
            [VMEM] * 4,
            scratch_shapes=[pltpu.VMEM((2, 1, 2, 2 * ocean_rows, LANES), f32)],
        )(masked, z_current, z_wet, tables)
        parts = [part]
        for bits in range(1, spec):
            parts.append(from_mesh(part, 0, bits))
    else:
        z = z_current * z_wet.astype(f32)[None]
        both = lax.all_gather(jnp.concatenate([masked, z], axis=1), "spec", axis=2, tiled=True)
        ocean = both.reshape(2, 2 * ocean_rows, tiles, LANES, 2).transpose(4, 2, 0, 1, 3)
        parts = call(
            functools.partial(flow_all_kernel, list_rows, first), ((tiles, 2, padded, LANES),), [VMEM] * 2
        )(ocean, tables)
    angles = 2.0 * math.pi * (np.arange(directions) + 0.5) / directions
    cosine, sine = np.cos(angles), np.sin(angles)
    trig = np.stack([cosine, sine, sine * cosine, sine * sine, cosine * cosine]).astype(np.float32)
    trig = trig.reshape(5, 8, groups).transpose(0, 2, 1)
    trig = jnp.asarray(np.repeat(trig[:, :, :, None], LANES, axis=3))
    flow, turn, middle, inner, inner_stress = call(
        functools.partial(inner_kernel, freqs * spec, "spec", list_rows, len(parts)),
        (
            (2, tiles, padded, LANES),
            (2, list_rows - 2) + cell,
            (freqs, wave_rows - 2) + cell,
            (freqs, wave_rows - 4) + cell,
            (3, wave_rows - 4, tiles, 8, LANES),
        ),
        [VMEM] * (len(parts) + 1) + [SMEM] * 2 + [VMEM],
        scratch_shapes=[
            pltpu.VMEM((3, tiles, padded, LANES), f32),
            pltpu.VMEM((4, list_rows) + cell, f32),
        ],
    )(*parts, trig, courant, energy, held)
    outer, stress = call(
        functools.partial(outer_kernel, freqs * spec, "spec"),
        ((freqs, 4) + cell, (3, tiles, wave_rows, LANES)),
        [VMEM] + [SMEM] * 2 + [VMEM] * 7,
        scratch_shapes=[
            pltpu.VMEM((4,) + cell, f32),
            pltpu.VMEM((3, 4, tiles, 8, LANES), f32),
            pltpu.VMEM((4, list_rows) + cell, f32),
        ],
    )(trig, courant, energy, held, low, high, flow, turn, middle, inner_stress)
    if aligned:
        xz = from_mesh(stress, -1, 1)
        z = from_mesh(stress, -1, 0)
        x = from_mesh(stress, 0, 1)
    out_field, coupling = call(
        functools.partial(settle_kernel, "spec", aligned, tail_rows),
        (field.shape, (chosen, 9, 2 * wave_rows, LANES)),
        [VMEM] * 4,
        out_specs=(HBM, VMEM),
        scratch_shapes=[pltpu.VMEM(home, f32), pltpu.SemaphoreType.DMA((freqs, tiles))],
    )(inner, outer, tail, tables)
    new_action = jnp.transpose(out_field, (0, 1, 3, 2, 4)).reshape(action.shape)
    column = (packed_rows(wave_rows + 3), LANES)
    scratch = [pltpu.VMEM(column, f32), pltpu.VMEM((9, 2 * wave_rows, LANES), f32)]
    if aligned:
        keep, send = call(functools.partial(pair_kernel, "spec"), (column, column), [VMEM] * 4)(stress, x, z, xz)
        come = from_mesh(send, 0, 2)
        (updated,) = call(
            force_kernel,
            (currents.shape,),
            [VMEM] * 5,
            scratch_shapes=scratch + [pltpu.VMEM((2, width // LANES, ocean_rows, LANES), f32)],
        )(keep, come, coupling, masked, wet_float)
    else:
        stress = lax.psum(stress, "spec")
        prev = from_offset(stress, "space", -1)
        (pushed,) = call(
            push_all_kernel, ((2, 2, 2, tiles, wave_rows, LANES),), [VMEM] * 3, scratch_shapes=scratch
        )(stress, prev, coupling)
        grid = jnp.transpose(pushed, (1, 4, 2, 3, 5, 0)).reshape(2, ocean_rows, ocean_cols)
        share = lax.dynamic_slice_in_dim(grid, lax.axis_index("spec") * width, width, 2)
        updated = damping * masked + force_gain * wet_float[None] * share
    return (new_action, updated)


def solution(mesh):
    in_specs = (
        P("spec", None, "space", None),
        P(None, "space", "spec"),
        P("space", "spec"),
        P(),
        P(),
        P("space", None, None),
        P("space", None, None),
    )
    out_specs = (P("spec", None, "space", None), P(None, "space", "spec"))
    return jax.shard_map(window, mesh=mesh, in_specs=in_specs, out_specs=out_specs, check_vma=False)
```

```python
import functools
import math

import jax
import jax.numpy as jnp
import numpy as np
from jax import lax
from jax.experimental import pallas as pl
from jax.experimental.pallas import tpu as pltpu
from jax.sharding import PartitionSpec as P


drift_factor = 0.2
refract_factor = 1.5
damping = 0.95
force_gain = 0.5

LANES = 128
VMEM = pl.BlockSpec(memory_space=pltpu.VMEM)
SMEM = pl.BlockSpec(memory_space=pltpu.SMEM)
HBM = pl.BlockSpec(memory_space=pltpu.MemorySpace.HBM)
TAIL_VREGS = 4


def from_offset(block, axis, offset):
    count = lax.axis_size(axis)
    return lax.ppermute(block, axis, [((i + offset) % count, i) for i in range(count)])


def from_mesh(block, offset, bits):
    space, spec = lax.axis_size("space"), lax.axis_size("spec")
    route = [
        (((i + offset) % space) * spec + (j ^ bits), i * spec + j) for i in range(space) for j in range(spec)
    ]
    return lax.ppermute(block, ("space", "spec"), route)


def params(**kw):
    return pltpu.CompilerParams(vmem_limit_bytes=48 * 1024 * 1024, **kw)


def split_matrix(width):
    row = lax.broadcasted_iota(jnp.int32, (width, width), 0)
    col = lax.broadcasted_iota(jnp.int32, (width, width), 1)
    half = width // 2
    source = jnp.where(col < half, 2 * col, 2 * (col - half) + 1)
    return (row == source).astype(jnp.float32).astype(jnp.bfloat16)


def merge_matrix(width):
    row = lax.broadcasted_iota(jnp.int32, (width, width), 0)
    col = lax.broadcasted_iota(jnp.int32, (width, width), 1)
    half = width // 2
    target = jnp.where(row < half, 2 * row, 2 * (row - half) + 1)
    return (col == target).astype(jnp.float32).astype(jnp.bfloat16)


def pick_columns(cells, matrix):
    rows = cells.shape[0]
    first = cells.astype(jnp.bfloat16)
    rest = cells - first.astype(jnp.float32)
    second = rest.astype(jnp.bfloat16)
    third = (rest - second.astype(jnp.float32)).astype(jnp.bfloat16)
    parts = jnp.dot(
        jnp.concatenate([first, second, third], axis=0), matrix, preferred_element_type=jnp.float32
    )
    return parts[:rows] + parts[rows : 2 * rows] + parts[2 * rows :]


def roll_lanes(x, shift):
    lane = lax.broadcasted_iota(jnp.int32, x.shape, x.ndim - 1)
    turned = pltpu.roll(x, shift % LANES, x.ndim - 1)
    if shift == 1:
        return jnp.where(lane == 0, roll_lead(turned, 1, x.ndim - 3), turned)
    return jnp.where(lane == LANES - 1, roll_lead(turned, -1, x.ndim - 3), turned)


def roll_lead(x, shift, axis):
    count = x.shape[axis]
    cut = (-shift) % count
    if cut == 0:
        return x
    return jnp.concatenate(
        [lax.slice_in_dim(x, cut, count, axis=axis), lax.slice_in_dim(x, 0, cut, axis=axis)], axis=axis
    )


def roll_directions(x, shift):
    groups = x.shape[0]
    if shift == 1:
        edge = pltpu.roll(x[groups - 1 :], 1, 2)
        return jnp.concatenate([edge, x[: groups - 1]], axis=0)
    edge = pltpu.roll(x[:1], 7, 2)
    return jnp.concatenate([x[1:], edge], axis=0)


def row_view(ref, freq):
    return ref.at[freq].reshape(ref.shape[1] * ref.shape[2] * 8, LANES)


def row_slots(groups, tiles, row):
    return [
        [pl.ds((tile * 8 * groups + group) * 8 + row, 8, stride=groups * 8) for tile in range(tiles)]
        for group in range(groups)
    ]


def load_row(view, groups, tiles, row):
    slots = row_slots(groups, tiles, row)
    return jnp.stack([jnp.stack([view[slot, :] for slot in line]) for line in slots])


def store_row(view, row, value):
    groups, tiles = value.shape[:2]
    for group, line in enumerate(row_slots(groups, tiles, row)):
        for tile, slot in enumerate(line):
            view[slot, :] = value[group, tile]


def tail_slot(which, slot):
    return which * TAIL_VREGS + slot // 8, slot % 8


def chosen_tiles(axis, aligned, tiles):
    if not aligned:
        return list(range(tiles))
    index = lax.axis_index(axis)
    return [index, lax.rem(index + tiles - 1, tiles)]


def tile_copies(tiled, whole, sems):
    freqs, tiles = tiled.shape[:2]
    for freq in range(freqs):
        for tile in range(tiles):
            yield freq, pltpu.make_async_copy(tiled.at[freq, tile], whole.at[freq, :, tile], sems.at[freq, tile])


def open_kernel(
    ocean_cols, tail_rows, axis, aligned, current_hbm, wet_hbm, src_hbm, weight_hbm, field_hbm,
    masked_ref, wet_out, table_ref, tail_ref, field_ref, low_ref, high_ref,
    current_ref, wet_ref, src_ref, weight_ref, raw_ref, sems, field_sems,
):
    copies = [
        pltpu.make_async_copy(source, target, sems.at[k])
        for k, (source, target) in enumerate(
            ((current_hbm, current_ref), (wet_hbm, wet_ref), (src_hbm, src_ref), (weight_hbm, weight_ref))
        )
    ]
    list_rows, corners, columns = src_ref.shape
    freqs, tiles, directions, wave_rows, _ = field_ref.shape
    moves = [
        pltpu.make_async_copy(field_hbm.at[freq], raw_ref.at[freq], field_sems.at[freq]) for freq in range(freqs)
    ]
    for copy in copies:
        copy.start()
    for copy in moves:
        copy.start()
    groups = directions // 8
    shape = (list_rows, columns)
    entry_row = lax.broadcasted_iota(jnp.int32, shape, 0)
    column = lax.broadcasted_iota(jnp.int32, shape, 1)
    base = (2 * (entry_row - 2) + wave_rows) * ocean_cols
    cell = [
        base + jnp.where(2 * column + step >= ocean_cols, 2 * column + step - ocean_cols, 2 * column + step)
        for step in range(3)
    ]
    for copy in copies:
        copy.wait()
    wet = wet_ref[...].astype(jnp.float32)
    wet_out[...] = wet
    masked_ref[...] = current_ref[...] * wet[None]
    sums = [jnp.zeros(shape, jnp.float32) for _ in range(9)]
    for corner in range(corners):
        source = src_ref[:, corner, :]
        weight = weight_ref[:, corner, :]
        for step_row in range(3):
            for step_col in range(3):
                hit = source == cell[step_col] + step_row * ocean_cols
                place = 3 * step_row + step_col
                sums[place] = sums[place] + jnp.where(hit, weight, 0.0)
    for place in range(9):
        for tile in range(tiles):
            table_ref[place, tile, :list_rows] = sums[place][:, tile * LANES : (tile + 1) * LANES]
    first = 2 + wave_rows // 2 - 1
    for which, tile in enumerate(chosen_tiles(axis, aligned, tiles)):
        for place in range(9):
            for row in range(tail_rows):
                vreg, line = tail_slot(which, place * tail_rows + row)
                tail_ref[vreg, line : line + 1, :] = table_ref[place, tile, first + row : first + row + 1, :]
    for freq in range(freqs):
        moves[freq].wait()
        for tile in range(tiles):
            field_ref[freq, tile] = raw_ref[freq, :, tile]
        view = row_view(field_ref, freq)
        for row in range(2):
            at = (freq * 2 + row) * groups
            low_ref[at : at + groups] = load_row(view, groups, tiles, wave_rows - 2 + row)
            high_ref[at : at + groups] = load_row(view, groups, tiles, row)


def flow_tile(table_ref, tile, evens, odds, nexts):
    total = None
    for step_row in range(3):
        even = evens[step_row]
        list_rows = even.shape[0]
        lane = lax.broadcasted_iota(jnp.int32, even.shape, 1)
        edge = 0.0 if nexts is None else pltpu.roll(nexts[step_row], LANES - 1, 1)
        shifted = jnp.where(lane == LANES - 1, edge, pltpu.roll(even, LANES - 1, 1))
        for step_col, lifted in enumerate((even, odds[step_row], shifted)):
            term = table_ref[3 * step_row + step_col, tile, :list_rows] * lifted
            total = term if total is None else total + term
    return total


def row_steps(ref, parity, tile, comp, first, list_rows):
    return [ref[parity, tile, comp, pl.ds(first + step, list_rows, stride=2), :] for step in range(3)]


def flow_kernel(axis, list_rows, first, own_ref, current_ref, wet_ref, table_ref, part_ref, ocean_ref):
    comps, rows, width = own_ref.shape
    tiles = table_ref.shape[1]
    half = width // 2
    tile = lax.axis_index(axis)
    after = current_ref[...] * wet_ref[...].astype(jnp.float32)[None]
    cells = jnp.concatenate([x.reshape(comps * rows, width) for x in (own_ref[...], after)], axis=0)
    split = pick_columns(cells, split_matrix(width))
    split = split.reshape(2, comps, rows, width)
    for parity in range(2):
        for block in range(2):
            ocean_ref[parity, 0, :, block * rows : (block + 1) * rows] = split[
                block, :, :, parity * half : (parity + 1) * half
            ]
    before = lax.rem(tile + tiles - 1, tiles)
    lane = lax.broadcasted_iota(jnp.int32, (list_rows, LANES), 1)
    spill = None
    for comp in range(comps):
        even = row_steps(ocean_ref, 0, 0, comp, first, list_rows)
        odd = row_steps(ocean_ref, 1, 0, comp, first, list_rows)
        part_ref[comp * list_rows : (comp + 1) * list_rows] = flow_tile(table_ref, tile, even, odd, None)
        for step in range(3):
            weight = table_ref[3 * step + 2, before, :list_rows]
            weight = weight if comp == 0 else pltpu.roll(weight, LANES - comp, 1)
            edge = jnp.where(lane == LANES - 1 - comp, pltpu.roll(even[step], LANES - 1 - comp, 1), 0.0)
            spill = weight * edge if spill is None else spill + weight * edge
    part_ref[comps * list_rows : (comps + 1) * list_rows] = spill


def flow_all_kernel(list_rows, first, ocean_ref, table_ref, flow_ref):
    tiles = table_ref.shape[1]
    for comp in range(2):
        evens = [row_steps(ocean_ref, 0, k, comp, first, list_rows) for k in range(tiles)]
        odds = [row_steps(ocean_ref, 1, k, comp, first, list_rows) for k in range(tiles)]
        for tile in range(tiles):
            flow_ref[tile, comp, :list_rows] = flow_tile(
                table_ref, tile, evens[tile], odds[tile], evens[(tile + 1) % tiles]
            )


def spread_row(ref, lead, row, groups):
    tiles = ref.shape[-3]
    lines = [ref[(*lead, tile, pl.ds(row, 8, stride=0), slice(None))] for tile in range(tiles)]
    return jnp.broadcast_to(jnp.stack(lines)[None], (groups, tiles, 8, LANES))


class Speeds:
    def __init__(self, speed, trig_ref, flow_ref, keep_ref):
        groups, tiles = trig_ref.shape[1], flow_ref.shape[1]
        shape = (groups, tiles, 8, LANES)
        self.groups, self.flow_ref, self.keep_ref = groups, flow_ref, keep_ref
        self.base = [jnp.broadcast_to((speed * trig_ref[k])[:, None], shape) for k in range(2)]
        self.seen = set()

    def parts(self, comp, row):
        slot = row + 2
        if (comp, row) in self.seen:
            return self.keep_ref[2 * comp, slot], self.keep_ref[2 * comp + 1, slot]
        value = self.base[comp] + spread_row(self.flow_ref, (comp,), slot, self.groups)
        up, down = jnp.maximum(value, 0.0), jnp.minimum(value, 0.0)
        self.keep_ref[2 * comp, slot], self.keep_ref[2 * comp + 1, slot] = up, down
        self.seen.add((comp, row))
        return up, down


def sweep(read, speeds, turn_ref, low, high, write):
    here = read(low)
    up, down = speeds.parts(1, low)
    face_before = speeds.parts(1, low - 1)[0] * read(low - 1) + down * here
    for row in range(low, high):
        after = read(row + 1)
        up_after, down_after = speeds.parts(1, row + 1)
        face_here = up * here + down_after * after
        right, left = speeds.parts(0, row)
        face_x = right * here + roll_lanes(left * here, -1)
        face_turn = turn_ref[0, row + 1] * here + roll_directions(turn_ref[1, row + 1] * here, -1)
        write(
            row,
            here
            - (face_x - roll_lanes(face_x, 1))
            - (face_here - face_before)
            - (face_turn - roll_directions(face_turn, 1)),
        )
        face_before, here, up = face_here, after, up_after


def add_stress(value, tables, sum_ref, slot):
    for kind, table in enumerate(tables):
        sum_ref[kind, slot] += jnp.sum(table * value, axis=0)


def stress_tables(trig_ref, energy_ref, number, total_freq, shape):
    directions = shape[0] * 8
    ratio = 0.5 + 0.5 * number.astype(jnp.float32) / (total_freq - 1)
    amplitude = energy_ref[number] / math.sqrt(directions * total_freq)
    scale, rest = amplitude * ratio, amplitude * (ratio - 0.5)
    tables = (scale * trig_ref[4] + rest, scale * trig_ref[3] + rest, scale * trig_ref[2])
    return [jnp.broadcast_to(table[:, None], shape) for table in tables]


def add_stress_plain(value, trig_ref, scale, rest, sum_ref, slot):
    shape = value.shape
    cross = jnp.broadcast_to(trig_ref[2][:, None], shape)
    cos2 = jnp.broadcast_to(trig_ref[4][:, None], shape)
    plain = jnp.sum(value, axis=0)
    weighted = jnp.sum(cos2 * value, axis=0)
    mixed = jnp.sum(cross * value, axis=0)
    sum_ref[0, slot] += scale * weighted + rest * plain
    sum_ref[1, slot] += scale * (plain - weighted) + rest * plain
    sum_ref[2, slot] += scale * mixed


def stress_scales(energy_ref, number, total_freq, directions):
    ratio = 0.5 + 0.5 * number.astype(jnp.float32) / (total_freq - 1)
    amplitude = energy_ref[number] / math.sqrt(directions * total_freq)
    return amplitude * ratio, amplitude * (ratio - 0.5)


def inner_kernel(total_freq, axis, list_rows, parts, *refs):
    part_refs = refs[:parts]
    (trig_ref, speed_ref, energy_ref, field_ref) = refs[parts : parts + 4]
    flow_ref, turn_ref, mid_ref, out_ref, sum_ref = refs[parts + 4 : parts + 9]
    grad_ref, keep_ref = refs[parts + 9 :]
    freqs, tiles, directions, wave_rows, _ = field_ref.shape
    groups = directions // 8
    index = lax.axis_index(axis)
    for comp in range(2):
        if parts == 1:
            for tile in range(tiles):
                flow_ref[comp, tile] = part_refs[0][tile, comp]
        else:
            for bits in range(parts):
                rows = slice(comp * list_rows, (comp + 1) * list_rows)
                flow_ref[comp, index ^ bits, :list_rows] = part_refs[bits][rows]
            lane = lax.broadcasted_iota(jnp.int32, (list_rows, LANES), 1)
            for bits in range(parts):
                before = lax.rem((index ^ bits) + tiles - 1, tiles)
                spill = part_refs[bits][2 * list_rows : 3 * list_rows]
                spill = spill if comp == 0 else pltpu.roll(spill, comp, 1)
                flow_ref[comp, before, :list_rows] += jnp.where(lane == LANES - 1, spill, 0.0)
    inner = list_rows - 2
    east, north = flow_ref[0, :, 1 : 1 + inner], flow_ref[1, :, 1 : 1 + inner]
    east_y = (flow_ref[0, :, 2 : 2 + inner] - flow_ref[0, :, 0:inner]) * 0.5
    north_y = (flow_ref[1, :, 2 : 2 + inner] - flow_ref[1, :, 0:inner]) * 0.5
    east_x = (roll_lanes(east, -1) - roll_lanes(east, 1)) * 0.5
    north_x = (roll_lanes(north, -1) - roll_lanes(north, 1)) * 0.5
    grad_ref[0, :, :inner] = refract_factor * (east_x - north_y)
    grad_ref[1, :, :inner] = refract_factor * east_y
    grad_ref[2, :, :inner] = refract_factor * north_x
    for comp in range(2):
        flow_ref[comp, :, :list_rows] = drift_factor * flow_ref[comp, :, :list_rows]
    cross, sin2, cos2 = (
        jnp.broadcast_to(trig_ref[k][:, None], (groups, tiles, 8, LANES)) for k in (2, 3, 4)
    )
    for row in range(inner):
        first, second, third = (spread_row(grad_ref, (k,), row, groups) for k in range(3))
        turn = cross * first + sin2 * second - cos2 * third
        turn_ref[0, row] = jnp.maximum(turn, 0.0)
        turn_ref[1, row] = jnp.minimum(turn, 0.0)
    sum_ref[...] = jnp.zeros_like(sum_ref)
    start = index * freqs

    def one_frequency(freq, carry):
        speeds = Speeds(speed_ref[start + freq], trig_ref, flow_ref, keep_ref)
        source = row_view(field_ref, freq)

        def keep(row, value):
            mid_ref[freq, row - 1] = value

        sweep(lambda row: load_row(source, groups, tiles, row), speeds, turn_ref, 1, wave_rows - 1, keep)
        scale, rest = stress_scales(energy_ref, start + freq, total_freq, directions)

        def finish(row, value):
            out_ref[freq, row - 2] = value
            add_stress_plain(value, trig_ref, scale, rest, sum_ref, row - 2)

        sweep(lambda row: mid_ref[freq, row - 1], speeds, turn_ref, 2, wave_rows - 2, finish)
        return carry

    lax.fori_loop(0, freqs, one_frequency, 0)


def outer_kernel(
    total_freq, axis, trig_ref, speed_ref, energy_ref, field_ref, low_ref, high_ref, flow_ref, turn_ref,
    mid_ref, inner_ref, out_ref, stress_ref, rim_ref, sum_ref, keep_ref,
):
    freqs, tiles, directions, wave_rows, _ = field_ref.shape
    groups = directions // 8
    start = lax.axis_index(axis) * freqs
    sum_ref[...] = jnp.zeros_like(sum_ref)
    rim = {-1: 0, 0: 1, wave_rows - 1: 2, wave_rows: 3}
    last = {0: 0, 1: 1, wave_rows - 2: 2, wave_rows - 1: 3}

    def one_frequency(freq, carry):
        speeds = Speeds(speed_ref[start + freq], trig_ref, flow_ref, keep_ref)
        source = row_view(field_ref, freq)

        def cells(row):
            if 0 <= row < wave_rows:
                return load_row(source, groups, tiles, row)
            at = pl.ds((freq * 2 + row % 2) * groups, groups)
            return low_ref[at] if row < 0 else high_ref[at]

        def keep(row, value):
            rim_ref[rim[row]] = value

        def middle(row):
            return rim_ref[rim[row]] if row in rim else mid_ref[freq, row - 1]

        tables = stress_tables(trig_ref, energy_ref, start + freq, total_freq, (groups, tiles, 8, LANES))

        def finish(row, value):
            out_ref[freq, last[row]] = value
            add_stress(value, tables, sum_ref, last[row])

        sweep(cells, speeds, turn_ref, -1, 1, keep)
        sweep(cells, speeds, turn_ref, wave_rows - 1, wave_rows + 1, keep)
        sweep(middle, speeds, turn_ref, 0, 2, finish)
        sweep(middle, speeds, turn_ref, wave_rows - 2, wave_rows, finish)
        return carry

    lax.fori_loop(0, freqs, one_frequency, 0)
    for kind in range(3):
        for row in range(wave_rows):
            part = sum_ref[kind, last[row]] if row in last else inner_ref[kind, row - 2]
            line = jnp.sum(part, axis=1, keepdims=True)
            for tile in range(tiles):
                stress_ref[kind, tile, row : row + 1] = line[tile]


def edge_tile(after, before):
    lane = lax.broadcasted_iota(jnp.int32, after.shape, after.ndim - 1)
    return jnp.where(lane < LANES // 2, after, before)


def pack_stress(out_ref, center, edge, count):
    merged = None
    for kind in range(3):
        upper, lower = center(kind)
        cut = kind * count + upper.shape[0]
        out_ref[kind * count : cut] = upper
        out_ref[cut : (kind + 1) * count] = lower
        parts = edge(kind)
        if kind == 0:
            merged = list(parts)
            continue
        for k, part in enumerate(parts):
            lane = lax.broadcasted_iota(jnp.int32, part.shape, 1) - 4 * kind
            mine = jnp.logical_and(lane >= -2, lane <= 0)
            merged[k] = jnp.where(mine, pltpu.roll(part, 4 * kind, 1), merged[k])
    cut = 3 * count + merged[0].shape[0]
    out_ref[3 * count : cut] = merged[0]
    out_ref[cut : 4 * count] = merged[1]


def packed_rows(count):
    return -(-4 * count // 8) * 8


def pair_kernel(axis, own_ref, x_ref, z_ref, xz_ref, keep_ref, send_ref):
    tiles, wave_rows = own_ref.shape[1:3]
    half = wave_rows // 2
    index = lax.axis_index(axis)

    def own(kind, tile):
        return own_ref[kind, tile] + x_ref[kind, tile]

    def prev(kind, tile):
        return z_ref[kind, tile] + xz_ref[kind, tile]

    for target, out_ref in ((index, keep_ref), (index ^ 2, send_ref)):
        after = lax.rem(target + 1, tiles)
        before = lax.rem(target + tiles - 1, tiles)

        def center(kind):
            return prev(kind, target)[wave_rows - half - 2 :], own(kind, target)[: half + 1]

        def edge(kind):
            return (
                edge_tile(prev(kind, after), prev(kind, before))[wave_rows - half - 2 :],
                edge_tile(own(kind, after), own(kind, before))[: half + 1],
            )

        pack_stress(out_ref, center, edge, wave_rows + 3)


def settle_kernel(
    axis, aligned, tail_rows, inner_ref, outer_ref, tail_ref, table_ref, out_hbm, coupling_ref, field_ref, sems
):
    freqs, tiles, _, wave_rows, _ = field_ref.shape
    moves = list(tile_copies(field_ref, out_hbm, sems))
    for freq in range(freqs):
        sink = row_view(field_ref, freq)
        for row in range(wave_rows):
            if 2 <= row < wave_rows - 2:
                value = inner_ref[freq, row - 2]
            else:
                value = outer_ref[freq, row if row < 2 else row - wave_rows + 4]
            store_row(sink, row, value)
        for other, copy in moves:
            if other == freq:
                copy.start()
    count = wave_rows + 1
    for which, tile in enumerate(chosen_tiles(axis, aligned, tiles)):
        for place in range(9):
            for row in range(tail_rows):
                vreg, line = tail_slot(which, place * tail_rows + row)
                coupling_ref[which, place, row : row + 1, :] = tail_ref[vreg, line : line + 1, :]
            coupling_ref[which, place, tail_rows:count] = table_ref[place, tile, 0 : count - tail_rows]
    for _, copy in moves:
        copy.wait()


def push_tile(stress_ref, coupling_ref, here, edge, push_ref, count):
    lane = lax.broadcasted_iota(jnp.int32, (count, LANES), 1)
    span = count + 2

    def rows(part, kind, low):
        if part == 0:
            return stress_ref[kind * span + low : kind * span + low + count]
        value = stress_ref[3 * span + low : 3 * span + low + count]
        return value if kind == 0 else pltpu.roll(value, LANES - 4 * kind, 1)

    def along_y(part, kind):
        return (rows(part, kind, 2) - rows(part, kind, 0)) * 0.5

    def along_x(part, kind):
        tile, rim = rows(0, kind, 1), rows(1, kind, 1)
        after = jnp.where(lane == LANES - 1, pltpu.roll(rim, LANES - 1, 1), pltpu.roll(tile, LANES - 1, 1))
        if part == 0:
            before = jnp.where(lane == 0, pltpu.roll(rim, 1, 1), pltpu.roll(tile, 1, 1))
            return (after - before) * 0.5
        return (pltpu.roll(tile, LANES - 1, 1) - pltpu.roll(rim, 1, 1)) * 0.5

    def forces(part):
        return (
            -(along_x(part, 0) + along_y(part, 2)),
            -(along_x(part, 2) + along_y(part, 1)),
        )

    inner, rim = forces(0), forces(1)
    result = []
    for comp in range(2):
        for place in range(9):
            value = coupling_ref[here, place, :count] * inner[comp]
            if place % 3 == 2:
                spill = coupling_ref[edge, place, :count] * rim[comp]
                value = jnp.where(lane == 0, pltpu.roll(spill, 1, 1), pltpu.roll(value, 1, 1))
            push_ref[place, :count] = value
        near = [push_ref[place, 1:count] for place in range(9)]
        far = [push_ref[place, 0 : count - 1] for place in range(9)]
        result.append(
            (
                (near[0] + far[6] + near[2] + far[8], near[1] + far[7]),
                (near[3] + near[5], near[4]),
            )
        )
    return result


def force_kernel(keep_ref, come_ref, coupling_ref, masked_ref, wet_ref, out_ref, stress_ref, push_ref, merge_ref):
    ocean_rows, width = wet_ref.shape
    wave_rows = ocean_rows // 2
    count = wave_rows + 1
    stress_ref[...] = keep_ref[...] + come_ref[...]
    pushed = push_tile(stress_ref, coupling_ref, 0, 1, push_ref, count)
    cells = jnp.concatenate(
        [
            jnp.concatenate([even, odd], axis=1)
            for component in pushed
            for even, odd in component
        ],
        axis=0,
    )
    merged = pick_columns(cells, merge_matrix(width)).reshape(2, 2, wave_rows, width)
    wet = wet_ref[...]
    for comp in range(2):
        for tile in range(width // LANES):
            lanes = slice(tile * LANES, (tile + 1) * LANES)
            for parity in range(2):
                lines = pl.ds(parity, wave_rows, stride=2)
                merge_ref[comp, tile, lines, :] = merged[comp, parity, :, lanes]
            out_ref[comp, :, lanes] = (
                damping * masked_ref[comp, :, lanes] + force_gain * wet[:, lanes] * merge_ref[comp, tile]
            )


def push_all_kernel(own_ref, prev_ref, coupling_ref, out_ref, stress_ref, push_ref):
    tiles, wave_rows = own_ref.shape[1:3]
    half = wave_rows // 2
    for tile in range(tiles):
        after, before = (tile + 1) % tiles, (tile - 1) % tiles

        def center(kind):
            return prev_ref[kind, tile][wave_rows - half - 2 :], own_ref[kind, tile][: half + 1]

        def edge(kind):
            return (
                edge_tile(prev_ref[kind, after], prev_ref[kind, before])[wave_rows - half - 2 :],
                edge_tile(own_ref[kind, after], own_ref[kind, before])[: half + 1],
            )

        pack_stress(stress_ref, center, edge, wave_rows + 3)
        pushed = push_tile(stress_ref, coupling_ref, tile, before, push_ref, wave_rows + 1)
        for comp in range(2):
            for parity in range(2):
                for side in range(2):
                    out_ref[side, comp, parity, tile] = pushed[comp][parity][side]


def call(kernel, outs, ins, out_specs=None, **kw):
    f32 = jnp.float32
    shapes = tuple(jax.ShapeDtypeStruct(shape, f32) for shape in outs)
    if out_specs is None:
        out_specs = (VMEM,) * len(outs)
    return pl.pallas_call(kernel, out_shape=shapes, in_specs=ins, out_specs=out_specs, compiler_params=params(), **kw)


def in_hbm(*arrays):
    return [pltpu.with_memory_space_constraint(x, pltpu.MemorySpace.HBM) for x in arrays]


def window(action, currents, wet, courant, energy, src, weights):
    f32 = jnp.float32
    freqs, directions, wave_rows, columns = action.shape
    groups, tiles = directions // 8, columns // LANES
    list_rows = src.shape[0]
    ocean_rows, width = wet.shape
    spec = lax.axis_size("spec")
    ocean_cols = width * spec
    aligned = width == 2 * LANES and spec == 4
    tail_rows = wave_rows // 2 - 1
    lead = freqs * 2 * groups
    chosen = 2 if aligned else tiles
    padded = -(-list_rows // 8) * 8
    first = wave_rows - 4
    field = jnp.transpose(action.reshape(freqs, directions, wave_rows, tiles, LANES), (0, 1, 3, 2, 4))
    source, weight = jnp.transpose(src, (0, 2, 1)), jnp.transpose(weights, (0, 2, 1))
    cell = (groups, tiles, 8, LANES)
    home = (freqs, tiles, directions, wave_rows, LANES)
    z_current = from_offset(currents, "space", 1)
    z_wet = from_offset(wet, "space", 1)
    masked, wet_float, tables, tail, held, low, high = call(
        functools.partial(open_kernel, ocean_cols, tail_rows, "spec", aligned),
        (
            currents.shape,
            wet.shape,
            (9, tiles, padded, LANES),
            (chosen * TAIL_VREGS, 8, LANES),
            home,
            (lead, tiles, 8, LANES),
            (lead, tiles, 8, LANES),
        ),
        [HBM] * 5,
        scratch_shapes=[
            pltpu.VMEM(currents.shape, f32),
            pltpu.VMEM(wet.shape, jnp.int32),
            pltpu.VMEM(source.shape, jnp.int32),
            pltpu.VMEM(weight.shape, f32),
            pltpu.VMEM(field.shape, f32),
            pltpu.SemaphoreType.DMA((4,)),
            pltpu.SemaphoreType.DMA((freqs,)),
        ],
    )(*in_hbm(currents, wet, source, weight, field))
    low = from_offset(low, "space", -1)
    high = from_offset(high, "space", 1)
    tail = from_offset(tail, "space", -1)
    if aligned:
        (part,) = call(
            functools.partial(flow_kernel, "spec", list_rows, first),
            ((-(-3 * list_rows // 8) * 8, LANES),),
            [VMEM] * 4,
            scratch_shapes=[pltpu.VMEM((2, 1, 2, 2 * ocean_rows, LANES), f32)],
        )(masked, z_current, z_wet, tables)
        parts = [part]
        for bits in range(1, spec):
            parts.append(from_mesh(part, 0, bits))
    else:
        z = z_current * z_wet.astype(f32)[None]
        both = lax.all_gather(jnp.concatenate([masked, z], axis=1), "spec", axis=2, tiled=True)
        ocean = both.reshape(2, 2 * ocean_rows, tiles, LANES, 2).transpose(4, 2, 0, 1, 3)
        parts = call(
            functools.partial(flow_all_kernel, list_rows, first), ((tiles, 2, padded, LANES),), [VMEM] * 2
        )(ocean, tables)
    angles = 2.0 * math.pi * (np.arange(directions) + 0.5) / directions
    cosine, sine = np.cos(angles), np.sin(angles)
    trig = np.stack([cosine, sine, sine * cosine, sine * sine, cosine * cosine]).astype(np.float32)
    trig = trig.reshape(5, 8, groups).transpose(0, 2, 1)
    trig = jnp.asarray(np.repeat(trig[:, :, :, None], LANES, axis=3))
    flow, turn, middle, inner, inner_stress = call(
        functools.partial(inner_kernel, freqs * spec, "spec", list_rows, len(parts)),
        (
            (2, tiles, padded, LANES),
            (2, list_rows - 2) + cell,
            (freqs, wave_rows - 2) + cell,
            (freqs, wave_rows - 4) + cell,
            (3, wave_rows - 4, tiles, 8, LANES),
        ),
        [VMEM] * (len(parts) + 1) + [SMEM] * 2 + [VMEM],
        scratch_shapes=[
            pltpu.VMEM((3, tiles, padded, LANES), f32),
            pltpu.VMEM((4, list_rows) + cell, f32),
        ],
    )(*parts, trig, courant, energy, held)
    outer, stress = call(
        functools.partial(outer_kernel, freqs * spec, "spec"),
        ((freqs, 4) + cell, (3, tiles, wave_rows, LANES)),
        [VMEM] + [SMEM] * 2 + [VMEM] * 7,
        scratch_shapes=[
            pltpu.VMEM((4,) + cell, f32),
            pltpu.VMEM((3, 4, tiles, 8, LANES), f32),
            pltpu.VMEM((4, list_rows) + cell, f32),
        ],
    )(trig, courant, energy, held, low, high, flow, turn, middle, inner_stress)
    if aligned:
        xz = from_mesh(stress, -1, 1)
        z = from_mesh(stress, -1, 0)
        x = from_mesh(stress, 0, 1)
    out_field, coupling = call(
        functools.partial(settle_kernel, "spec", aligned, tail_rows),
        (field.shape, (chosen, 9, 2 * wave_rows, LANES)),
        [VMEM] * 4,
        out_specs=(HBM, VMEM),
        scratch_shapes=[pltpu.VMEM(home, f32), pltpu.SemaphoreType.DMA((freqs, tiles))],
    )(inner, outer, tail, tables)
    new_action = jnp.transpose(out_field, (0, 1, 3, 2, 4)).reshape(action.shape)
    column = (packed_rows(wave_rows + 3), LANES)
    scratch = [pltpu.VMEM(column, f32), pltpu.VMEM((9, 2 * wave_rows, LANES), f32)]
    if aligned:
        keep, send = call(functools.partial(pair_kernel, "spec"), (column, column), [VMEM] * 4)(stress, x, z, xz)
        come = from_mesh(send, 0, 2)
        (updated,) = call(
            force_kernel,
            (currents.shape,),
            [VMEM] * 5,
            scratch_shapes=scratch + [pltpu.VMEM((2, width // LANES, ocean_rows, LANES), f32)],
        )(keep, come, coupling, masked, wet_float)
    else:
        stress = lax.psum(stress, "spec")
        prev = from_offset(stress, "space", -1)
        (pushed,) = call(
            push_all_kernel, ((2, 2, 2, tiles, wave_rows, LANES),), [VMEM] * 3, scratch_shapes=scratch
        )(stress, prev, coupling)
        grid = jnp.transpose(pushed, (1, 4, 2, 3, 5, 0)).reshape(2, ocean_rows, ocean_cols)
        share = lax.dynamic_slice_in_dim(grid, lax.axis_index("spec") * width, width, 2)
        updated = damping * masked + force_gain * wet_float[None] * share
    return (new_action, updated)


def solution(mesh):
    in_specs = (
        P("spec", None, "space", None),
        P(None, "space", "spec"),
        P("space", "spec"),
        P(),
        P(),
        P("space", None, None),
        P("space", None, None),
    )
    out_specs = (P("spec", None, "space", None), P(None, "space", "spec"))
    return jax.shard_map(window, mesh=mesh, in_specs=in_specs, out_specs=out_specs, check_vma=False)
```
